256 devices in a mesh: lat: 8 (over z), lon: 32 (over y, x, core).
Axes of the slice: x: 4, y: 4, z: 8, core: 2. Of those that a mesh axis runs over, the one named last changes fastest.
Arguments:
- corona: float32 [8, 128, 512, 128], P(None, 'lat', 'lon'), may hold values from -6 to 6
- kappa: float32 [128, 512, 128], P('lat', 'lon'), may hold values from 0.05 to 1
- mixing: float32 [8, 8], replicated, may hold values from -2 to 2
- helio_prev: float32 [8, 1024, 1024], P(None, 'lon', 'lat'), may hold values from -6 to 6
- owner: int32 [524288, 1], P(('lat', 'lon')), may hold values from 0 to 255; in each aligned block of 2048 rows (0 to 2047, 2048 to 4095, ...) at most 16 rows name the same one
- dest_cell: int32 [524288], P(('lat', 'lon')), may hold values from 0 to 4095
- corner_base: int32 [524288], P(('lat', 'lon')), may hold values from 0 to 1910, as said below
- fractions: float32 [3, 524288], P(None, ('lat', 'lon')), may hold values from 0 to 1
Outputs:
- stepped: float32 [8, 128, 512, 128], P(None, 'lat', 'lon')
- helio_face: float32 [8, 1024, 1024], P(None, 'lon', 'lat')
The draws below stay inside these ranges and needn't reach their ends.
Inputs may be any that keep to these rules, and one draw needn't show every extreme that they name: Among the targets of one device no owner appears more than 16 times, a bound that some block reaches. corner_base = (t * 16 + p) * 8 + r with t < 15, p < 15, r < 7.
All inputs are finite; a program needn't handle non-finite values.
Results may differ from the reference program's by a relative error of at most 0.000075.
Values sent between devices are 32-bit elements; how exact they have to be, the bound alone decides.
No kernel may reach another device: no remote copies, remote signals or barrier semaphores. Data moves between devices by JAX's collectives and lax.ppermute only.
A program may use at most 64 MiB of HBM per device.

```python
import math
import jax
import jax.numpy as jnp
import numpy as np
from jax import lax

FIELDS = 8
CT = 16
CP = 16
NR = 128
SH = 8
T_DEV = 2048
FP = 32
FT = 128
NT = 128
NP = 512
NFP = 1024
NFT = 1024
TARGETS = 524288
CAP = 16
N_LON = 32
DEVICES = 256


def draw_corner_base(key, part):
    key_t, key_p, key_r = jax.random.split(jax.random.fold_in(key, 7), 3)
    theta = jax.random.randint(key_t, (TARGETS,), 0, CT - 1)
    phi = jax.random.randint(key_p, (TARGETS,), 0, CP - 1)
    layer = jax.random.randint(key_r, (TARGETS,), 0, SH - 1)
    return ((theta * CP + phi) * SH + layer).astype(jnp.int32)


def touch_ends(drawn, rng, smallest, largest):
    longest = drawn.shape.index(max(drawn.shape))
    spots = []
    for shift in (0, 1):
        where = [jax.random.randint(jax.random.fold_in(rng, axis), (), 0, length) for axis, length in enumerate(drawn.shape)]
        where[longest] = (where[longest] + shift) % drawn.shape[longest]
        spots.append(tuple(where))
    return drawn.at[spots[0]].set(smallest).at[spots[1]].set(largest)


def block_levels(own_key, extent, cuts, low, top_value):
    def one(dim, parts):
        steps = jax.random.uniform(jax.random.fold_in(jax.random.fold_in(own_key, 6), dim), (parts,), jnp.float32, low / len(cuts), top_value / len(cuts))
        return jnp.repeat(jnp.exp(steps), extent[dim] // parts).reshape((-1,) + (1,) * (len(extent) - dim - 1))

    gain = one(*cuts[0])
    for cut in cuts[1:]:
        gain = gain * one(*cut)
    return gain


def deal_out(own_key, own, number, rows, amount, top, reach, slope):
    order = jax.random.permutation(own_key, amount)
    crowded, common = portions_of(amount, rows * top, reach, slope, True), portions_of(amount, rows * top, reach, slope, False)
    places = jnp.arange(amount)

    def named(lengths, offset_by):
        used = int((lengths > 0).sum())
        fixed = max(1, used // 4)
        passed = fixed + (places - fixed + offset_by * (used - fixed)) % max(1, amount - fixed)
        return jnp.zeros((amount,), jnp.int32).at[order[jnp.where(places < fixed, places, passed)]].set(jnp.asarray(lengths, jnp.int32))

    lengths = jnp.where(number % 4 == 0, named(crowded, number // 4), named(common, number - number // 4 - 1))
    mixed = jax.random.permutation(jax.random.fold_in(own, 3), amount)
    source_of, sink = mixed[0:amount // 2 * 2:2], mixed[1:amount // 2 * 2:2]
    margin = jnp.minimum(lengths[source_of] - 1, reach - lengths[sink]) // 2
    margin = jnp.where((source_of == order[0]) | (sink == order[0]) | (lengths[sink] == 0), 0, jnp.maximum(margin, 0))
    passed = jax.random.randint(jax.random.fold_in(own, 4), (amount // 2,), 0, 1 << 20) % (margin + 1)
    lengths = lengths.at[source_of].add(-passed).at[sink].add(passed)
    members = jnp.searchsorted(jnp.cumsum(lengths), jnp.arange(rows * top), side="right").astype(jnp.int32)
    grid = members.reshape(top, rows).T
    grid = grid[jax.random.permutation(jax.random.fold_in(own, 1), rows)]
    offset_by = jax.random.randint(jax.random.fold_in(own, 2), (rows, 1), 0, top)
    return jnp.take_along_axis(grid, (jnp.arange(top)[None, :] + offset_by) % top, axis=1)


def portions_of(number_of, total, most, lean, full):
    loads = [(1 << 20) // math.isqrt(rank ** lean) + 1 for rank in range(1, number_of + 1)]
    largest = most if full else min(most, max(-(-total // number_of), total * loads[0] // sum(loads)))
    least = 1 if total - largest >= number_of - 1 else 0
    holding, rest = [largest] + [least] * (number_of - 1), total - largest - least * (number_of - 1)
    while rest > 0:
        movable = [i for i in range(1, number_of) if holding[i] < largest] or [i for i in range(1, number_of) if holding[i] < most]
        pool, remaining = sum([loads[i] for i in movable]), rest
        for i in movable:
            more = min(most - holding[i], max(1, remaining * loads[i] // pool), rest)
            holding[i] = holding[i] + more
            rest = rest - more
    return np.array(holding)


def gaussian(own_key, dims, scale, most, pieces=(), held_as=jnp.bfloat16):
    gain = block_levels(own_key, dims, pieces, -0.22, 0.18) if pieces else 1.0
    entries = jax.random.normal(own_key, dims, jnp.float32) * scale * gain
    return jnp.minimum(jnp.maximum(entries, -most), most).astype(held_as)


def setup_inputs(seed: int = 0) -> dict:
    arg_keys = jax.random.split(jax.random.key(seed), 9)
    corona = gaussian(arg_keys[0], (FIELDS, NT, NP, NR), 1.0, 6.0, ((1, 8), (2, 32)), jnp.float32)
    kappa = jnp.clip(jnp.exp(math.log(1.0) - 2.9957323 * jax.random.uniform(arg_keys[1], (NT, NP, NR), jnp.float32) ** block_levels(arg_keys[1], (NT, NP, NR), ((0, 8), (1, 32)), -0.2, 0.2)), 0.05, 1.0)
    mixing = gaussian(arg_keys[2], (FIELDS, FIELDS), FIELDS ** -0.5, 2.0, (), jnp.float32)
    helio_prev = gaussian(arg_keys[3], (FIELDS, NFP, NFT), 1.0, 6.0, ((1, 32), (2, 8)), jnp.float32)
    owner_keys = jax.random.split(jax.random.fold_in(arg_keys[4], 1), TARGETS // T_DEV)
    owner_turns = jax.random.permutation(jax.random.fold_in(arg_keys[4], 3), TARGETS // T_DEV)
    owner = jax.vmap(lambda own, number: deal_out(jax.random.fold_in(arg_keys[4], 2), own, number, T_DEV, DEVICES, 1, CAP, 2))(owner_keys, owner_turns).reshape((TARGETS, 1))
    dest_cell = touch_ends(jax.random.randint(arg_keys[5], (TARGETS,), 0, FP * FT), jax.random.fold_in(arg_keys[5], 1), 0, (FP * FT) - 1).astype(jnp.int32)
    corner_base = draw_corner_base(jax.random.fold_in(arg_keys[8], 71), 0)
    fractions = jnp.clip(1.0 * jax.random.uniform(arg_keys[7], (3, TARGETS), jnp.float32) ** block_levels(arg_keys[7], (3, TARGETS), ((1, 256),), -0.2, 0.2), 0.0, 1.0)
    return {"corona": corona, "kappa": kappa, "mixing": mixing, "helio_prev": helio_prev, "owner": owner, "dest_cell": dest_cell, "corner_base": corner_base, "fractions": fractions}


def flux_step(field, cond, mixing):
    center = field[:, 1:-1, 1:-1, :]
    cond_c = cond[1:-1, 1:-1, :]
    radial = jnp.pad(center, ((0, 0), (0, 0), (0, 0), (1, 1)))
    cond_r = jnp.pad(cond_c, ((0, 0), (0, 0), (1, 1)))
    pairs = [(field[:, 2:, 1:-1, :], cond[2:, 1:-1, :]), (field[:, :-2, 1:-1, :], cond[:-2, 1:-1, :]),
             (field[:, 1:-1, 2:, :], cond[1:-1, 2:, :]), (field[:, 1:-1, :-2, :], cond[1:-1, :-2, :]),
             (radial[..., 2:], cond_r[..., 2:]), (radial[..., :-2], cond_r[..., :-2])]
    lapl = jnp.zeros_like(center)
    for near, cond_n in pairs:
        lapl = lapl + (0.5 * (cond_c + cond_n))[None] * (near - center)
    mixed = jnp.einsum("gf,fabr->gabr", mixing, center, precision=lax.Precision.HIGHEST)
    return center + 0.15 * lapl + 0.3 * mixed


def reference(corona, kappa, mixing, helio_prev, owner, dest_cell, corner_base, fractions):
    cond = jnp.pad(kappa, ((1, 1), (1, 1), (0, 0)))
    pad_spec = ((0, 0), (1, 1), (1, 1), (0, 0))
    first = flux_step(jnp.pad(corona, pad_spec), cond, mixing)
    stepped = flux_step(jnp.pad(first, pad_spec), cond, mixing)
    shell = stepped[:, :, :, NR - SH:]
    target = jnp.arange(TARGETS, dtype=jnp.int32)
    source = target // T_DEV
    src_lat = source // N_LON
    src_lon = source % N_LON
    t_idx = corner_base // (CP * SH)
    p_idx = (corner_base // SH) % CP
    r_idx = corner_base % SH
    g_lat = src_lat * CT + t_idx
    g_lon = src_lon * CP + p_idx
    value = jnp.zeros((FIELDS, TARGETS), jnp.float32)
    for a in range(2):
        for b in range(2):
            for c in range(2):
                weight = (fractions[0] if a else 1.0 - fractions[0]) * (fractions[1] if b else 1.0 - fractions[1]) * (fractions[2] if c else 1.0 - fractions[2])
                value = value + weight[None] * shell[:, g_lat + a, g_lon + b, r_idx + c]
    dest_owner = owner[:, 0]
    own_lat = dest_owner // N_LON
    own_lon = dest_owner % N_LON
    cell_p = dest_cell // FT
    cell_t = dest_cell % FT
    flat_idx = ((own_lon * FP + cell_p) * NFT + own_lat * FT + cell_t).astype(jnp.int32)
    added = jax.ops.segment_sum(value.T, flat_idx, num_segments=NFP * NFT)
    coupled = helio_prev + added.T.reshape(FIELDS, NFP, NFT)
    ext = jnp.pad(coupled, ((0, 0), (1, 1), (1, 1)))
    helio_face = coupled + 0.2 * (ext[:, 2:, 1:-1] + ext[:, :-2, 1:-1] + ext[:, 1:-1, 2:] + ext[:, 1:-1, :-2] - 4.0 * coupled)
    return stepped, helio_face
```

```python
import functools

import jax
import jax.numpy as jnp
from jax import lax
from jax.experimental import pallas as pl
from jax.experimental.pallas import tpu as pltpu
from jax.sharding import PartitionSpec as P

SH = 8
CAP = 16
BLOCK = 256
VMEM = pltpu.VMEM
F32 = jnp.float32
BF16 = jnp.bfloat16


def vspec():
    return pl.BlockSpec(memory_space=VMEM)


def sspec():
    return pl.BlockSpec(memory_space=pltpu.SMEM)


def iota(shape, dim):
    return lax.broadcasted_iota(jnp.int32, shape, dim)


def halves(x):
    high = x.astype(BF16)
    return high, (x - high.astype(F32)).astype(BF16)


def neighbours(axis, step):
    count = lax.axis_size(axis)
    return [(i, i + step) for i in range(count) if 0 <= i + step < count]


def theta_edges(corona, kappa, low, high):
    fields, _, tile_p, radial = low.shape[0] - 1, None, low.shape[2], low.shape[3]
    tile_t = corona.shape[1]
    low[:fields] = corona[:, 0:2]
    low[fields] = kappa[0:2]
    high[:fields] = corona[:, tile_t - 2 : tile_t]
    high[fields] = kappa[tile_t - 2 : tile_t]


def phi_edges(tile_t, tile_p, corona, kappa, from_low, from_high, low, high):
    fields = corona.shape[0]
    for f in range(fields + 1):
        for out, near, far in ((low, 0, 1), (high, tile_p - 1, tile_p - 2)):
            for at, col in ((0, near), (tile_t, far)):
                rows = pl.ds(col, tile_t, stride=tile_p)
                out[f, at : at + tile_t, :] = corona[f, rows, :] if f < fields else kappa[rows, :]
            out[f, 2 * tile_t : 2 * tile_t + 1, :] = from_low[f, 1, near : near + 1, :]
            out[f, 2 * tile_t + 1 : 2 * tile_t + 2, :] = from_high[f, 0, near : near + 1, :]


def ranks(face_t, owner, dest, rank_out, meta_out):
    n_dev = meta_out.shape[0]
    count = owner.shape[1]
    width = min(BLOCK, count)
    before = (iota((width, width), 0) < iota((width, width), 1)).astype(F32).astype(BF16)
    owners = iota((n_dev, width), 0)
    slots = iota((CAP, width), 0).astype(F32)
    carry = jnp.zeros((n_dev, 1), F32)
    meta = jnp.zeros((n_dev, 128), F32)
    for b in range(count // width):
        cols = slice(b * width, (b + 1) * width)
        hit = owners == owner[:, cols]
        hit_f = jnp.where(hit, 1.0, 0.0)
        hit_b = hit_f.astype(BF16)
        ahead = jnp.dot(hit_b, before, preferred_element_type=F32) + carry
        rank = jnp.sum(jnp.where(hit, ahead, 0.0), axis=0, keepdims=True)
        carry = ahead[:, width - 1 : width] + hit_f[:, width - 1 : width]
        rank_out[:, cols] = rank
        cell = dest[:, cols]
        cell_t = (cell % face_t).astype(F32)
        cell_p = (cell // face_t).astype(F32)
        mine = slots == rank
        rows = jnp.concatenate(
            [
                jnp.where(mine, cell_t, 0.0),
                jnp.where(mine, cell_p, 0.0),
                jnp.zeros((128 - 2 * CAP, width), F32),
            ],
            axis=0,
        ).astype(BF16)
        meta = meta + lax.dot_general(
            hit_b, rows, (((1,), (1,)), ((), ())), preferred_element_type=F32
        )
    meta_out[...] = meta


def flux(fields, mixing, cond, value, inner):
    kc, *kn = cond()
    radial = kc.shape[-1]
    lane = iota(kc.shape, 1)
    weights = [0.075 * (kc + k) for k in kn]
    k_up = jnp.where(lane == radial - 1, 0.0, pltpu.roll(kc, radial - 1, 1))
    k_down = jnp.where(lane == 0, 0.0, pltpu.roll(kc, 1, 1))
    up = 0.075 * (kc + k_up)
    down = 0.075 * (kc + k_down)
    total = 1.0 - ((weights[0] + weights[1]) + (weights[2] + weights[3]) + (up + down))
    up = jnp.where(lane == radial - 1, 0.0, up)
    down = jnp.where(lane == 0, 0.0, down)
    centres = [inner(f) for f in range(fields)]
    for g in range(fields):
        c = centres[g]
        acc = total * c
        for w, near in zip(weights, value(g)):
            acc = acc + w * near
        acc = acc + up * pltpu.roll(c, radial - 1, 1) + down * pltpu.roll(c, 1, 1)
        for f in range(fields):
            acc = acc + (0.3 * mixing[g, f]) * centres[f]
        yield g, acc


def main(
    n_dev, mixing, place, corona, kappa, t_low, t_high, p_low, p_high, base, frac, owner, rank,
    meta, stepped, message, wide, once, column,
):
    fields, tile_t, tile_p, radial = corona.shape
    wide_n = tile_p + 16
    for f in range(fields + 1):
        own = corona[f] if f < fields else kappa[...]
        wide[f, 2 : 2 + tile_t, 8 : 8 + tile_p, :] = own
        wide[f, 0:2, 8 : 8 + tile_p, :] = t_low[f]
        wide[f, 2 + tile_t : 4 + tile_t, 8 : 8 + tile_p, :] = t_high[f]
        for side, (halo, near, far) in enumerate(((p_low, 7, 6), (p_high, 8 + tile_p, 9 + tile_p))):
            for t in range(tile_t):
                wide[f, 2 + t, near : near + 1, :] = halo[f, t : t + 1, :]
            wide[f, 1, near : near + 1, :] = halo[f, 2 * tile_t : 2 * tile_t + 1, :]
            wide[f, 2 + tile_t, near : near + 1, :] = halo[f, 2 * tile_t + 1 : 2 * tile_t + 2, :]
            column[side, f, 8 : 8 + tile_t, :] = halo[f, 0:tile_t, :]
            column[side, f, 7:8, :] = halo[f, 2 * tile_t : 2 * tile_t + 1, :]
            column[side, f, 8 + tile_t : 9 + tile_t, :] = halo[f, 2 * tile_t + 1 : 2 * tile_t + 2, :]

    lat, lon, last_lat, last_lon = place[0], place[1], place[2], place[3]

    def around(ref, f, t, dt):
        return [
            ref[f, t + dt - 1, 8 : 8 + tile_p, :],
            ref[f, t + dt + 1, 8 : 8 + tile_p, :],
            ref[f, t + dt, 7 : 7 + tile_p, :],
            ref[f, t + dt, 9 : 9 + tile_p, :],
        ]

    def first_row(t, _):
        exists = jnp.logical_and(
            jnp.logical_or(t > 0, lat > 0), jnp.logical_or(t < tile_t + 1, lat < last_lat)
        )
        keep = jnp.where(exists, 1.0, 0.0)
        for g, acc in flux(
            fields,
            mixing,
            lambda: [wide[fields, t + 1, 8 : 8 + tile_p, :]] + around(wide, fields, t, 1),
            lambda f: around(wide, f, t, 1),
            lambda f: wide[f, t + 1, 8 : 8 + tile_p, :],
        ):
            once[g, t, 8 : 8 + tile_p, :] = acc * keep
        return 0

    lax.fori_loop(0, tile_t + 2, first_row, 0)

    for side, halo, own_col, at in ((0, p_low, 0, 7), (1, p_high, tile_p - 1, 8 + tile_p)):
        keep = jnp.where(lon > 0, 1.0, 0.0) if side == 0 else jnp.where(lon < last_lon, 1.0, 0.0)

        def beside(f, side=side, halo=halo, own_col=own_col):
            own = jnp.concatenate(
                [wide[f, 2 + t, 8 + own_col : 9 + own_col, :] for t in range(tile_t)], axis=0
            )
            return [
                column[side, f, 7 : 7 + tile_t, :],
                column[side, f, 9 : 9 + tile_t, :],
                halo[f, tile_t : 2 * tile_t, :],
                own,
            ]

        for g, acc in flux(
            fields,
            mixing,
            lambda: [column[side, fields, 8 : 8 + tile_t, :]] + beside(fields),
            beside,
            lambda f: column[side, f, 8 : 8 + tile_t, :],
        ):
            acc = acc * keep
            for t in range(tile_t):
                once[g, 1 + t, at : at + 1, :] = acc[t : t + 1, :]

    def second_row(t, _):
        for g, acc in flux(
            fields,
            mixing,
            lambda: [wide[fields, t + 2, 8 : 8 + tile_p, :]] + around(wide, fields, t, 2),
            lambda f: around(once, f, t, 1),
            lambda f: once[f, t + 1, 8 : 8 + tile_p, :],
        ):
            stepped[g, t] = acc
        return 0

    lax.fori_loop(0, tile_t, second_row, 0)

    columns = tile_t * tile_p
    lane = iota((columns, radial), 1)
    shell = jnp.zeros((columns, radial), F32)
    for f in range(fields):
        moved = pltpu.roll(stepped[f].reshape(columns, radial), (f * SH + SH) % radial, 1)
        shell = jnp.where(lane // SH == f, moved, shell)
    high = shell.astype(BF16).astype(F32)
    both = high + pltpu.roll(shell - high, fields * SH, 1)
    left = jnp.transpose(both).astype(BF16)

    count = base.shape[1]
    width = min(BLOCK, count)
    owners = iota((n_dev, width), 0)
    packed = jnp.zeros((n_dev, 2 * fields * CAP), F32)
    for b in range(count // width):
        cols = slice(b * width, (b + 1) * width)
        cell = base[:, cols]

        def pair(size, at, fraction):
            rows = iota((size, width), 0)
            return jnp.where(rows == at, 1.0 - fraction, jnp.where(rows == at + 1, fraction, 0.0))

        w_t = pair(tile_t, cell // (tile_p * SH), frac[0:1, cols])
        w_p = pair(tile_p, (cell // SH) % tile_p, frac[1:2, cols])
        w_r = pair(SH, cell % SH, frac[2:3, cols])
        table = (w_t[:, None, :] * w_p[None, :, :]).reshape(columns, width)
        table_high, table_low = halves(table)
        coarse = jnp.dot(left, table_high, preferred_element_type=F32)
        fine = jnp.dot(left[: fields * SH], table_low, preferred_element_type=F32)
        by_layer = coarse[: fields * SH] + (coarse[fields * SH :] + fine)
        value = jnp.sum(by_layer.reshape(fields, SH, width) * w_r[None], axis=1)
        order = rank[:, cols]
        placed = jnp.concatenate(
            [jnp.where(order == float(k), value, 0.0) for k in range(CAP)], axis=0
        )
        placed_high, placed_low = halves(placed)
        hit = jnp.where(owners == owner[:, cols], 1.0, 0.0).astype(BF16)
        packed = packed + lax.dot_general(
            hit,
            jnp.concatenate([placed_high, placed_low], axis=0),
            (((1,), (1,)), ((), ())),
            preferred_element_type=F32,
        )
    half = fields * CAP
    message[pl.ds(0, n_dev, stride=2), :] = packed[:, :half] + packed[:, half:]
    message[pl.ds(1, n_dev, stride=2), :] = meta[...]


def land(n_dev, got, prev, coupled, p_first, p_last, t_first, t_last):
    fields, face_p, face_t = prev.shape
    values = jnp.transpose(got[pl.ds(0, n_dev, stride=2), :])
    cells = jnp.transpose(got[pl.ds(1, n_dev, stride=2), :])
    along_t = iota((face_t, n_dev), 0).astype(F32)
    along_p = iota((face_p, n_dev), 0).astype(F32)
    rows = fields * face_p
    total = jnp.zeros((2 * rows, face_t), F32)
    for k in range(CAP):
        at_t = jnp.where(along_t == cells[k : k + 1, :], 1.0, 0.0).astype(BF16)
        at_p = along_p == cells[CAP + k : CAP + k + 1, :]
        value = values[k * fields : (k + 1) * fields, :]
        high = value.astype(BF16).astype(F32)
        parts = [
            jnp.where(at_p[None], part[:, None, :], 0.0).reshape(rows, n_dev).astype(BF16)
            for part in (high, value - high)
        ]
        total = total + lax.dot_general(
            jnp.concatenate(parts, axis=0),
            at_t,
            (((1,), (1,)), ((), ())),
            preferred_element_type=F32,
        )
    new = prev[...].reshape(rows, face_t) + (total[:rows] + total[rows:])
    coupled[...] = new.reshape(fields, face_p, face_t)
    turned = jnp.transpose(new)
    t_first[...] = turned[0:1, :]
    t_last[...] = turned[face_t - 1 : face_t, :]
    for f in range(fields):
        p_first[f : f + 1, :] = new[f * face_p : f * face_p + 1, :]
        p_last[f : f + 1, :] = new[(f + 1) * face_p - 1 : (f + 1) * face_p, :]


def smooth(coupled, p_low, p_high, t_low, t_high, out):
    fields, face_p, face_t = coupled.shape
    x = coupled[...]
    row = iota((face_p, face_t), 0)[None]
    lane = iota((face_p, face_t), 1)[None]

    def column(ref):
        return jnp.transpose(jnp.broadcast_to(ref[...], (face_t, fields * face_p))).reshape(x.shape)

    below = jnp.where(row == 0, p_low[...][:, None, :], pltpu.roll(x, 1, 1))
    above = jnp.where(row == face_p - 1, p_high[...][:, None, :], pltpu.roll(x, face_p - 1, 1))
    left = jnp.where(lane == 0, column(t_low), pltpu.roll(x, 1, 2))
    right = jnp.where(lane == face_t - 1, column(t_high), pltpu.roll(x, face_t - 1, 2))
    out[...] = x + 0.2 * (above + below + right + left - 4.0 * x)


def call(kernel, outs, specs, name, scratch=()):
    return pl.pallas_call(
        kernel,
        out_shape=[jax.ShapeDtypeStruct(s, F32) for s in outs],
        in_specs=specs,
        out_specs=[vspec()] * len(outs),
        scratch_shapes=list(scratch),
        name=name,
        compiler_params=pltpu.CompilerParams(vmem_limit_bytes=40 * 1024 * 1024),
    )


def body(corona, kappa, mixing, helio_prev, owner, dest_cell, corner_base, fractions):
    fields, tile_t, tile_p, radial = corona.shape
    n_lat, n_lon = lax.axis_size("lat"), lax.axis_size("lon")
    n_dev = n_lat * n_lon
    count = corner_base.shape[0]
    _, face_p, face_t = helio_prev.shape
    owner = owner.reshape(1, count)
    dest_cell = dest_cell.reshape(1, count)
    base = corner_base.reshape(1, count)
    place = jnp.stack(
        [lax.axis_index("lat"), lax.axis_index("lon"), jnp.int32(n_lat - 1), jnp.int32(n_lon - 1)]
    )

    edge = (fields + 1, 2, tile_p, radial)
    low, high = call(theta_edges, [edge] * 2, [vspec()] * 2, "theta_edges")(corona, kappa)
    t_low = lax.ppermute(high, "lat", neighbours("lat", 1))
    t_high = lax.ppermute(low, "lat", neighbours("lat", -1))

    rank, meta = call(
        functools.partial(ranks, face_t), [(1, count), (n_dev, 128)], [vspec()] * 2, "ranks"
    )(owner, dest_cell)

    edge = (fields + 1, 2 * tile_t + 8, radial)
    low, high = call(
        functools.partial(phi_edges, tile_t, tile_p), [edge] * 2, [vspec()] * 4, "phi_edges"
    )(
        corona.reshape(fields, tile_t * tile_p, radial),
        kappa.reshape(tile_t * tile_p, radial),
        t_low,
        t_high,
    )
    p_low = lax.ppermute(high, "lon", neighbours("lon", 1))
    p_high = lax.ppermute(low, "lon", neighbours("lon", -1))

    stepped, message = call(
        functools.partial(main, n_dev),
        [corona.shape, (2 * n_dev, 128)],
        [sspec()] * 2 + [vspec()] * 11,
        "steps",
        [
            VMEM((fields + 1, tile_t + 4, tile_p + 16, radial), F32),
            VMEM((fields, tile_t + 2, tile_p + 16, radial), F32),
            VMEM((2, fields + 1, tile_t + 16, radial), F32),
        ],
    )(
        mixing, place, corona, kappa, t_low, t_high, p_low, p_high, base, fractions, owner, rank,
        meta,
    )

    got = lax.all_to_all(message, ("lat", "lon"), split_axis=0, concat_axis=0, tiled=True)

    coupled, p_first, p_last, t_first, t_last = call(
        functools.partial(land, n_dev),
        [helio_prev.shape, (fields, face_t), (fields, face_t)] + [(1, fields * face_p)] * 2,
        [vspec()] * 2,
        "land",
    )(got, helio_prev)
    from_t_low = lax.ppermute(t_last, "lat", neighbours("lat", 1))
    from_t_high = lax.ppermute(t_first, "lat", neighbours("lat", -1))
    from_p_low = lax.ppermute(p_last, "lon", neighbours("lon", 1))
    from_p_high = lax.ppermute(p_first, "lon", neighbours("lon", -1))
    (face,) = call(smooth, [helio_prev.shape], [vspec()] * 5, "smooth")(
        coupled, from_p_low, from_p_high, from_t_low, from_t_high
    )
    return (stepped, face)


def solution(mesh):
    return jax.shard_map(
        body,
        mesh=mesh,
        in_specs=(
            P(None, "lat", "lon", None),
            P("lat", "lon", None),
            P(),
            P(None, "lon", "lat"),
            P(("lat", "lon"), None),
            P(("lat", "lon")),
            P(("lat", "lon")),
            P(None, ("lat", "lon")),
        ),
        out_specs=(P(None, "lat", "lon", None), P(None, "lon", "lat")),
        check_vma=False,
    )
```

```python
import functools

import jax
import jax.numpy as jnp
from jax import lax
from jax.experimental import pallas as pl
from jax.experimental.pallas import tpu as pltpu
from jax.sharding import PartitionSpec as P

SH = 8
CAP = 16
BLOCK = 256
VMEM = pltpu.VMEM
F32 = jnp.float32
BF16 = jnp.bfloat16


def vspec():
    return pl.BlockSpec(memory_space=VMEM)


def sspec():
    return pl.BlockSpec(memory_space=pltpu.SMEM)


def iota(shape, dim):
    return lax.broadcasted_iota(jnp.int32, shape, dim)


def halves(x):
    high = x.astype(BF16)
    return high, (x - high.astype(F32)).astype(BF16)


def shifted(x, axis, step):
    count = lax.axis_size(axis)
    return lax.ppermute(x, axis, [(i, (i + step) % count) for i in range(count)])


def theta_edges(corona, kappa, low, high, sems):
    fields, tile_t = corona.shape[0], corona.shape[1]
    copies = []
    for side, (out, start) in enumerate(((low, 0), (high, tile_t - 2))):
        rows = pl.ds(start, 2)
        copies.append(
            pltpu.make_async_copy(corona.at[:, rows], out.at[pl.ds(0, fields)], sems.at[2 * side])
        )
        copies.append(pltpu.make_async_copy(kappa.at[rows], out.at[fields], sems.at[2 * side + 1]))
    for copy in copies:
        copy.start()
    for copy in copies:
        copy.wait()


def phi_edges(tile_t, tile_p, corona, kappa, low, high):
    fields = corona.shape[0]
    for f in range(fields + 1):
        for out, near, far in ((low, 0, 1), (high, tile_p - 1, tile_p - 2)):
            for at, col in ((0, near), (tile_t, far)):
                rows = pl.ds(col, tile_t, stride=tile_p)
                out[f, at : at + tile_t, :] = corona[f, rows, :] if f < fields else kappa[rows, :]


def corner_cells(t_low, t_high, low, high):
    count, _, tile_p, _ = t_low.shape
    for f in range(count):
        for out, col in ((low, 0), (high, tile_p - 1)):
            out[2 * f : 2 * f + 1, :] = t_low[f, 1, col : col + 1, :]
            out[2 * f + 1 : 2 * f + 2, :] = t_high[f, 0, col : col + 1, :]


def ranks(face_t, owner, dest, rank_out, meta_out):
    n_dev = meta_out.shape[0]
    count = owner.shape[1]
    width = min(BLOCK, count)
    before = (iota((width, width), 0) < iota((width, width), 1)).astype(F32).astype(BF16)
    owners = iota((n_dev, width), 0)
    slots = iota((CAP, width), 0).astype(F32)
    carry = jnp.zeros((n_dev, 1), F32)
    meta = jnp.zeros((n_dev, 128), F32)
    for b in range(count // width):
        cols = slice(b * width, (b + 1) * width)
        hit = owners == owner[:, cols]
        hit_f = jnp.where(hit, 1.0, 0.0)
        hit_b = hit_f.astype(BF16)
        ahead = jnp.dot(hit_b, before, preferred_element_type=F32) + carry
        rank = jnp.sum(jnp.where(hit, ahead, 0.0), axis=0, keepdims=True)
        carry = ahead[:, width - 1 : width] + hit_f[:, width - 1 : width]
        rank_out[:, cols] = rank
        cell = dest[:, cols]
        cell_t = (cell % face_t).astype(F32)
        cell_p = (cell // face_t).astype(F32)
        mine = slots == rank
        rows = jnp.concatenate(
            [
                jnp.where(mine, cell_t, 0.0),
                jnp.where(mine, cell_p, 0.0),
                jnp.zeros((128 - 2 * CAP, width), F32),
            ],
            axis=0,
        ).astype(BF16)
        meta = meta + lax.dot_general(
            hit_b, rows, (((1,), (1,)), ((), ())), preferred_element_type=F32
        )
    meta_out[...] = meta


def flux(fields, mixing, cond, value, inner):
    kc, *kn = cond()
    radial = kc.shape[-1]
    lane = iota(kc.shape, 1)
    weights = [0.075 * (kc + k) for k in kn]
    k_up = jnp.where(lane == radial - 1, 0.0, pltpu.roll(kc, radial - 1, 1))
    k_down = jnp.where(lane == 0, 0.0, pltpu.roll(kc, 1, 1))
    up = 0.075 * (kc + k_up)
    down = 0.075 * (kc + k_down)
    total = 1.0 - ((weights[0] + weights[1]) + (weights[2] + weights[3]) + (up + down))
    up = jnp.where(lane == radial - 1, 0.0, up)
    down = jnp.where(lane == 0, 0.0, down)
    centres = [inner(f) for f in range(fields)]
    for g in range(fields):
        c = centres[g]
        acc = total * c
        for w, near in zip(weights, value(g)):
            acc = acc + w * near
        acc = acc + up * pltpu.roll(c, radial - 1, 1) + down * pltpu.roll(c, 1, 1)
        for f in range(fields):
            acc = acc + (0.3 * mixing[g, f]) * centres[f]
        yield g, acc


def main(
    n_dev, mixing, place, corona, kappa, t_low, t_high, p_low, p_high, c_low, c_high, base, frac,
    owner, rank, meta, stepped, message, wide, once, column,
):
    fields, tile_t, tile_p, radial = corona.shape
    lat, lon, last_lat, last_lon = place[0], place[1], place[2], place[3]
    has_t = [jnp.where(lat > 0, 1.0, 0.0), jnp.where(lat < last_lat, 1.0, 0.0)]
    has_p = [jnp.where(lon > 0, 1.0, 0.0), jnp.where(lon < last_lon, 1.0, 0.0)]
    for f in range(fields + 1):
        own = corona[f] if f < fields else kappa[...]
        wide[f, 2 : 2 + tile_t, 8 : 8 + tile_p, :] = own
        wide[f, 0:2, 8 : 8 + tile_p, :] = t_low[f] * has_t[0]
        wide[f, 2 + tile_t : 4 + tile_t, 8 : 8 + tile_p, :] = t_high[f] * has_t[1]
        for side, (halo, corner, near) in enumerate(
            ((p_low, c_low, 7), (p_high, c_high, 8 + tile_p))
        ):
            column[side, f, 8 : 8 + tile_t, :] = halo[f, 0:tile_t, :] * has_p[side]
            below = corner[2 * f : 2 * f + 1, :] * (has_p[side] * has_t[0])
            above = corner[2 * f + 1 : 2 * f + 2, :] * (has_p[side] * has_t[1])
            column[side, f, 7:8, :] = below
            column[side, f, 8 + tile_t : 9 + tile_t, :] = above
            for t in range(tile_t + 2):
                wide[f, 1 + t, near : near + 1, :] = column[side, f, 7 + t : 8 + t, :]

    def around(ref, f, t, dt):
        return [
            ref[f, t + dt - 1, 8 : 8 + tile_p, :],
            ref[f, t + dt + 1, 8 : 8 + tile_p, :],
            ref[f, t + dt, 7 : 7 + tile_p, :],
            ref[f, t + dt, 9 : 9 + tile_p, :],
        ]

    def first_row(t, _):
        exists = jnp.logical_and(
            jnp.logical_or(t > 0, lat > 0), jnp.logical_or(t < tile_t + 1, lat < last_lat)
        )
        keep = jnp.where(exists, 1.0, 0.0)
        for g, acc in flux(
            fields,
            mixing,
            lambda: [wide[fields, t + 1, 8 : 8 + tile_p, :]] + around(wide, fields, t, 1),
            lambda f: around(wide, f, t, 1),
            lambda f: wide[f, t + 1, 8 : 8 + tile_p, :],
        ):
            once[g, t, 8 : 8 + tile_p, :] = acc * keep
        return 0

    lax.fori_loop(0, tile_t + 2, first_row, 0)

    for side, halo, own_col, at in ((0, p_low, 0, 7), (1, p_high, tile_p - 1, 8 + tile_p)):
        def beside(f, side=side, halo=halo, own_col=own_col):
            own = jnp.concatenate(
                [wide[f, 2 + t, 8 + own_col : 9 + own_col, :] for t in range(tile_t)], axis=0
            )
            return [
                column[side, f, 7 : 7 + tile_t, :],
                column[side, f, 9 : 9 + tile_t, :],
                halo[f, tile_t : 2 * tile_t, :] * has_p[side],
                own,
            ]

        for g, acc in flux(
            fields,
            mixing,
            lambda: [column[side, fields, 8 : 8 + tile_t, :]] + beside(fields),
            beside,
            lambda f: column[side, f, 8 : 8 + tile_t, :],
        ):
            acc = acc * has_p[side]
            for t in range(tile_t):
                once[g, 1 + t, at : at + 1, :] = acc[t : t + 1, :]

    def second_row(t, _):
        for g, acc in flux(
            fields,
            mixing,
            lambda: [wide[fields, t + 2, 8 : 8 + tile_p, :]] + around(wide, fields, t, 2),
            lambda f: around(once, f, t, 1),
            lambda f: once[f, t + 1, 8 : 8 + tile_p, :],
        ):
            stepped[g, t] = acc
        return 0

    lax.fori_loop(0, tile_t, second_row, 0)

    columns = tile_t * tile_p
    lane = iota((columns, radial), 1)
    shell = jnp.zeros((columns, radial), F32)
    for f in range(fields):
        moved = pltpu.roll(stepped[f].reshape(columns, radial), (f * SH + SH) % radial, 1)
        shell = jnp.where(lane // SH == f, moved, shell)
    high = shell.astype(BF16).astype(F32)
    both = high + pltpu.roll(shell - high, fields * SH, 1)
    left = jnp.transpose(both).astype(BF16)

    count = base.shape[1]
    width = min(BLOCK, count)
    owners = iota((n_dev, width), 0)
    packed = jnp.zeros((n_dev, 2 * fields * CAP), F32)
    for b in range(count // width):
        cols = slice(b * width, (b + 1) * width)
        cell = base[:, cols]

        def pair(size, at, fraction):
            rows = iota((size, width), 0)
            return jnp.where(rows == at, 1.0 - fraction, jnp.where(rows == at + 1, fraction, 0.0))

        w_t = pair(tile_t, cell // (tile_p * SH), frac[0:1, cols])
        w_p = pair(tile_p, (cell // SH) % tile_p, frac[1:2, cols])
        w_r = pair(SH, cell % SH, frac[2:3, cols])
        table = (w_t[:, None, :] * w_p[None, :, :]).reshape(columns, width)
        table_high, table_low = halves(table)
        coarse = jnp.dot(left, table_high, preferred_element_type=F32)
        fine = jnp.dot(left[: fields * SH], table_low, preferred_element_type=F32)
        by_layer = coarse[: fields * SH] + (coarse[fields * SH :] + fine)
        value = jnp.sum(by_layer.reshape(fields, SH, width) * w_r[None], axis=1)
        order = rank[:, cols]
        placed = jnp.concatenate(
            [jnp.where(order == float(k), value, 0.0) for k in range(CAP)], axis=0
        )
        placed_high, placed_low = halves(placed)
        hit = jnp.where(owners == owner[:, cols], 1.0, 0.0).astype(BF16)
        packed = packed + lax.dot_general(
            hit,
            jnp.concatenate([placed_high, placed_low], axis=0),
            (((1,), (1,)), ((), ())),
            preferred_element_type=F32,
        )
    half = fields * CAP
    message[pl.ds(0, n_dev, stride=2), :] = packed[:, :half] + packed[:, half:]
    message[pl.ds(1, n_dev, stride=2), :] = meta[...]


def land(n_dev, got, prev, coupled, p_first, p_last, t_first, t_last):
    fields, face_p, face_t = prev.shape
    values = jnp.transpose(got[pl.ds(0, n_dev, stride=2), :])
    cells = jnp.transpose(got[pl.ds(1, n_dev, stride=2), :])
    along_t = iota((face_t, n_dev), 0).astype(F32)
    along_p = iota((face_p, n_dev), 0).astype(F32)
    rows = fields * face_p
    total = jnp.zeros((2 * rows, face_t), F32)
    for k in range(CAP):
        at_t = jnp.where(along_t == cells[k : k + 1, :], 1.0, 0.0).astype(BF16)
        at_p = along_p == cells[CAP + k : CAP + k + 1, :]
        value = values[k * fields : (k + 1) * fields, :]
        high = value.astype(BF16).astype(F32)
        parts = [
            jnp.where(at_p[None], part[:, None, :], 0.0).reshape(rows, n_dev).astype(BF16)
            for part in (high, value - high)
        ]
        total = total + lax.dot_general(
            jnp.concatenate(parts, axis=0),
            at_t,
            (((1,), (1,)), ((), ())),
            preferred_element_type=F32,
        )
    new = prev[...].reshape(rows, face_t) + (total[:rows] + total[rows:])
    coupled[...] = new.reshape(fields, face_p, face_t)
    turned = jnp.transpose(new)
    t_first[...] = turned[0:1, :]
    t_last[...] = turned[face_t - 1 : face_t, :]
    for f in range(fields):
        p_first[f : f + 1, :] = new[f * face_p : f * face_p + 1, :]
        p_last[f : f + 1, :] = new[(f + 1) * face_p - 1 : (f + 1) * face_p, :]


def smooth(place, coupled, p_low, p_high, t_low, t_high, out):
    fields, face_p, face_t = coupled.shape
    x = coupled[...]
    row = iota((face_p, face_t), 0)[None]
    lane = iota((face_p, face_t), 1)[None]

    lat, lon, last_lat, last_lon = place[0], place[1], place[2], place[3]

    def rim(ref, exists):
        return ref[...] * jnp.where(exists, 1.0, 0.0)

    def column(edge):
        return jnp.transpose(jnp.broadcast_to(edge, (face_t, fields * face_p))).reshape(x.shape)

    below = jnp.where(row == 0, rim(p_low, lon > 0)[:, None, :], pltpu.roll(x, 1, 1))
    above = jnp.where(
        row == face_p - 1, rim(p_high, lon < last_lon)[:, None, :], pltpu.roll(x, face_p - 1, 1)
    )
    left = jnp.where(lane == 0, column(rim(t_low, lat > 0)), pltpu.roll(x, 1, 2))
    right = jnp.where(
        lane == face_t - 1, column(rim(t_high, lat < last_lat)), pltpu.roll(x, face_t - 1, 2)
    )
    out[...] = x + 0.2 * (above + below + right + left - 4.0 * x)


def call(kernel, outs, specs, name, scratch=(), room=40 * 1024 * 1024):
    return pl.pallas_call(
        kernel,
        out_shape=[jax.ShapeDtypeStruct(s, F32) for s in outs],
        in_specs=specs,
        out_specs=[vspec()] * len(outs),
        scratch_shapes=list(scratch),
        name=name,
        compiler_params=pltpu.CompilerParams(vmem_limit_bytes=room),
    )


def body(corona, kappa, mixing, helio_prev, owner, dest_cell, corner_base, fractions):
    fields, tile_t, tile_p, radial = corona.shape
    n_lat, n_lon = lax.axis_size("lat"), lax.axis_size("lon")
    n_dev = n_lat * n_lon
    count = corner_base.shape[0]
    _, face_p, face_t = helio_prev.shape
    owner = owner.reshape(1, count)
    dest_cell = dest_cell.reshape(1, count)
    base = corner_base.reshape(1, count)
    place = jnp.stack(
        [lax.axis_index("lat"), lax.axis_index("lon"), jnp.int32(n_lat - 1), jnp.int32(n_lon - 1)]
    )

    edge = (fields + 1, 2, tile_p, radial)
    low, high = call(
        theta_edges,
        [edge] * 2,
        [pl.BlockSpec(memory_space=pltpu.HBM)] * 2,
        "theta_edges",
        [pltpu.SemaphoreType.DMA((4,))],
        64 * 1024 * 1024 - 600 * 1024,
    )(corona, kappa)
    t_low = shifted(high, "lat", 1)
    t_high = shifted(low, "lat", -1)

    edge = (fields + 1, 2 * tile_t, radial)
    low, high = call(
        functools.partial(phi_edges, tile_t, tile_p), [edge] * 2, [vspec()] * 2, "phi_edges"
    )(corona.reshape(fields, tile_t * tile_p, radial), kappa.reshape(tile_t * tile_p, radial))
    p_low = shifted(high, "lon", 1)
    p_high = shifted(low, "lon", -1)

    rank, meta = call(
        functools.partial(ranks, face_t), [(1, count), (n_dev, 128)], [vspec()] * 2, "ranks"
    )(owner, dest_cell)

    edge = (2 * (fields + 1), radial)
    low, high = call(corner_cells, [edge] * 2, [vspec()] * 2, "corner_cells")(t_low, t_high)
    c_low = shifted(high, "lon", 1)
    c_high = shifted(low, "lon", -1)

    stepped, message = call(
        functools.partial(main, n_dev),
        [corona.shape, (2 * n_dev, 128)],
        [sspec()] * 2 + [vspec()] * 13,
        "steps",
        [
            VMEM((fields + 1, tile_t + 4, tile_p + 16, radial), F32),
            VMEM((fields, tile_t + 2, tile_p + 16, radial), F32),
            VMEM((2, fields + 1, tile_t + 16, radial), F32),
        ],
    )(
        mixing, place, corona, kappa, t_low, t_high, p_low, p_high, c_low, c_high, base, fractions,
        owner, rank, meta,
    )

    got = lax.all_to_all(message, ("lat", "lon"), split_axis=0, concat_axis=0, tiled=True)

    coupled, p_first, p_last, t_first, t_last = call(
        functools.partial(land, n_dev),
        [helio_prev.shape, (fields, face_t), (fields, face_t)] + [(1, fields * face_p)] * 2,
        [vspec()] * 2,
        "land",
    )(got, helio_prev)
    from_t_low = shifted(t_last, "lat", 1)
    from_t_high = shifted(t_first, "lat", -1)
    from_p_low = shifted(p_last, "lon", 1)
    from_p_high = shifted(p_first, "lon", -1)
    (face,) = call(smooth, [helio_prev.shape], [sspec()] + [vspec()] * 5, "smooth")(
        place, coupled, from_p_low, from_p_high, from_t_low, from_t_high
    )
    return (stepped, face)


def solution(mesh):
    return jax.shard_map(
        body,
        mesh=mesh,
        in_specs=(
            P(None, "lat", "lon", None),
            P("lat", "lon", None),
            P(),
            P(None, "lon", "lat"),
            P(("lat", "lon"), None),
            P(("lat", "lon")),
            P(("lat", "lon")),
            P(None, ("lat", "lon")),
        ),
        out_specs=(P(None, "lat", "lon", None), P(None, "lon", "lat")),
        check_vma=False,
    )
```

```python
import functools

import jax
import jax.numpy as jnp
from jax import lax
from jax.experimental import pallas as pl
from jax.experimental.pallas import tpu as pltpu
from jax.sharding import PartitionSpec as P

SH = 8
CAP = 16
BLOCK = 256
VMEM = pltpu.VMEM
F32 = jnp.float32
BF16 = jnp.bfloat16


def vspec():
    return pl.BlockSpec(memory_space=VMEM)


def sspec():
    return pl.BlockSpec(memory_space=pltpu.SMEM)


def iota(shape, dim):
    return lax.broadcasted_iota(jnp.int32, shape, dim)


def halves(x):
    high = x.astype(BF16)
    return high, (x - high.astype(F32)).astype(BF16)


def shifted(x, axis, step):
    count = lax.axis_size(axis)
    return lax.ppermute(x, axis, [(i, (i + step) % count) for i in range(count)])


def theta_edges(corona, kappa, low, high, sems):
    fields, tile_t = corona.shape[0], corona.shape[1]
    copies = []
    for side, (out, start) in enumerate(((low, 0), (high, tile_t - 2))):
        rows = pl.ds(start, 2)
        copies.append(
            pltpu.make_async_copy(corona.at[:, rows], out.at[pl.ds(0, fields)], sems.at[2 * side])
        )
        copies.append(pltpu.make_async_copy(kappa.at[rows], out.at[fields], sems.at[2 * side + 1]))
    for copy in copies:
        copy.start()
    for copy in copies:
        copy.wait()


def phi_edges(tile_t, tile_p, corona, kappa, low, high):
    fields = corona.shape[0]
    for f in range(fields + 1):
        for out, near, far in ((low, 0, 1), (high, tile_p - 1, tile_p - 2)):
            for at, col in ((0, near), (tile_t, far)):
                rows = pl.ds(col, tile_t, stride=tile_p)
                out[f, at : at + tile_t, :] = corona[f, rows, :] if f < fields else kappa[rows, :]


def corner_cells(t_low, t_high, low, high):
    count, _, tile_p, _ = t_low.shape
    for f in range(count):
        for out, col in ((low, 0), (high, tile_p - 1)):
            out[0, f : f + 1, :] = t_low[f, 1, col : col + 1, :]
            out[1, f : f + 1, :] = t_high[f, 0, col : col + 1, :]


def exists():
    found = []
    for axis in ("lat", "lon"):
        at, count = lax.axis_index(axis), lax.axis_size(axis)
        found.append([jnp.where(at > 0, 1.0, 0.0), jnp.where(at < count - 1, 1.0, 0.0)])
    return found


def plan(
    face_t, tile_t, tile_p, owner, dest, base, frac, rank_out, meta_out, hit_out, high_out, low_out,
    radial_out,
):
    n_dev = meta_out.shape[0]
    count = owner.shape[1]
    width = min(BLOCK, count)
    before = (iota((width, width), 0) < iota((width, width), 1)).astype(F32).astype(BF16)
    owners = iota((n_dev, width), 0)
    slots = iota((CAP, width), 0).astype(F32)
    carry = jnp.zeros((n_dev, 1), F32)
    meta = jnp.zeros((n_dev, 128), F32)
    for b in range(count // width):
        cols = slice(b * width, (b + 1) * width)
        hit = owners == owner[:, cols]
        hit_f = jnp.where(hit, 1.0, 0.0)
        hit_b = hit_f.astype(BF16)
        hit_out[:, cols] = hit_b
        ahead = jnp.dot(hit_b, before, preferred_element_type=F32) + carry
        rank = jnp.sum(jnp.where(hit, ahead, 0.0), axis=0, keepdims=True)
        carry = ahead[:, width - 1 : width] + hit_f[:, width - 1 : width]
        rank_out[:, cols] = rank
        cell = dest[:, cols]
        cell_t = (cell % face_t).astype(F32)
        cell_p = (cell // face_t).astype(F32)
        mine = slots == rank
        rows = jnp.concatenate(
            [
                jnp.where(mine, cell_t, 0.0),
                jnp.where(mine, cell_p, 0.0),
                jnp.zeros((128 - 2 * CAP, width), F32),
            ],
            axis=0,
        ).astype(BF16)
        meta = meta + lax.dot_general(
            hit_b, rows, (((1,), (1,)), ((), ())), preferred_element_type=F32
        )
        corner = base[:, cols]

        def pair(size, at, fraction):
            rows = iota((size, width), 0)
            return jnp.where(rows == at, 1.0 - fraction, jnp.where(rows == at + 1, fraction, 0.0))

        w_t = pair(tile_t, corner // (tile_p * SH), frac[0:1, cols])
        w_p = pair(tile_p, (corner // SH) % tile_p, frac[1:2, cols])
        radial_out[:, cols] = pair(SH, corner % SH, frac[2:3, cols])
        table = (w_t[:, None, :] * w_p[None, :, :]).reshape(tile_t * tile_p, width)
        high_out[:, cols], low_out[:, cols] = halves(table)
    meta_out[...] = meta


def flux(fields, mixing, cond, value, inner):
    kc, *kn = cond()
    radial = kc.shape[-1]
    lane = iota(kc.shape, 1)
    weights = [0.075 * (kc + k) for k in kn]
    k_up = jnp.where(lane == radial - 1, 0.0, pltpu.roll(kc, radial - 1, 1))
    k_down = jnp.where(lane == 0, 0.0, pltpu.roll(kc, 1, 1))
    up = 0.075 * (kc + k_up)
    down = 0.075 * (kc + k_down)
    total = 1.0 - ((weights[0] + weights[1]) + (weights[2] + weights[3]) + (up + down))
    up = jnp.where(lane == radial - 1, 0.0, up)
    down = jnp.where(lane == 0, 0.0, down)
    centres = [inner(f) for f in range(fields)]
    for g in range(fields):
        c = centres[g]
        acc = total * c
        for w, near in zip(weights, value(g)):
            acc = acc + w * near
        acc = acc + up * pltpu.roll(c, radial - 1, 1) + down * pltpu.roll(c, 1, 1)
        for f in range(fields):
            acc = acc + (0.3 * mixing[g, f]) * centres[f]
        yield g, acc


def steps(mixing, corona, kappa, t_low, t_high, p_low, p_high, stepped, wide, once, column):
    fields, tile_t, tile_p, radial = corona.shape
    has_t, has_p = exists()
    nothing = jnp.zeros((1, radial), F32)
    for f in range(fields + 1):
        own = corona[f] if f < fields else kappa[...]
        wide[f, 2 : 2 + tile_t, 8 : 8 + tile_p, :] = own
        wide[f, 0:2, 8 : 8 + tile_p, :] = t_low[f] * has_t[0]
        wide[f, 2 + tile_t : 4 + tile_t, 8 : 8 + tile_p, :] = t_high[f] * has_t[1]
        for side, (halo, near) in enumerate(((p_low, 7), (p_high, 8 + tile_p))):
            column[side, f, 8 : 8 + tile_t, :] = halo[f, 0:tile_t, :] * has_p[side]
            column[side, f, 7:8, :] = nothing
            column[side, f, 8 + tile_t : 9 + tile_t, :] = nothing
            for t in range(tile_t + 2):
                wide[f, 1 + t, near : near + 1, :] = column[side, f, 7 + t : 8 + t, :]

    def around(ref, f, t, dt):
        return [
            ref[f, t + dt - 1, 8 : 8 + tile_p, :],
            ref[f, t + dt + 1, 8 : 8 + tile_p, :],
            ref[f, t + dt, 7 : 7 + tile_p, :],
            ref[f, t + dt, 9 : 9 + tile_p, :],
        ]

    def first_row(t, _):
        keep = jnp.where(t == 0, has_t[0], jnp.where(t == tile_t + 1, has_t[1], 1.0))
        for g, acc in flux(
            fields,
            mixing,
            lambda: [wide[fields, t + 1, 8 : 8 + tile_p, :]] + around(wide, fields, t, 1),
            lambda f: around(wide, f, t, 1),
            lambda f: wide[f, t + 1, 8 : 8 + tile_p, :],
        ):
            once[g, t, 8 : 8 + tile_p, :] = acc * keep
        return 0

    lax.fori_loop(0, tile_t + 2, first_row, 0)

    for side, halo, own_col, at in ((0, p_low, 0, 7), (1, p_high, tile_p - 1, 8 + tile_p)):
        def beside(f, side=side, halo=halo, own_col=own_col):
            own = jnp.concatenate(
                [wide[f, 2 + t, 8 + own_col : 9 + own_col, :] for t in range(tile_t)], axis=0
            )
            return [
                column[side, f, 7 : 7 + tile_t, :],
                column[side, f, 9 : 9 + tile_t, :],
                halo[f, tile_t : 2 * tile_t, :] * has_p[side],
                own,
            ]

        for g, acc in flux(
            fields,
            mixing,
            lambda: [column[side, fields, 8 : 8 + tile_t, :]] + beside(fields),
            beside,
            lambda f: column[side, f, 8 : 8 + tile_t, :],
        ):
            acc = acc * has_p[side]
            for t in range(tile_t):
                once[g, 1 + t, at : at + 1, :] = acc[t : t + 1, :]

    def second_row(t, _):
        for g, acc in flux(
            fields,
            mixing,
            lambda: [wide[fields, t + 2, 8 : 8 + tile_p, :]] + around(wide, fields, t, 2),
            lambda f: around(once, f, t, 1),
            lambda f: once[f, t + 1, 8 : 8 + tile_p, :],
        ):
            stepped[g, t] = acc
        return 0

    lax.fori_loop(0, tile_t, second_row, 0)


def route(
    n_dev, kappa, p_low, p_high, own_low, own_high, c_low, c_high, stepped, rank, meta, hit,
    table_high, table_low, w_r, patch, message, shell,
):
    fields, tile_t, tile_p, radial = stepped.shape
    has_t, has_p = exists()
    columns = tile_t * tile_p
    lane = iota((columns, radial), 1)
    rows = jnp.zeros((columns, radial), F32)
    for f in range(fields):
        moved = pltpu.roll(stepped[f].reshape(columns, radial), (f * SH + SH) % radial, 1)
        rows = jnp.where(lane // SH == f, moved, rows)
    shell[...] = rows
    for a in range(2):
        for b, (halo, own, diagonal) in enumerate(
            ((p_low, own_low, c_low), (p_high, own_high, c_high))
        ):
            t, p = a * (tile_t - 1), b * (tile_p - 1)
            k_t, u_t = own[a, fields : fields + 1] * has_t[a], own[a, 0:fields] * has_t[a]
            k_p = halo[fields, t : t + 1, :] * has_p[b]
            u_p = jnp.concatenate([halo[f, t : t + 1, :] for f in range(fields)], axis=0) * has_p[b]
            both = has_t[a] * has_p[b]
            k_d, u_d = diagonal[a, fields : fields + 1] * both, diagonal[a, 0:fields] * both
            k = kappa[t, p : p + 1, :]
            by_t = 0.075 * ((k_t + k_d) * u_d - k_d * u_t)
            by_p = 0.075 * ((k_p + k_d) * u_d - k_d * u_p)
            extra = 0.075 * ((k + k_t) * by_t + (k + k_p) * by_p)
            patch[2 * a + b] = extra
            row = jnp.zeros((1, radial), F32)
            for f in range(fields):
                moved = pltpu.roll(extra[f : f + 1], (f * SH + SH) % radial, 1)
                row = jnp.where(lane[0:1] // SH == f, moved, row)
            at = t * tile_p + p
            shell[at : at + 1, :] = shell[at : at + 1, :] + row
    rows = shell[...]
    high = rows.astype(BF16).astype(F32)
    both = high + pltpu.roll(rows - high, fields * SH, 1)
    left = jnp.transpose(both).astype(BF16)

    count = rank.shape[1]
    width = min(BLOCK, count)
    packed = jnp.zeros((n_dev, 2 * fields * CAP), F32)
    for b in range(count // width):
        cols = slice(b * width, (b + 1) * width)
        coarse = jnp.dot(left, table_high[:, cols], preferred_element_type=F32)
        fine = jnp.dot(left[: fields * SH], table_low[:, cols], preferred_element_type=F32)
        by_layer = coarse[: fields * SH] + (coarse[fields * SH :] + fine)
        value = jnp.sum(by_layer.reshape(fields, SH, width) * w_r[:, cols][None], axis=1)
        order = rank[:, cols]
        placed = jnp.concatenate(
            [jnp.where(order == float(k), value, 0.0) for k in range(CAP)], axis=0
        )
        placed_high, placed_low = halves(placed)
        packed = packed + lax.dot_general(
            hit[:, cols],
            jnp.concatenate([placed_high, placed_low], axis=0),
            (((1,), (1,)), ((), ())),
            preferred_element_type=F32,
        )
    half = fields * CAP
    message[pl.ds(0, n_dev, stride=2), :] = packed[:, :half] + packed[:, half:]
    message[pl.ds(1, n_dev, stride=2), :] = meta[...]


def finish(stepped, patch, out):
    fields, tile_t, tile_p, _ = stepped.shape
    out[...] = stepped[...]
    for a in range(2):
        for b in range(2):
            t, p = a * (tile_t - 1), b * (tile_p - 1)
            for f in range(fields):
                out[f, t, p : p + 1, :] = (
                    stepped[f, t, p : p + 1, :] + patch[2 * a + b, f : f + 1, :]
                )


def land(n_dev, got, prev, coupled, p_first, p_last, t_first, t_last):
    fields, face_p, face_t = prev.shape
    values = jnp.transpose(got[pl.ds(0, n_dev, stride=2), :])
    cells = jnp.transpose(got[pl.ds(1, n_dev, stride=2), :])
    along_t = iota((face_t, n_dev), 0).astype(F32)
    along_p = iota((face_p, n_dev), 0).astype(F32)
    rows = fields * face_p
    total = jnp.zeros((2 * rows, face_t), F32)
    for k in range(CAP):
        at_t = jnp.where(along_t == cells[k : k + 1, :], 1.0, 0.0).astype(BF16)
        at_p = along_p == cells[CAP + k : CAP + k + 1, :]
        value = values[k * fields : (k + 1) * fields, :]
        high = value.astype(BF16).astype(F32)
        parts = [
            jnp.where(at_p[None], part[:, None, :], 0.0).reshape(rows, n_dev).astype(BF16)
            for part in (high, value - high)
        ]
        total = total + lax.dot_general(
            jnp.concatenate(parts, axis=0),
            at_t,
            (((1,), (1,)), ((), ())),
            preferred_element_type=F32,
        )
    new = prev[...].reshape(rows, face_t) + (total[:rows] + total[rows:])
    coupled[...] = new.reshape(fields, face_p, face_t)
    turned = jnp.transpose(new)
    t_first[...] = turned[0:1, :]
    t_last[...] = turned[face_t - 1 : face_t, :]
    for f in range(fields):
        p_first[f : f + 1, :] = new[f * face_p : f * face_p + 1, :]
        p_last[f : f + 1, :] = new[(f + 1) * face_p - 1 : (f + 1) * face_p, :]


def smooth(coupled, p_low, p_high, t_low, t_high, out):
    fields, face_p, face_t = coupled.shape
    x = coupled[...]
    row = iota((face_p, face_t), 0)[None]
    lane = iota((face_p, face_t), 1)[None]

    has_t, has_p = exists()

    def rim(ref, has):
        return ref[...] * has

    def column(edge):
        return jnp.transpose(jnp.broadcast_to(edge, (face_t, fields * face_p))).reshape(x.shape)

    below = jnp.where(row == 0, rim(p_low, has_p[0])[:, None, :], pltpu.roll(x, 1, 1))
    above = jnp.where(
        row == face_p - 1, rim(p_high, has_p[1])[:, None, :], pltpu.roll(x, face_p - 1, 1)
    )
    left = jnp.where(lane == 0, column(rim(t_low, has_t[0])), pltpu.roll(x, 1, 2))
    right = jnp.where(
        lane == face_t - 1, column(rim(t_high, has_t[1])), pltpu.roll(x, face_t - 1, 2)
    )
    out[...] = x + 0.2 * (above + below + right + left - 4.0 * x)


def call(kernel, outs, specs, name, scratch=(), out_spec=None, room=40 * 1024 * 1024):
    outs = [s if isinstance(s, jax.ShapeDtypeStruct) else jax.ShapeDtypeStruct(s, F32) for s in outs]
    return pl.pallas_call(
        kernel,
        out_shape=outs,
        in_specs=specs,
        out_specs=[out_spec or vspec()] * len(outs),
        scratch_shapes=list(scratch),
        name=name,
        compiler_params=pltpu.CompilerParams(vmem_limit_bytes=room),
    )


def body(corona, kappa, mixing, helio_prev, owner, dest_cell, corner_base, fractions):
    fields, tile_t, tile_p, radial = corona.shape
    n_lat, n_lon = lax.axis_size("lat"), lax.axis_size("lon")
    n_dev = n_lat * n_lon
    count = corner_base.shape[0]
    _, face_p, face_t = helio_prev.shape
    owner = owner.reshape(1, count)
    dest_cell = dest_cell.reshape(1, count)
    base = corner_base.reshape(1, count)
    edge = (fields + 1, 2, tile_p, radial)
    low, high = call(
        theta_edges,
        [edge] * 2,
        [pl.BlockSpec(memory_space=pltpu.HBM)] * 2,
        "theta_edges",
        [pltpu.SemaphoreType.DMA((4,))],
        pl.BlockSpec(memory_space=pltpu.HBM),
        64 * 1024 * 1024 - 600 * 1024,
    )(corona, kappa)
    t_low = shifted(high, "lat", 1)
    t_high = shifted(low, "lat", -1)

    edge = (fields + 1, 2 * tile_t, radial)
    low, high = call(
        functools.partial(phi_edges, tile_t, tile_p), [edge] * 2, [vspec()] * 2, "phi_edges"
    )(corona.reshape(fields, tile_t * tile_p, radial), kappa.reshape(tile_t * tile_p, radial))
    p_low = shifted(high, "lon", 1)
    p_high = shifted(low, "lon", -1)

    table = jax.ShapeDtypeStruct((tile_t * tile_p, count), BF16)
    rank, meta, hit, table_high, table_low, w_r = call(
        functools.partial(plan, face_t, tile_t, tile_p),
        [(1, count), (n_dev, 128), jax.ShapeDtypeStruct((n_dev, count), BF16), table, table]
        + [(SH, count)],
        [vspec()] * 4,
        "plan",
    )(owner, dest_cell, base, fractions)

    own_low, own_high = call(
        corner_cells, [(2, fields + 1, radial)] * 2, [vspec()] * 2, "corner_cells"
    )(t_low, t_high)
    c_low = shifted(own_high, "lon", 1)
    c_high = shifted(own_low, "lon", -1)

    (almost,) = call(
        steps,
        [corona.shape],
        [sspec()] + [vspec()] * 6,
        "steps",
        [
            VMEM((fields + 1, tile_t + 4, tile_p + 16, radial), F32),
            VMEM((fields, tile_t + 2, tile_p + 16, radial), F32),
            VMEM((2, fields + 1, tile_t + 16, radial), F32),
        ],
    )(mixing, corona, kappa, t_low, t_high, p_low, p_high)

    patch, message = call(
        functools.partial(route, n_dev),
        [(4, fields, radial), (2 * n_dev, 128)],
        [vspec()] * 14,
        "route",
        [VMEM((tile_t * tile_p, radial), F32)],
    )(
        kappa, p_low, p_high, own_low, own_high, c_low, c_high, almost, rank, meta, hit, table_high,
        table_low, w_r,
    )
    (stepped,) = call(finish, [corona.shape], [vspec()] * 2, "finish")(almost, patch)

    got = lax.all_to_all(message, ("lat", "lon"), split_axis=0, concat_axis=0, tiled=True)

    coupled, p_first, p_last, t_first, t_last = call(
        functools.partial(land, n_dev),
        [helio_prev.shape, (fields, face_t), (fields, face_t)] + [(1, fields * face_p)] * 2,
        [vspec()] * 2,
        "land",
    )(got, helio_prev)
    from_t_low = shifted(t_last, "lat", 1)
    from_t_high = shifted(t_first, "lat", -1)
    from_p_low = shifted(p_last, "lon", 1)
    from_p_high = shifted(p_first, "lon", -1)
    (face,) = call(smooth, [helio_prev.shape], [vspec()] * 5, "smooth")(
        coupled, from_p_low, from_p_high, from_t_low, from_t_high
    )
    return (stepped, face)


def solution(mesh):
    return jax.shard_map(
        body,
        mesh=mesh,
        in_specs=(
            P(None, "lat", "lon", None),
            P("lat", "lon", None),
            P(),
            P(None, "lon", "lat"),
            P(("lat", "lon"), None),
            P(("lat", "lon")),
            P(("lat", "lon")),
            P(None, ("lat", "lon")),
        ),
        out_specs=(P(None, "lat", "lon", None), P(None, "lon", "lat")),
        check_vma=False,
    )
```

```python
import functools

import jax
import jax.numpy as jnp
from jax import lax
from jax.experimental import pallas as pl
from jax.experimental.pallas import tpu as pltpu
from jax.sharding import PartitionSpec as P

SH = 8
CAP = 16
BLOCK = 256
VMEM = pltpu.VMEM
F32 = jnp.float32
BF16 = jnp.bfloat16


def vspec():
    return pl.BlockSpec(memory_space=VMEM)


def sspec():
    return pl.BlockSpec(memory_space=pltpu.SMEM)


def iota(shape, dim):
    return lax.broadcasted_iota(jnp.int32, shape, dim)


def halves(x):
    high = x.astype(BF16)
    return high, (x - high.astype(F32)).astype(BF16)


def shifted(x, axis, step):
    count = lax.axis_size(axis)
    return lax.ppermute(x, axis, [(i, (i + step) % count) for i in range(count)])


def theta_edges(corona, kappa, low, high, sems):
    fields, tile_t = corona.shape[0], corona.shape[1]
    copies = []
    for side, (out, start) in enumerate(((low, 0), (high, tile_t - 2))):
        rows = pl.ds(start, 2)
        copies.append(
            pltpu.make_async_copy(corona.at[:, rows], out.at[pl.ds(0, fields)], sems.at[2 * side])
        )
        copies.append(pltpu.make_async_copy(kappa.at[rows], out.at[fields], sems.at[2 * side + 1]))
    for copy in copies:
        copy.start()
    for copy in copies:
        copy.wait()


def phi_edges(tile_t, tile_p, corona, kappa, low, high):
    fields = corona.shape[0]
    for f in range(fields + 1):
        for out, near, far in ((low, 0, 1), (high, tile_p - 1, tile_p - 2)):
            for at, col in ((0, near), (tile_t, far)):
                rows = pl.ds(col, tile_t, stride=tile_p)
                out[f, at : at + tile_t, :] = corona[f, rows, :] if f < fields else kappa[rows, :]


def corner_cells(t_low, t_high, low, high):
    count, _, tile_p, _ = t_low.shape
    for f in range(count):
        for out, col in ((low, 0), (high, tile_p - 1)):
            out[0, f : f + 1, :] = t_low[f, 1, col : col + 1, :]
            out[1, f : f + 1, :] = t_high[f, 0, col : col + 1, :]


def exists():
    found = []
    for axis in ("lat", "lon"):
        at, count = lax.axis_index(axis), lax.axis_size(axis)
        found.append([jnp.where(at > 0, 1.0, 0.0), jnp.where(at < count - 1, 1.0, 0.0)])
    return found


def plan(
    face_t, tile_t, tile_p, owner, dest, base, frac, rank_out, meta_out, hit_out, high_out, low_out,
    radial_out,
):
    n_dev = meta_out.shape[0]
    count = owner.shape[1]
    width = min(BLOCK, count)
    before = (iota((width, width), 0) < iota((width, width), 1)).astype(F32).astype(BF16)
    owners = iota((n_dev, width), 0)
    slots = iota((CAP, width), 0).astype(F32)
    carry = jnp.zeros((n_dev, 1), F32)
    meta = jnp.zeros((n_dev, 128), F32)
    for b in range(count // width):
        cols = slice(b * width, (b + 1) * width)
        hit = owners == owner[:, cols]
        hit_f = jnp.where(hit, 1.0, 0.0)
        hit_b = hit_f.astype(BF16)
        hit_out[:, cols] = hit_b
        ahead = jnp.dot(hit_b, before, preferred_element_type=F32) + carry
        rank = jnp.sum(jnp.where(hit, ahead, 0.0), axis=0, keepdims=True)
        carry = ahead[:, width - 1 : width] + hit_f[:, width - 1 : width]
        rank_out[:, cols] = rank
        cell = dest[:, cols]
        cell_t = (cell % face_t).astype(F32)
        cell_p = (cell // face_t).astype(F32)
        mine = slots == rank
        rows = jnp.concatenate(
            [
                jnp.where(mine, cell_t, 0.0),
                jnp.where(mine, cell_p, 0.0),
                jnp.zeros((128 - 2 * CAP, width), F32),
            ],
            axis=0,
        ).astype(BF16)
        meta = meta + lax.dot_general(
            hit_b, rows, (((1,), (1,)), ((), ())), preferred_element_type=F32
        )
        corner = base[:, cols]

        def pair(size, at, fraction):
            rows = iota((size, width), 0)
            return jnp.where(rows == at, 1.0 - fraction, jnp.where(rows == at + 1, fraction, 0.0))

        w_t = pair(tile_t, corner // (tile_p * SH), frac[0:1, cols])
        w_p = pair(tile_p, (corner // SH) % tile_p, frac[1:2, cols])
        radial_out[:, cols] = pair(SH, corner % SH, frac[2:3, cols])
        table = (w_t[:, None, :] * w_p[None, :, :]).reshape(tile_t * tile_p, width)
        high_out[:, cols], low_out[:, cols] = halves(table)
    meta_out[...] = meta


def spread(mixing, spread_out):
    fields = mixing.shape[0]
    for g in range(fields):
        for f in range(fields):
            spread_out[g * fields + f] = jnp.full(spread_out.shape[1:], 0.3 * mixing[g, f], F32)


def flux(mix, conds, centres, near):
    kc, *kn = conds
    radial = kc.shape[-1]
    fields = len(centres)
    lane = iota(kc.shape, 1)
    weights = [0.075 * (kc + k) for k in kn]
    up = 0.075 * (kc + jnp.where(lane == radial - 1, 0.0, pltpu.roll(kc, radial - 1, 1)))
    down = 0.075 * (kc + jnp.where(lane == 0, 0.0, pltpu.roll(kc, 1, 1)))
    total = 1.0 - ((weights[0] + weights[1]) + (weights[2] + weights[3]) + (up + down))
    up = jnp.where(lane == radial - 1, 0.0, up)
    down = jnp.where(lane == 0, 0.0, down)
    for g in range(fields):
        c = centres[g]
        acc = total * c
        for w, beside in zip(weights, near(g)):
            acc = acc + w * beside
        acc = acc + up * pltpu.roll(c, radial - 1, 1) + down * pltpu.roll(c, 1, 1)
        for f in range(fields):
            m = mix[g * fields + f]
            acc = acc + jnp.concatenate([m] * (c.shape[0] // 8), axis=0) * centres[f]
        yield g, acc


WIDE = 32


def along_phi(ref, f, t, tile_p, dt=0, dp=0):
    at = (t + dt) * WIDE + 8 + dp
    if isinstance(t, jax.Array) and dp == 0:
        at = pl.multiple_of(at, 8)
    return ref[f, pl.ds(at, tile_p), :]


def along_theta(ref, f, t, p, count):
    return ref[f, pl.ds(t * WIDE + 8 + p, count, stride=WIDE), :]


AROUND = ((-1, 0), (1, 0), (0, -1), (0, 1))


def row_flux(mix, field, cond, t_field, t_cond, tile_p, fields):
    last = cond.shape[0] - 1
    return flux(
        mix,
        [along_phi(cond, last, t_cond, tile_p)]
        + [along_phi(cond, last, t_cond, tile_p, *d) for d in AROUND],
        [along_phi(field, f, t_field, tile_p) for f in range(fields)],
        lambda g: [along_phi(field, g, t_field, tile_p, *d) for d in AROUND],
    )


def column_flux(mix, field, cond, t_field, t_cond, p, count, fields):
    last = cond.shape[0] - 1
    return flux(
        mix,
        [along_theta(cond, last, t_cond, p, count)]
        + [along_theta(cond, last, t_cond + dt, p + dp, count) for dt, dp in AROUND],
        [along_theta(field, f, t_field, p, count) for f in range(fields)],
        lambda g: [along_theta(field, g, t_field + dt, p + dp, count) for dt, dp in AROUND],
    )


def inside(mixing, corona, kappa, once_out, twice_out, wide, once, mix):
    fields, tile_t, tile_p, radial = corona.shape
    spread(mixing, mix)
    zeros = jnp.zeros((8, radial), F32)
    plane = jnp.zeros((WIDE, radial), F32)
    for f in range(fields + 1):
        for t in range(tile_t + 2):
            if t in (0, tile_t + 1):
                wide[f, pl.ds(t * WIDE, WIDE), :] = plane
                if f < fields:
                    once[f, pl.ds(t * WIDE, WIDE), :] = plane
                continue
            for ref in (wide, once) if f < fields else (wide,):
                ref[f, pl.ds(t * WIDE, 8), :] = zeros
                ref[f, pl.ds(t * WIDE + 8 + tile_p, 8), :] = zeros
            own = corona[f, t - 1] if f < fields else kappa[t - 1]
            wide[f, pl.ds(t * WIDE + 8, tile_p), :] = own

    def first(t, _):
        for g, acc in row_flux(mix, wide, wide, t, t, tile_p, fields):
            once[g, pl.ds(pl.multiple_of(t * WIDE + 8, 8), tile_p), :] = acc
            once_out[g, t - 1] = acc
        return 0

    lax.fori_loop(1, tile_t + 1, first, 0)

    def second(t, _):
        for g, acc in row_flux(mix, once, wide, t, t, tile_p, fields):
            twice_out[g, t - 1] = acc
        return 0

    lax.fori_loop(2, tile_t, second, 0)


def around(
    mixing, corona, kappa, t_low, t_high, p_low, p_high, once_in, twice_in, stepped, wide, once, mix,
):
    fields, tile_t, tile_p, radial = corona.shape
    has_t, has_p = exists()
    spread(mixing, mix)
    nothing = jnp.zeros((1, radial), F32)
    for f in range(fields + 1):
        for t in range(tile_t):
            own = corona[f, t] if f < fields else kappa[t]
            wide[f, pl.ds((t + 2) * WIDE + 8, tile_p), :] = own
        for k in range(2):
            wide[f, pl.ds(k * WIDE + 8, tile_p), :] = t_low[f, k] * has_t[0]
            wide[f, pl.ds((tile_t + 2 + k) * WIDE + 8, tile_p), :] = t_high[f, k] * has_t[1]
        for side, (halo, near, far) in enumerate(((p_low, 7, 6), (p_high, 8 + tile_p, 9 + tile_p))):
            for k, col in enumerate((near, far)):
                cells = halo[f, k * tile_t : (k + 1) * tile_t, :] * has_p[side]
                wide[f, pl.ds(2 * WIDE + col, tile_t, stride=WIDE), :] = cells
            for t in (1, tile_t + 2):
                wide[f, pl.ds(t * WIDE + near, 1), :] = nothing
        if f < fields:
            for t in range(tile_t):
                once[f, pl.ds((t + 1) * WIDE + 8, tile_p), :] = once_in[f, t]

    for t in (-1, 0, tile_t - 1, tile_t):
        for g, acc in row_flux(mix, wide, wide, t + 2, t + 2, tile_p, fields):
            if t in (-1, tile_t):
                acc = acc * has_t[0 if t < 0 else 1]
            once[g, pl.ds((t + 1) * WIDE + 8, tile_p), :] = acc
    for p in (-1, 0, tile_p - 1, tile_p):
        for g, acc in column_flux(mix, wide, wide, 2, 2, p, tile_t, fields):
            if p in (-1, tile_p):
                acc = acc * has_p[0 if p < 0 else 1]
            once[g, pl.ds(WIDE + 8 + p, tile_t, stride=WIDE), :] = acc

    for f in range(fields):
        stepped[f] = twice_in[f]
    for t in (0, 1, tile_t - 2, tile_t - 1):
        for g, acc in row_flux(mix, once, wide, t + 1, t + 2, tile_p, fields):
            stepped[g, t * tile_p : (t + 1) * tile_p, :] = acc
    for p in (0, 1, tile_p - 2, tile_p - 1):
        for g, acc in column_flux(mix, once, wide, 1, 2, p, tile_t, fields):
            stepped[g, pl.ds(p, tile_t, stride=tile_p), :] = acc


def route(
    n_dev, kappa, p_low, p_high, own_low, own_high, c_low, c_high, stepped, rank, meta, hit,
    table_high, table_low, w_r, patch, message, shell,
):
    fields, columns, radial = stepped.shape
    tile_t, tile_p, _ = kappa.shape
    has_t, has_p = exists()
    lane = iota((columns, radial), 1)
    rows = jnp.zeros((columns, radial), F32)
    for f in range(fields):
        moved = pltpu.roll(stepped[f], (f * SH + SH) % radial, 1)
        rows = jnp.where(lane // SH == f, moved, rows)
    shell[...] = rows
    for a in range(2):
        for b, (halo, own, diagonal) in enumerate(
            ((p_low, own_low, c_low), (p_high, own_high, c_high))
        ):
            t, p = a * (tile_t - 1), b * (tile_p - 1)
            k_t, u_t = own[a, fields : fields + 1] * has_t[a], own[a, 0:fields] * has_t[a]
            k_p = halo[fields, t : t + 1, :] * has_p[b]
            u_p = jnp.concatenate([halo[f, t : t + 1, :] for f in range(fields)], axis=0) * has_p[b]
            both = has_t[a] * has_p[b]
            k_d, u_d = diagonal[a, fields : fields + 1] * both, diagonal[a, 0:fields] * both
            k = kappa[t, p : p + 1, :]
            by_t = 0.075 * ((k_t + k_d) * u_d - k_d * u_t)
            by_p = 0.075 * ((k_p + k_d) * u_d - k_d * u_p)
            extra = 0.075 * ((k + k_t) * by_t + (k + k_p) * by_p)
            patch[2 * a + b] = extra
            row = jnp.zeros((1, radial), F32)
            for f in range(fields):
                moved = pltpu.roll(extra[f : f + 1], (f * SH + SH) % radial, 1)
                row = jnp.where(lane[0:1] // SH == f, moved, row)
            at = t * tile_p + p
            shell[at : at + 1, :] = shell[at : at + 1, :] + row
    rows = shell[...]
    high = rows.astype(BF16).astype(F32)
    both = high + pltpu.roll(rows - high, fields * SH, 1)
    left = jnp.transpose(both).astype(BF16)

    count = rank.shape[1]
    width = min(BLOCK, count)
    packed = jnp.zeros((n_dev, 2 * fields * CAP), F32)
    for b in range(count // width):
        cols = slice(b * width, (b + 1) * width)
        coarse = jnp.dot(left, table_high[:, cols], preferred_element_type=F32)
        fine = jnp.dot(left[: fields * SH], table_low[:, cols], preferred_element_type=F32)
        by_layer = coarse[: fields * SH] + (coarse[fields * SH :] + fine)
        value = jnp.sum(by_layer.reshape(fields, SH, width) * w_r[:, cols][None], axis=1)
        order = rank[:, cols]
        placed = jnp.concatenate(
            [jnp.where(order == float(k), value, 0.0) for k in range(CAP)], axis=0
        )
        placed_high, placed_low = halves(placed)
        packed = packed + lax.dot_general(
            hit[:, cols],
            jnp.concatenate([placed_high, placed_low], axis=0),
            (((1,), (1,)), ((), ())),
            preferred_element_type=F32,
        )
    half = fields * CAP
    message[pl.ds(0, n_dev, stride=2), :] = packed[:, :half] + packed[:, half:]
    message[pl.ds(1, n_dev, stride=2), :] = meta[...]


def finish(tile_t, tile_p, stepped, patch, out):
    out[...] = stepped[...]
    for a in range(2):
        for b in range(2):
            at = a * (tile_t - 1) * tile_p + b * (tile_p - 1)
            for f in range(stepped.shape[0]):
                out[f, at : at + 1, :] = (
                    stepped[f, at : at + 1, :] + patch[2 * a + b, f : f + 1, :]
                )


def land(n_dev, got, prev, coupled, p_first, p_last, t_first, t_last):
    fields, face_p, face_t = prev.shape
    values = jnp.transpose(got[pl.ds(0, n_dev, stride=2), :])
    cells = jnp.transpose(got[pl.ds(1, n_dev, stride=2), :])
    along_t = iota((face_t, n_dev), 0).astype(F32)
    along_p = iota((face_p, n_dev), 0).astype(F32)
    rows = fields * face_p
    total = jnp.zeros((2 * rows, face_t), F32)
    for k in range(CAP):
        at_t = jnp.where(along_t == cells[k : k + 1, :], 1.0, 0.0).astype(BF16)
        at_p = along_p == cells[CAP + k : CAP + k + 1, :]
        value = values[k * fields : (k + 1) * fields, :]
        high = value.astype(BF16).astype(F32)
        parts = [
            jnp.where(at_p[None], part[:, None, :], 0.0).reshape(rows, n_dev).astype(BF16)
            for part in (high, value - high)
        ]
        total = total + lax.dot_general(
            jnp.concatenate(parts, axis=0),
            at_t,
            (((1,), (1,)), ((), ())),
            preferred_element_type=F32,
        )
    new = prev[...].reshape(rows, face_t) + (total[:rows] + total[rows:])
    coupled[...] = new.reshape(fields, face_p, face_t)
    turned = jnp.transpose(new)
    t_first[...] = turned[0:1, :]
    t_last[...] = turned[face_t - 1 : face_t, :]
    for f in range(fields):
        p_first[f : f + 1, :] = new[f * face_p : f * face_p + 1, :]
        p_last[f : f + 1, :] = new[(f + 1) * face_p - 1 : (f + 1) * face_p, :]


def smooth(coupled, p_low, p_high, t_low, t_high, out):
    fields, face_p, face_t = coupled.shape
    x = coupled[...]
    row = iota((face_p, face_t), 0)[None]
    lane = iota((face_p, face_t), 1)[None]

    has_t, has_p = exists()

    def rim(ref, has):
        return ref[...] * has

    def column(edge):
        return jnp.transpose(jnp.broadcast_to(edge, (face_t, fields * face_p))).reshape(x.shape)

    below = jnp.where(row == 0, rim(p_low, has_p[0])[:, None, :], pltpu.roll(x, 1, 1))
    above = jnp.where(
        row == face_p - 1, rim(p_high, has_p[1])[:, None, :], pltpu.roll(x, face_p - 1, 1)
    )
    left = jnp.where(lane == 0, column(rim(t_low, has_t[0])), pltpu.roll(x, 1, 2))
    right = jnp.where(
        lane == face_t - 1, column(rim(t_high, has_t[1])), pltpu.roll(x, face_t - 1, 2)
    )
    out[...] = x + 0.2 * (above + below + right + left - 4.0 * x)


def call(kernel, outs, specs, name, scratch=(), room=40 * 1024 * 1024):
    outs = [s if isinstance(s, jax.ShapeDtypeStruct) else jax.ShapeDtypeStruct(s, F32) for s in outs]
    return pl.pallas_call(
        kernel,
        out_shape=outs,
        in_specs=specs,
        out_specs=[vspec()] * len(outs),
        scratch_shapes=list(scratch),
        name=name,
        compiler_params=pltpu.CompilerParams(vmem_limit_bytes=room),
    )


def body(corona, kappa, mixing, helio_prev, owner, dest_cell, corner_base, fractions):
    fields, tile_t, tile_p, radial = corona.shape
    n_lat, n_lon = lax.axis_size("lat"), lax.axis_size("lon")
    n_dev = n_lat * n_lon
    count = corner_base.shape[0]
    _, face_p, face_t = helio_prev.shape
    owner = owner.reshape(1, count)
    dest_cell = dest_cell.reshape(1, count)
    base = corner_base.reshape(1, count)
    edge = (fields + 1, 2, tile_p, radial)
    low, high = call(
        theta_edges,
        [edge] * 2,
        [pl.BlockSpec(memory_space=pltpu.HBM)] * 2,
        "theta_edges",
        [pltpu.SemaphoreType.DMA((4,))],
        room=58 * 1024 * 1024,
    )(corona, kappa)
    t_low = shifted(high, "lat", 1)
    t_high = shifted(low, "lat", -1)

    edge = (fields + 1, 2 * tile_t, radial)
    low, high = call(
        functools.partial(phi_edges, tile_t, tile_p), [edge] * 2, [vspec()] * 2, "phi_edges"
    )(corona.reshape(fields, tile_t * tile_p, radial), kappa.reshape(tile_t * tile_p, radial))
    p_low = shifted(high, "lon", 1)
    p_high = shifted(low, "lon", -1)

    table = jax.ShapeDtypeStruct((tile_t * tile_p, count), BF16)
    rank, meta, hit, table_high, table_low, w_r = call(
        functools.partial(plan, face_t, tile_t, tile_p),
        [(1, count), (n_dev, 128), jax.ShapeDtypeStruct((n_dev, count), BF16), table, table]
        + [(SH, count)],
        [vspec()] * 4,
        "plan",
    )(owner, dest_cell, base, fractions)

    t_low, t_high, rank = lax.optimization_barrier((t_low, t_high, rank))
    once, twice = call(
        inside,
        [corona.shape] * 2,
        [sspec()] + [vspec()] * 2,
        "inside",
        [
            VMEM((fields + 1, (tile_t + 2) * WIDE, radial), F32),
            VMEM((fields, (tile_t + 2) * WIDE, radial), F32),
            VMEM((fields * fields, 8, radial), F32),
        ],
    )(mixing, corona, kappa)

    own_low, own_high = call(
        corner_cells, [(2, fields + 1, radial)] * 2, [vspec()] * 2, "corner_cells"
    )(t_low, t_high)
    c_low = shifted(own_high, "lon", 1)
    c_high = shifted(own_low, "lon", -1)

    flat = (fields, tile_t * tile_p, radial)
    padded = [
        VMEM((fields + 1, (tile_t + 4) * WIDE, radial), F32),
        VMEM((fields, (tile_t + 2) * WIDE, radial), F32),
        VMEM((fields * fields, 8, radial), F32),
    ]
    (almost,) = call(around, [flat], [sspec()] + [vspec()] * 8, "around", padded)(
        mixing, corona, kappa, t_low, t_high, p_low, p_high, once, twice.reshape(flat)
    )

    patch, message = call(
        functools.partial(route, n_dev),
        [(4, fields, radial), (2 * n_dev, 128)],
        [vspec()] * 14,
        "route",
        [VMEM((tile_t * tile_p, radial), F32)],
    )(
        kappa, p_low, p_high, own_low, own_high, c_low, c_high, almost, rank, meta, hit, table_high,
        table_low, w_r,
    )
    (stepped,) = call(
        functools.partial(finish, tile_t, tile_p), [flat], [vspec()] * 2, "finish"
    )(almost, patch)

    got = lax.all_to_all(message, ("lat", "lon"), split_axis=0, concat_axis=0, tiled=True)

    coupled, p_first, p_last, t_first, t_last = call(
        functools.partial(land, n_dev),
        [helio_prev.shape, (fields, face_t), (fields, face_t)] + [(1, fields * face_p)] * 2,
        [vspec()] * 2,
        "land",
    )(got, helio_prev)
    from_t_low = shifted(t_last, "lat", 1)
    from_t_high = shifted(t_first, "lat", -1)
    from_p_low = shifted(p_last, "lon", 1)
    from_p_high = shifted(p_first, "lon", -1)
    (face,) = call(smooth, [helio_prev.shape], [vspec()] * 5, "smooth")(
        coupled, from_p_low, from_p_high, from_t_low, from_t_high
    )
    return (stepped.reshape(corona.shape), face)


def solution(mesh):
    return jax.shard_map(
        body,
        mesh=mesh,
        in_specs=(
            P(None, "lat", "lon", None),
            P("lat", "lon", None),
            P(),
            P(None, "lon", "lat"),
            P(("lat", "lon"), None),
            P(("lat", "lon")),
            P(("lat", "lon")),
            P(None, ("lat", "lon")),
        ),
        out_specs=(P(None, "lat", "lon", None), P(None, "lon", "lat")),
        check_vma=False,
    )
```

```python
import functools

import jax
import jax.numpy as jnp
from jax import lax
from jax.experimental import pallas as pl
from jax.experimental.pallas import tpu as pltpu
from jax.sharding import PartitionSpec as P

SH = 8
CAP = 16
BLOCK = 256
VMEM = pltpu.VMEM
F32 = jnp.float32
BF16 = jnp.bfloat16


def vspec():
    return pl.BlockSpec(memory_space=VMEM)


def sspec():
    return pl.BlockSpec(memory_space=pltpu.SMEM)


def iota(shape, dim):
    return lax.broadcasted_iota(jnp.int32, shape, dim)


def halves(x):
    high = x.astype(BF16)
    return high, (x - high.astype(F32)).astype(BF16)


def shifted(x, axis, step):
    count = lax.axis_size(axis)
    return lax.ppermute(x, axis, [(i, (i + step) % count) for i in range(count)])


def theta_edges(corona, kappa, low, high, sems):
    fields, tile_t = corona.shape[0], corona.shape[1]
    copies = []
    for side, (out, start) in enumerate(((low, 0), (high, tile_t - 2))):
        rows = pl.ds(start, 2)
        copies.append(
            pltpu.make_async_copy(corona.at[:, rows], out.at[pl.ds(0, fields)], sems.at[2 * side])
        )
        copies.append(pltpu.make_async_copy(kappa.at[rows], out.at[fields], sems.at[2 * side + 1]))
    for copy in copies:
        copy.start()
    for copy in copies:
        copy.wait()


def phi_edges(tile_t, tile_p, corona, kappa, low, high):
    fields = corona.shape[0]
    for f in range(fields + 1):
        for out, near, far in ((low, 0, 1), (high, tile_p - 1, tile_p - 2)):
            for at, col in ((0, near), (tile_t, far)):
                rows = pl.ds(col, tile_t, stride=tile_p)
                out[f, at : at + tile_t, :] = corona[f, rows, :] if f < fields else kappa[rows, :]


def corner_cells(t_low, t_high, low, high):
    count, _, tile_p, _ = t_low.shape
    for f in range(count):
        for out, col in ((low, 0), (high, tile_p - 1)):
            out[0, f : f + 1, :] = t_low[f, 1, col : col + 1, :]
            out[1, f : f + 1, :] = t_high[f, 0, col : col + 1, :]


def exists():
    found = []
    for axis in ("lat", "lon"):
        at, count = lax.axis_index(axis), lax.axis_size(axis)
        found.append([jnp.where(at > 0, 1.0, 0.0), jnp.where(at < count - 1, 1.0, 0.0)])
    return found


def plan(
    face_t, tile_t, tile_p, owner, dest, base, frac, rank_out, meta_out, hit_out, high_out, low_out,
    radial_out,
):
    n_dev = meta_out.shape[0]
    count = owner.shape[1]
    width = min(BLOCK, count)
    before = (iota((width, width), 0) < iota((width, width), 1)).astype(F32).astype(BF16)
    owners = iota((n_dev, width), 0)
    slots = iota((CAP, width), 0).astype(F32)
    carry = jnp.zeros((n_dev, 1), F32)
    meta = jnp.zeros((n_dev, 128), F32)
    for b in range(count // width):
        cols = slice(b * width, (b + 1) * width)
        hit = owners == owner[:, cols]
        hit_f = jnp.where(hit, 1.0, 0.0)
        hit_b = hit_f.astype(BF16)
        hit_out[:, cols] = hit_b
        ahead = jnp.dot(hit_b, before, preferred_element_type=F32) + carry
        rank = jnp.sum(jnp.where(hit, ahead, 0.0), axis=0, keepdims=True)
        carry = ahead[:, width - 1 : width] + hit_f[:, width - 1 : width]
        rank_out[:, cols] = rank
        cell = dest[:, cols]
        cell_t = (cell % face_t).astype(F32)
        cell_p = (cell // face_t).astype(F32)
        mine = slots == rank
        rows = jnp.concatenate(
            [
                jnp.where(mine, cell_t, 0.0),
                jnp.where(mine, cell_p, 0.0),
                jnp.zeros((128 - 2 * CAP, width), F32),
            ],
            axis=0,
        ).astype(BF16)
        meta = meta + lax.dot_general(
            hit_b, rows, (((1,), (1,)), ((), ())), preferred_element_type=F32
        )
        corner = base[:, cols]

        def pair(size, at, fraction):
            rows = iota((size, width), 0)
            return jnp.where(rows == at, 1.0 - fraction, jnp.where(rows == at + 1, fraction, 0.0))

        w_t = pair(tile_t, corner // (tile_p * SH), frac[0:1, cols])
        w_p = pair(tile_p, (corner // SH) % tile_p, frac[1:2, cols])
        radial_out[:, cols] = pair(SH, corner % SH, frac[2:3, cols])
        table = (w_t[:, None, :] * w_p[None, :, :]).reshape(tile_t * tile_p, width)
        high_out[:, cols], low_out[:, cols] = halves(table)
    meta_out[...] = meta


def steps(
    tile_t, tile_p, mixing, corona, kappa, t_low, t_high, p_low, p_high, stepped, wide, once, plane,
    coef,
):
    fields = mixing.shape[0]
    radial = corona.shape[1]
    cells = tile_t * tile_p
    pitch, inner = tile_p + 4, tile_p + 2
    has_t, has_p = exists()

    def at(t, p):
        return (t + 2) * pitch + p + 2

    def inside(t, p):
        return (t + 1) * inner + p + 1

    nothing = jnp.zeros((fields, radial), F32)
    rows = 2 * tile_p
    for k in range(2):
        for ref, mask, t in ((t_low, has_t[0], k - 2), (t_high, has_t[1], tile_t + k)):
            for p in range(tile_p):
                wide[at(t, p)] = ref[pl.ds(k * tile_p + p, fields, stride=rows), :] * mask
            plane[t + 2, 8 : 8 + tile_p, :] = (
                ref[fields * rows + k * tile_p : fields * rows + (k + 1) * tile_p, :] * mask
            )
    rows = 2 * tile_t
    for k in range(2):
        for ref, mask, p in ((p_low, has_p[0], -1 - k), (p_high, has_p[1], tile_p + k)):
            for t in range(tile_t):
                wide[at(t, p)] = ref[pl.ds(k * tile_t + t, fields, stride=rows), :] * mask
                row = fields * rows + k * tile_t + t
                plane[t + 2, 8 + p : 9 + p, :] = ref[row : row + 1, :] * mask
    for t in (-1, tile_t):
        for p in (-1, tile_p):
            wide[at(t, p)] = nothing
            plane[t + 2, 8 + p : 9 + p, :] = nothing[0:1]

    def own(t, _):
        for p in range(tile_p):
            wide[(t + 2) * pitch + p + 2] = corona[pl.ds(t * tile_p + p, fields, stride=cells), :]
        plane[t + 2, 8 : 8 + tile_p, :] = kappa[t]
        return 0

    lax.fori_loop(0, tile_t, own, 0)

    span = coef.shape[2]
    lane = iota((span, radial), 1)

    def weigh(t, _):
        def kap(dt, dp):
            return plane[t + 1 + dt, 7 + dp : 7 + dp + span, :]

        k = kap(0, 0)
        around = [0.075 * (k + kap(*d)) for d in ((-1, 0), (1, 0), (0, -1), (0, 1))]
        above = jnp.where(lane == radial - 1, 0.0, pltpu.roll(k, radial - 1, 1))
        below = jnp.where(lane == 0, 0.0, pltpu.roll(k, 1, 1))
        above, below = 0.075 * (k + above), 0.075 * (k + below)
        for n, w in enumerate(around):
            coef[t, n] = w
        coef[t, 4] = jnp.where(lane == radial - 1, 0.0, above)
        coef[t, 5] = jnp.where(lane == 0, 0.0, below)
        coef[t, 6] = 1.0 - (
            (around[0] + around[1]) + (around[2] + around[3]) + (above + below)
        )
        return 0

    lax.fori_loop(0, tile_t + 2, weigh, 0)

    row = iota((fields, radial), 0)
    turned = []
    for k in range(fields):
        m = jnp.zeros((fields, radial), F32)
        for g in range(fields):
            m = jnp.where(row == g, 0.3 * mixing[g, (g - k) % fields], m)
        turned.append(m)

    def flux(ref, width, index, t, p):
        def w(n):
            return coef[t + 1, n, pl.ds(p + 1, fields, stride=0), :]

        c = ref[index]
        acc = (w(6) + turned[0]) * c
        acc = acc + (w(0) * ref[index - width] + w(1) * ref[index + width])
        acc = acc + (w(2) * ref[index - 1] + w(3) * ref[index + 1])
        acc = acc + (w(4) * pltpu.roll(c, radial - 1, 1) + w(5) * pltpu.roll(c, 1, 1))
        mixed = [turned[k] * pltpu.roll(c, k, 0) for k in range(1, fields)]
        while len(mixed) > 1:
            mixed = [a + b for a, b in zip(mixed[::2], mixed[1::2])] + mixed[len(mixed) & ~1 :]
        return acc + mixed[0]

    def first(t, _):
        for p in range(-1, tile_p + 1):
            once[(t + 1) * inner + p + 1] = flux(wide, pitch, (t + 2) * pitch + p + 2, t, p)
        return 0

    def rim(t, p):
        once[inside(t, p)] = flux(wide, pitch, at(t, p), t, p)

    lax.fori_loop(0, tile_t, first, 0)
    for p in range(tile_p):
        rim(-1, p)
        rim(tile_t, p)

    for mask, edge in (
        (has_t[0], [(-1, p) for p in range(tile_p)]),
        (has_t[1], [(tile_t, p) for p in range(tile_p)]),
        (has_p[0], [(t, -1) for t in range(tile_t)]),
        (has_p[1], [(t, tile_p) for t in range(tile_t)]),
    ):

        @pl.when(mask == 0.0)
        def _(edge=edge):
            for cell in edge:
                once[inside(*cell)] = nothing

    def second(t, _):
        for p in range(tile_p):
            stepped[pl.ds(t * tile_p + p, fields, stride=cells), :] = flux(
                once, inner, (t + 1) * inner + p + 1, t, p
            )
        return 0

    lax.fori_loop(0, tile_t, second, 0)


def route(
    n_dev, kappa, p_low, p_high, own_low, own_high, c_low, c_high, stepped, rank, meta, hit,
    table_high, table_low, w_r, patch, message, shell,
):
    fields, columns, radial = stepped.shape
    tile_t, tile_p, _ = kappa.shape
    has_t, has_p = exists()
    lane = iota((columns, radial), 1)
    rows = jnp.zeros((columns, radial), F32)
    for f in range(fields):
        moved = pltpu.roll(stepped[f], (f * SH + SH) % radial, 1)
        rows = jnp.where(lane // SH == f, moved, rows)
    shell[...] = rows
    for a in range(2):
        for b, (halo, own, diagonal) in enumerate(
            ((p_low, own_low, c_low), (p_high, own_high, c_high))
        ):
            t, p = a * (tile_t - 1), b * (tile_p - 1)
            k_t, u_t = own[a, fields : fields + 1] * has_t[a], own[a, 0:fields] * has_t[a]
            k_p = halo[fields, t : t + 1, :] * has_p[b]
            u_p = jnp.concatenate([halo[f, t : t + 1, :] for f in range(fields)], axis=0) * has_p[b]
            both = has_t[a] * has_p[b]
            k_d, u_d = diagonal[a, fields : fields + 1] * both, diagonal[a, 0:fields] * both
            k = kappa[t, p : p + 1, :]
            by_t = 0.075 * ((k_t + k_d) * u_d - k_d * u_t)
            by_p = 0.075 * ((k_p + k_d) * u_d - k_d * u_p)
            extra = 0.075 * ((k + k_t) * by_t + (k + k_p) * by_p)
            patch[2 * a + b] = extra
            row = jnp.zeros((1, radial), F32)
            for f in range(fields):
                moved = pltpu.roll(extra[f : f + 1], (f * SH + SH) % radial, 1)
                row = jnp.where(lane[0:1] // SH == f, moved, row)
            at = t * tile_p + p
            shell[at : at + 1, :] = shell[at : at + 1, :] + row
    rows = shell[...]
    high = rows.astype(BF16).astype(F32)
    both = high + pltpu.roll(rows - high, fields * SH, 1)
    left = jnp.transpose(both).astype(BF16)

    count = rank.shape[1]
    width = min(BLOCK, count)
    packed = jnp.zeros((n_dev, 2 * fields * CAP), F32)
    for b in range(count // width):
        cols = slice(b * width, (b + 1) * width)
        coarse = jnp.dot(left, table_high[:, cols], preferred_element_type=F32)
        fine = jnp.dot(left[: fields * SH], table_low[:, cols], preferred_element_type=F32)
        by_layer = coarse[: fields * SH] + (coarse[fields * SH :] + fine)
        value = jnp.sum(by_layer.reshape(fields, SH, width) * w_r[:, cols][None], axis=1)
        order = rank[:, cols]
        placed = jnp.concatenate(
            [jnp.where(order == float(k), value, 0.0) for k in range(CAP)], axis=0
        )
        placed_high, placed_low = halves(placed)
        packed = packed + lax.dot_general(
            hit[:, cols],
            jnp.concatenate([placed_high, placed_low], axis=0),
            (((1,), (1,)), ((), ())),
            preferred_element_type=F32,
        )
    half = fields * CAP
    message[pl.ds(0, n_dev, stride=2), :] = packed[:, :half] + packed[:, half:]
    message[pl.ds(1, n_dev, stride=2), :] = meta[...]


def finish(tile_t, tile_p, stepped, patch, out):
    out[...] = stepped[...]
    for a in range(2):
        for b in range(2):
            at = a * (tile_t - 1) * tile_p + b * (tile_p - 1)
            for f in range(stepped.shape[0]):
                out[f, at : at + 1, :] = (
                    stepped[f, at : at + 1, :] + patch[2 * a + b, f : f + 1, :]
                )


def land(n_dev, got, prev, coupled, p_first, p_last, t_first, t_last):
    fields, face_p, face_t = prev.shape
    values = jnp.transpose(got[pl.ds(0, n_dev, stride=2), :])
    cells = jnp.transpose(got[pl.ds(1, n_dev, stride=2), :])
    along_t = iota((face_t, n_dev), 0).astype(F32)
    along_p = iota((face_p, n_dev), 0).astype(F32)
    rows = fields * face_p
    total = jnp.zeros((2 * rows, face_t), F32)
    for k in range(CAP):
        at_t = jnp.where(along_t == cells[k : k + 1, :], 1.0, 0.0).astype(BF16)
        at_p = along_p == cells[CAP + k : CAP + k + 1, :]
        value = values[k * fields : (k + 1) * fields, :]
        high = value.astype(BF16).astype(F32)
        parts = [
            jnp.where(at_p[None], part[:, None, :], 0.0).reshape(rows, n_dev).astype(BF16)
            for part in (high, value - high)
        ]
        total = total + lax.dot_general(
            jnp.concatenate(parts, axis=0),
            at_t,
            (((1,), (1,)), ((), ())),
            preferred_element_type=F32,
        )
    new = prev[...].reshape(rows, face_t) + (total[:rows] + total[rows:])
    coupled[...] = new.reshape(fields, face_p, face_t)
    turned = jnp.transpose(new)
    t_first[...] = turned[0:1, :]
    t_last[...] = turned[face_t - 1 : face_t, :]
    for f in range(fields):
        p_first[f : f + 1, :] = new[f * face_p : f * face_p + 1, :]
        p_last[f : f + 1, :] = new[(f + 1) * face_p - 1 : (f + 1) * face_p, :]


def smooth(coupled, p_low, p_high, t_low, t_high, out):
    fields, face_p, face_t = coupled.shape
    x = coupled[...]
    row = iota((face_p, face_t), 0)[None]
    lane = iota((face_p, face_t), 1)[None]

    has_t, has_p = exists()

    def rim(ref, has):
        return ref[...] * has

    def column(edge):
        return jnp.transpose(jnp.broadcast_to(edge, (face_t, fields * face_p))).reshape(x.shape)

    below = jnp.where(row == 0, rim(p_low, has_p[0])[:, None, :], pltpu.roll(x, 1, 1))
    above = jnp.where(
        row == face_p - 1, rim(p_high, has_p[1])[:, None, :], pltpu.roll(x, face_p - 1, 1)
    )
    left = jnp.where(lane == 0, column(rim(t_low, has_t[0])), pltpu.roll(x, 1, 2))
    right = jnp.where(
        lane == face_t - 1, column(rim(t_high, has_t[1])), pltpu.roll(x, face_t - 1, 2)
    )
    out[...] = x + 0.2 * (above + below + right + left - 4.0 * x)


def call(kernel, outs, specs, name, scratch=(), room=40 * 1024 * 1024):
    outs = [s if isinstance(s, jax.ShapeDtypeStruct) else jax.ShapeDtypeStruct(s, F32) for s in outs]
    return pl.pallas_call(
        kernel,
        out_shape=outs,
        in_specs=specs,
        out_specs=[vspec()] * len(outs),
        scratch_shapes=list(scratch),
        name=name,
        compiler_params=pltpu.CompilerParams(vmem_limit_bytes=room),
    )


def body(corona, kappa, mixing, helio_prev, owner, dest_cell, corner_base, fractions):
    fields, tile_t, tile_p, radial = corona.shape
    n_lat, n_lon = lax.axis_size("lat"), lax.axis_size("lon")
    n_dev = n_lat * n_lon
    count = corner_base.shape[0]
    _, face_p, face_t = helio_prev.shape
    owner = owner.reshape(1, count)
    dest_cell = dest_cell.reshape(1, count)
    base = corner_base.reshape(1, count)
    edge = (fields + 1, 2, tile_p, radial)
    low, high = call(
        theta_edges,
        [edge] * 2,
        [pl.BlockSpec(memory_space=pltpu.HBM)] * 2,
        "theta_edges",
        [pltpu.SemaphoreType.DMA((4,))],
        room=58 * 1024 * 1024,
    )(corona, kappa)
    t_low = shifted(high, "lat", 1)
    t_high = shifted(low, "lat", -1)

    edge = (fields + 1, 2 * tile_t, radial)
    low, high = call(
        functools.partial(phi_edges, tile_t, tile_p), [edge] * 2, [vspec()] * 2, "phi_edges"
    )(corona.reshape(fields, tile_t * tile_p, radial), kappa.reshape(tile_t * tile_p, radial))
    p_low = shifted(high, "lon", 1)
    p_high = shifted(low, "lon", -1)

    table = jax.ShapeDtypeStruct((tile_t * tile_p, count), BF16)
    rank, meta, hit, table_high, table_low, w_r = call(
        functools.partial(plan, face_t, tile_t, tile_p),
        [(1, count), (n_dev, 128), jax.ShapeDtypeStruct((n_dev, count), BF16), table, table]
        + [(SH, count)],
        [vspec()] * 4,
        "plan",
    )(owner, dest_cell, base, fractions)

    t_low, t_high, rank = lax.optimization_barrier((t_low, t_high, rank))
    own_low, own_high = call(
        corner_cells, [(2, fields + 1, radial)] * 2, [vspec()] * 2, "corner_cells"
    )(t_low, t_high)
    c_low = shifted(own_high, "lon", 1)
    c_high = shifted(own_low, "lon", -1)

    flat = (fields, tile_t * tile_p, radial)
    (almost,) = call(
        functools.partial(steps, tile_t, tile_p),
        [(fields * tile_t * tile_p, radial)],
        [sspec()] + [vspec()] * 6,
        "steps",
        [
            VMEM(((tile_t + 4) * (tile_p + 4), fields, radial), F32),
            VMEM(((tile_t + 2) * (tile_p + 2), fields, radial), F32),
            VMEM((tile_t + 4, tile_p + 16, radial), F32),
            VMEM((tile_t + 2, 7, tile_p + 8, radial), F32),
        ],
    )(
        mixing,
        corona.reshape(-1, radial),
        kappa,
        t_low.reshape(-1, radial),
        t_high.reshape(-1, radial),
        p_low.reshape(-1, radial),
        p_high.reshape(-1, radial),
    )
    almost = almost.reshape(flat)

    patch, message = call(
        functools.partial(route, n_dev),
        [(4, fields, radial), (2 * n_dev, 128)],
        [vspec()] * 14,
        "route",
        [VMEM((tile_t * tile_p, radial), F32)],
    )(
        kappa, p_low, p_high, own_low, own_high, c_low, c_high, almost, rank, meta, hit, table_high,
        table_low, w_r,
    )
    (stepped,) = call(
        functools.partial(finish, tile_t, tile_p), [flat], [vspec()] * 2, "finish"
    )(almost, patch)

    got = lax.all_to_all(message, ("lat", "lon"), split_axis=0, concat_axis=0, tiled=True)

    coupled, p_first, p_last, t_first, t_last = call(
        functools.partial(land, n_dev),
        [helio_prev.shape, (fields, face_t), (fields, face_t)] + [(1, fields * face_p)] * 2,
        [vspec()] * 2,
        "land",
    )(got, helio_prev)
    from_t_low = shifted(t_last, "lat", 1)
    from_t_high = shifted(t_first, "lat", -1)
    from_p_low = shifted(p_last, "lon", 1)
    from_p_high = shifted(p_first, "lon", -1)
    (face,) = call(smooth, [helio_prev.shape], [vspec()] * 5, "smooth")(
        coupled, from_p_low, from_p_high, from_t_low, from_t_high
    )
    return (stepped.reshape(corona.shape), face)


def solution(mesh):
    return jax.shard_map(
        body,
        mesh=mesh,
        in_specs=(
            P(None, "lat", "lon", None),
            P("lat", "lon", None),
            P(),
            P(None, "lon", "lat"),
            P(("lat", "lon"), None),
            P(("lat", "lon")),
            P(("lat", "lon")),
            P(None, ("lat", "lon")),
        ),
        out_specs=(P(None, "lat", "lon", None), P(None, "lon", "lat")),
        check_vma=False,
    )
```

```python
import functools

import jax
import jax.numpy as jnp
from jax import lax
from jax.experimental import pallas as pl
from jax.experimental.pallas import tpu as pltpu
from jax.sharding import PartitionSpec as P

SH = 8
CAP = 16
BLOCK = 256
UNROLL = 16
VMEM = pltpu.VMEM
F32 = jnp.float32
BF16 = jnp.bfloat16


def vspec():
    return pl.BlockSpec(memory_space=VMEM)


def sspec():
    return pl.BlockSpec(memory_space=pltpu.SMEM)


def iota(shape, dim):
    return lax.broadcasted_iota(jnp.int32, shape, dim)


def halves(x):
    high = x.astype(BF16)
    return high, (x - high.astype(F32)).astype(BF16)


def shifted(x, axis, step):
    count = lax.axis_size(axis)
    return lax.ppermute(x, axis, [(i, (i + step) % count) for i in range(count)])


def theta_edges(corona, kappa, low, high, sems):
    fields, tile_t = corona.shape[0], corona.shape[1]
    copies = []
    for side, (out, start) in enumerate(((low, 0), (high, tile_t - 2))):
        rows = pl.ds(start, 2)
        copies.append(
            pltpu.make_async_copy(corona.at[:, rows], out.at[pl.ds(0, fields)], sems.at[2 * side])
        )
        copies.append(pltpu.make_async_copy(kappa.at[rows], out.at[fields], sems.at[2 * side + 1]))
    for copy in copies:
        copy.start()
    for copy in copies:
        copy.wait()


def phi_edges(tile_t, tile_p, corona, kappa, low, high):
    fields = corona.shape[0]
    for f in range(fields + 1):
        for out, near, far in ((low, 0, 1), (high, tile_p - 1, tile_p - 2)):
            for at, col in ((0, near), (tile_t, far)):
                rows = pl.ds(col, tile_t, stride=tile_p)
                out[f, at : at + tile_t, :] = corona[f, rows, :] if f < fields else kappa[rows, :]


def corner_cells(t_low, t_high, low, high):
    count, _, tile_p, _ = t_low.shape
    for f in range(count):
        for out, col in ((low, 0), (high, tile_p - 1)):
            out[0, f : f + 1, :] = t_low[f, 1, col : col + 1, :]
            out[1, f : f + 1, :] = t_high[f, 0, col : col + 1, :]


def exists():
    found = []
    for axis in ("lat", "lon"):
        at, count = lax.axis_index(axis), lax.axis_size(axis)
        found.append([jnp.where(at > 0, 1.0, 0.0), jnp.where(at < count - 1, 1.0, 0.0)])
    return found


def plan(
    face_t, tile_t, tile_p, owner, dest, base, frac, rank_out, meta_out, hit_out, high_out, low_out,
    radial_out,
):
    n_dev = meta_out.shape[0]
    count = owner.shape[1]
    width = min(BLOCK, count)
    before = (iota((width, width), 0) < iota((width, width), 1)).astype(F32).astype(BF16)
    owners = iota((n_dev, width), 0)
    slots = iota((CAP, width), 0).astype(F32)
    carry = jnp.zeros((n_dev, 1), F32)
    meta = jnp.zeros((n_dev, 128), F32)
    for b in range(count // width):
        cols = slice(b * width, (b + 1) * width)
        hit = owners == owner[:, cols]
        hit_f = jnp.where(hit, 1.0, 0.0)
        hit_b = hit_f.astype(BF16)
        hit_out[:, cols] = hit_b
        ahead = jnp.dot(hit_b, before, preferred_element_type=F32) + carry
        rank = jnp.sum(jnp.where(hit, ahead, 0.0), axis=0, keepdims=True)
        carry = ahead[:, width - 1 : width] + hit_f[:, width - 1 : width]
        rank_out[:, cols] = rank
        cell = dest[:, cols]
        cell_t = (cell % face_t).astype(F32)
        cell_p = (cell // face_t).astype(F32)
        mine = slots == rank
        rows = jnp.concatenate(
            [
                jnp.where(mine, cell_t, 0.0),
                jnp.where(mine, cell_p, 0.0),
                jnp.zeros((128 - 2 * CAP, width), F32),
            ],
            axis=0,
        ).astype(BF16)
        meta = meta + lax.dot_general(
            hit_b, rows, (((1,), (1,)), ((), ())), preferred_element_type=F32
        )
        corner = base[:, cols]

        def pair(size, at, fraction):
            rows = iota((size, width), 0)
            return jnp.where(rows == at, 1.0 - fraction, jnp.where(rows == at + 1, fraction, 0.0))

        w_t = pair(tile_t, corner // (tile_p * SH), frac[0:1, cols])
        w_p = pair(tile_p, (corner // SH) % tile_p, frac[1:2, cols])
        radial_out[:, cols] = pair(SH, corner % SH, frac[2:3, cols])
        table = (w_t[:, None, :] * w_p[None, :, :]).reshape(tile_t * tile_p, width)
        high_out[:, cols], low_out[:, cols] = halves(table)
    meta_out[...] = meta


def spread(mixing, spread_out):
    fields = mixing.shape[0]
    for g in range(fields):
        for f in range(fields):
            spread_out[g * fields + f] = jnp.full(spread_out.shape[1:], 0.3 * mixing[g, f], F32)


def flux(mix, conds, centres, near):
    kc, *kn = conds
    radial = kc.shape[-1]
    fields = len(centres)
    lane = iota(kc.shape, 1)
    weights = [0.075 * (kc + k) for k in kn]
    up = 0.075 * (kc + jnp.where(lane == radial - 1, 0.0, pltpu.roll(kc, radial - 1, 1)))
    down = 0.075 * (kc + jnp.where(lane == 0, 0.0, pltpu.roll(kc, 1, 1)))
    total = 1.0 - ((weights[0] + weights[1]) + (weights[2] + weights[3]) + (up + down))
    up = jnp.where(lane == radial - 1, 0.0, up)
    down = jnp.where(lane == 0, 0.0, down)
    for g in range(fields):
        c = centres[g]
        acc = total * c
        for w, beside in zip(weights, near(g)):
            acc = acc + w * beside
        acc = acc + up * pltpu.roll(c, radial - 1, 1) + down * pltpu.roll(c, 1, 1)
        for f in range(fields):
            m = mix[g * fields + f]
            acc = acc + jnp.concatenate([m] * (c.shape[0] // 8), axis=0) * centres[f]
        yield g, acc


WIDE = 32


def along_phi(ref, f, t, tile_p, dt=0, dp=0):
    at = (t + dt) * WIDE + 8 + dp
    if isinstance(t, jax.Array) and dp == 0:
        at = pl.multiple_of(at, 8)
    return ref[f, pl.ds(at, tile_p), :]


def along_theta(ref, f, t, p, count):
    return ref[f, pl.ds(t * WIDE + 8 + p, count, stride=WIDE), :]


AROUND = ((-1, 0), (1, 0), (0, -1), (0, 1))


def row_flux(mix, field, cond, t_field, t_cond, tile_p, fields):
    last = cond.shape[0] - 1
    return flux(
        mix,
        [along_phi(cond, last, t_cond, tile_p)]
        + [along_phi(cond, last, t_cond, tile_p, *d) for d in AROUND],
        [along_phi(field, f, t_field, tile_p) for f in range(fields)],
        lambda g: [along_phi(field, g, t_field, tile_p, *d) for d in AROUND],
    )


def column_flux(mix, field, cond, t_field, t_cond, p, count, fields):
    last = cond.shape[0] - 1
    return flux(
        mix,
        [along_theta(cond, last, t_cond, p, count)]
        + [along_theta(cond, last, t_cond + dt, p + dp, count) for dt, dp in AROUND],
        [along_theta(field, f, t_field, p, count) for f in range(fields)],
        lambda g: [along_theta(field, g, t_field + dt, p + dp, count) for dt, dp in AROUND],
    )


def steps(mixing, corona, kappa, t_low, t_high, p_low, p_high, stepped, wide, once, mix):
    fields, tile_t, tile_p, radial = corona.shape
    has_t, has_p = exists()
    spread(mixing, mix)
    nothing = jnp.zeros((1, radial), F32)
    for f in range(fields + 1):
        for t in range(tile_t):
            own = corona[f, t] if f < fields else kappa[t]
            wide[f, pl.ds((t + 2) * WIDE + 8, tile_p), :] = own
        for k in range(2):
            wide[f, pl.ds(k * WIDE + 8, tile_p), :] = t_low[f, k] * has_t[0]
            wide[f, pl.ds((tile_t + 2 + k) * WIDE + 8, tile_p), :] = t_high[f, k] * has_t[1]
        for side, (halo, near, far) in enumerate(((p_low, 7, 6), (p_high, 8 + tile_p, 9 + tile_p))):
            for k, col in enumerate((near, far)):
                cells = halo[f, k * tile_t : (k + 1) * tile_t, :] * has_p[side]
                wide[f, pl.ds(2 * WIDE + col, tile_t, stride=WIDE), :] = cells
            for t in (1, tile_t + 2):
                wide[f, pl.ds(t * WIDE + near, 1), :] = nothing

    def first(t):
        for g, acc in row_flux(mix, wide, wide, t + 2, t + 2, tile_p, fields):
            if isinstance(t, int) and t in (-1, tile_t):
                acc = acc * has_t[0 if t < 0 else 1]
            at = (t + 1) * WIDE + 8
            once[g, pl.ds(at if isinstance(t, int) else pl.multiple_of(at, 8), tile_p), :] = acc

    def second(t):
        for g, acc in row_flux(mix, once, wide, t + 1, t + 2, tile_p, fields):
            stepped[g, t] = acc

    first(-1)
    first(tile_t)
    for p in (-1, tile_p):
        for g, acc in column_flux(mix, wide, wide, 2, 2, p, tile_t, fields):
            once[g, pl.ds(WIDE + 8 + p, tile_t, stride=WIDE), :] = acc * has_p[0 if p < 0 else 1]
    for row in (first, second):
        by_rows(row, tile_t)


def by_rows(row, count):
    if UNROLL >= count:
        for t in range(count):
            row(t)
        return

    def some(i, carry):
        for k in range(UNROLL):
            row(i * UNROLL + k)
        return carry

    lax.fori_loop(0, count // UNROLL, some, 0)


def route(
    n_dev, kappa, p_low, p_high, own_low, own_high, c_low, c_high, stepped, rank, meta, hit,
    table_high, table_low, w_r, patch, message, shell,
):
    fields, columns, radial = stepped.shape
    tile_t, tile_p, _ = kappa.shape
    has_t, has_p = exists()
    lane = iota((columns, radial), 1)
    rows = jnp.zeros((columns, radial), F32)
    for f in range(fields):
        moved = pltpu.roll(stepped[f], (f * SH + SH) % radial, 1)
        rows = jnp.where(lane // SH == f, moved, rows)
    shell[...] = rows
    for a in range(2):
        for b, (halo, own, diagonal) in enumerate(
            ((p_low, own_low, c_low), (p_high, own_high, c_high))
        ):
            t, p = a * (tile_t - 1), b * (tile_p - 1)
            k_t, u_t = own[a, fields : fields + 1] * has_t[a], own[a, 0:fields] * has_t[a]
            k_p = halo[fields, t : t + 1, :] * has_p[b]
            u_p = jnp.concatenate([halo[f, t : t + 1, :] for f in range(fields)], axis=0) * has_p[b]
            both = has_t[a] * has_p[b]
            k_d, u_d = diagonal[a, fields : fields + 1] * both, diagonal[a, 0:fields] * both
            k = kappa[t, p : p + 1, :]
            by_t = 0.075 * ((k_t + k_d) * u_d - k_d * u_t)
            by_p = 0.075 * ((k_p + k_d) * u_d - k_d * u_p)
            extra = 0.075 * ((k + k_t) * by_t + (k + k_p) * by_p)
            patch[2 * a + b] = extra
            row = jnp.zeros((1, radial), F32)
            for f in range(fields):
                moved = pltpu.roll(extra[f : f + 1], (f * SH + SH) % radial, 1)
                row = jnp.where(lane[0:1] // SH == f, moved, row)
            at = t * tile_p + p
            shell[at : at + 1, :] = shell[at : at + 1, :] + row
    rows = shell[...]
    high = rows.astype(BF16).astype(F32)
    both = high + pltpu.roll(rows - high, fields * SH, 1)
    left = jnp.transpose(both).astype(BF16)

    count = rank.shape[1]
    width = min(BLOCK, count)
    packed = jnp.zeros((n_dev, 2 * fields * CAP), F32)
    for b in range(count // width):
        cols = slice(b * width, (b + 1) * width)
        coarse = jnp.dot(left, table_high[:, cols], preferred_element_type=F32)
        fine = jnp.dot(left[: fields * SH], table_low[:, cols], preferred_element_type=F32)
        by_layer = coarse[: fields * SH] + (coarse[fields * SH :] + fine)
        value = jnp.sum(by_layer.reshape(fields, SH, width) * w_r[:, cols][None], axis=1)
        order = rank[:, cols]
        placed = jnp.concatenate(
            [jnp.where(order == float(k), value, 0.0) for k in range(CAP)], axis=0
        )
        placed_high, placed_low = halves(placed)
        packed = packed + lax.dot_general(
            hit[:, cols],
            jnp.concatenate([placed_high, placed_low], axis=0),
            (((1,), (1,)), ((), ())),
            preferred_element_type=F32,
        )
    half = fields * CAP
    message[pl.ds(0, n_dev, stride=2), :] = packed[:, :half] + packed[:, half:]
    message[pl.ds(1, n_dev, stride=2), :] = meta[...]


def finish(tile_t, tile_p, stepped, patch, out):
    out[...] = stepped[...]
    for a in range(2):
        for b in range(2):
            at = a * (tile_t - 1) * tile_p + b * (tile_p - 1)
            for f in range(stepped.shape[0]):
                out[f, at : at + 1, :] = (
                    stepped[f, at : at + 1, :] + patch[2 * a + b, f : f + 1, :]
                )


def land(n_dev, got, prev, coupled, p_first, p_last, t_first, t_last):
    fields, face_p, face_t = prev.shape
    values = jnp.transpose(got[pl.ds(0, n_dev, stride=2), :])
    cells = jnp.transpose(got[pl.ds(1, n_dev, stride=2), :])
    along_t = iota((face_t, n_dev), 0).astype(F32)
    along_p = iota((face_p, n_dev), 0).astype(F32)
    rows = fields * face_p
    total = jnp.zeros((2 * rows, face_t), F32)
    for k in range(CAP):
        at_t = jnp.where(along_t == cells[k : k + 1, :], 1.0, 0.0).astype(BF16)
        at_p = along_p == cells[CAP + k : CAP + k + 1, :]
        value = values[k * fields : (k + 1) * fields, :]
        high = value.astype(BF16).astype(F32)
        parts = [
            jnp.where(at_p[None], part[:, None, :], 0.0).reshape(rows, n_dev).astype(BF16)
            for part in (high, value - high)
        ]
        total = total + lax.dot_general(
            jnp.concatenate(parts, axis=0),
            at_t,
            (((1,), (1,)), ((), ())),
            preferred_element_type=F32,
        )
    new = prev[...].reshape(rows, face_t) + (total[:rows] + total[rows:])
    coupled[...] = new.reshape(fields, face_p, face_t)
    turned = jnp.transpose(new)
    t_first[...] = turned[0:1, :]
    t_last[...] = turned[face_t - 1 : face_t, :]
    for f in range(fields):
        p_first[f : f + 1, :] = new[f * face_p : f * face_p + 1, :]
        p_last[f : f + 1, :] = new[(f + 1) * face_p - 1 : (f + 1) * face_p, :]


def smooth(coupled, p_low, p_high, t_low, t_high, out):
    fields, face_p, face_t = coupled.shape
    x = coupled[...]
    row = iota((face_p, face_t), 0)[None]
    lane = iota((face_p, face_t), 1)[None]

    has_t, has_p = exists()

    def rim(ref, has):
        return ref[...] * has

    def column(edge):
        return jnp.transpose(jnp.broadcast_to(edge, (face_t, fields * face_p))).reshape(x.shape)

    below = jnp.where(row == 0, rim(p_low, has_p[0])[:, None, :], pltpu.roll(x, 1, 1))
    above = jnp.where(
        row == face_p - 1, rim(p_high, has_p[1])[:, None, :], pltpu.roll(x, face_p - 1, 1)
    )
    left = jnp.where(lane == 0, column(rim(t_low, has_t[0])), pltpu.roll(x, 1, 2))
    right = jnp.where(
        lane == face_t - 1, column(rim(t_high, has_t[1])), pltpu.roll(x, face_t - 1, 2)
    )
    out[...] = x + 0.2 * (above + below + right + left - 4.0 * x)


def call(kernel, outs, specs, name, scratch=(), room=40 * 1024 * 1024):
    outs = [s if isinstance(s, jax.ShapeDtypeStruct) else jax.ShapeDtypeStruct(s, F32) for s in outs]
    return pl.pallas_call(
        kernel,
        out_shape=outs,
        in_specs=specs,
        out_specs=[vspec()] * len(outs),
        scratch_shapes=list(scratch),
        name=name,
        compiler_params=pltpu.CompilerParams(vmem_limit_bytes=room),
    )


def body(corona, kappa, mixing, helio_prev, owner, dest_cell, corner_base, fractions):
    fields, tile_t, tile_p, radial = corona.shape
    n_lat, n_lon = lax.axis_size("lat"), lax.axis_size("lon")
    n_dev = n_lat * n_lon
    count = corner_base.shape[0]
    _, face_p, face_t = helio_prev.shape
    owner = owner.reshape(1, count)
    dest_cell = dest_cell.reshape(1, count)
    base = corner_base.reshape(1, count)
    edge = (fields + 1, 2, tile_p, radial)
    low, high = call(
        theta_edges,
        [edge] * 2,
        [pl.BlockSpec(memory_space=pltpu.HBM)] * 2,
        "theta_edges",
        [pltpu.SemaphoreType.DMA((4,))],
        room=58 * 1024 * 1024,
    )(corona, kappa)
    t_low = shifted(high, "lat", 1)
    t_high = shifted(low, "lat", -1)

    edge = (fields + 1, 2 * tile_t, radial)
    low, high = call(
        functools.partial(phi_edges, tile_t, tile_p), [edge] * 2, [vspec()] * 2, "phi_edges"
    )(corona.reshape(fields, tile_t * tile_p, radial), kappa.reshape(tile_t * tile_p, radial))
    p_low = shifted(high, "lon", 1)
    p_high = shifted(low, "lon", -1)

    table = jax.ShapeDtypeStruct((tile_t * tile_p, count), BF16)
    rank, meta, hit, table_high, table_low, w_r = call(
        functools.partial(plan, face_t, tile_t, tile_p),
        [(1, count), (n_dev, 128), jax.ShapeDtypeStruct((n_dev, count), BF16), table, table]
        + [(SH, count)],
        [vspec()] * 4,
        "plan",
    )(owner, dest_cell, base, fractions)

    t_low, t_high, rank = lax.optimization_barrier((t_low, t_high, rank))
    own_low, own_high = call(
        corner_cells, [(2, fields + 1, radial)] * 2, [vspec()] * 2, "corner_cells"
    )(t_low, t_high)
    c_low = shifted(own_high, "lon", 1)
    c_high = shifted(own_low, "lon", -1)

    flat = (fields, tile_t * tile_p, radial)
    (almost,) = call(
        steps,
        [corona.shape],
        [sspec()] + [vspec()] * 6,
        "steps",
        [
            VMEM((fields + 1, (tile_t + 4) * WIDE, radial), F32),
            VMEM((fields, (tile_t + 2) * WIDE, radial), F32),
            VMEM((fields * fields, 8, radial), F32),
        ],
    )(mixing, corona, kappa, t_low, t_high, p_low, p_high)
    almost = almost.reshape(flat)

    patch, message = call(
        functools.partial(route, n_dev),
        [(4, fields, radial), (2 * n_dev, 128)],
        [vspec()] * 14,
        "route",
        [VMEM((tile_t * tile_p, radial), F32)],
    )(
        kappa, p_low, p_high, own_low, own_high, c_low, c_high, almost, rank, meta, hit, table_high,
        table_low, w_r,
    )
    (stepped,) = call(
        functools.partial(finish, tile_t, tile_p), [flat], [vspec()] * 2, "finish"
    )(almost, patch)

    got = lax.all_to_all(message, ("lat", "lon"), split_axis=0, concat_axis=0, tiled=True)

    coupled, p_first, p_last, t_first, t_last = call(
        functools.partial(land, n_dev),
        [helio_prev.shape, (fields, face_t), (fields, face_t)] + [(1, fields * face_p)] * 2,
        [vspec()] * 2,
        "land",
    )(got, helio_prev)
    from_t_low = shifted(t_last, "lat", 1)
    from_t_high = shifted(t_first, "lat", -1)
    from_p_low = shifted(p_last, "lon", 1)
    from_p_high = shifted(p_first, "lon", -1)
    (face,) = call(smooth, [helio_prev.shape], [vspec()] * 5, "smooth")(
        coupled, from_p_low, from_p_high, from_t_low, from_t_high
    )
    return (stepped.reshape(corona.shape), face)


def solution(mesh):
    return jax.shard_map(
        body,
        mesh=mesh,
        in_specs=(
            P(None, "lat", "lon", None),
            P("lat", "lon", None),
            P(),
            P(None, "lon", "lat"),
            P(("lat", "lon"), None),
            P(("lat", "lon")),
            P(("lat", "lon")),
            P(None, ("lat", "lon")),
        ),
        out_specs=(P(None, "lat", "lon", None), P(None, "lon", "lat")),
        check_vma=False,
    )
```

```python
import functools

import jax
import jax.numpy as jnp
from jax import lax
from jax.experimental import pallas as pl
from jax.experimental.pallas import tpu as pltpu
from jax.sharding import PartitionSpec as P

SH = 8
CAP = 16
BLOCK = 256
UNROLL = 16
VMEM = pltpu.VMEM
F32 = jnp.float32
BF16 = jnp.bfloat16


def vspec():
    return pl.BlockSpec(memory_space=VMEM)


def sspec():
    return pl.BlockSpec(memory_space=pltpu.SMEM)


def iota(shape, dim):
    return lax.broadcasted_iota(jnp.int32, shape, dim)


def halves(x):
    high = x.astype(BF16)
    return high, (x - high.astype(F32)).astype(BF16)


def swapped(first, second, axis):
    count = lax.axis_size(axis)
    other = [(i + (1 if i % 2 else -1)) % count for i in range(count)]
    return (
        lax.ppermute(first, axis, [(i, i ^ 1) for i in range(count)]),
        lax.ppermute(second, axis, list(enumerate(other))),
    )


def parity(axis):
    return lax.rem(lax.axis_index(axis), 2)


def sides(axis):
    at, count = lax.axis_index(axis), lax.axis_size(axis)
    odd = parity(axis).astype(F32)
    low = jnp.where(at > 0, 1.0, 0.0)
    high = jnp.where(at < count - 1, 1.0, 0.0)
    return (odd * low, (1.0 - odd) * low), ((1.0 - odd) * high, odd * high)


def blend(weights, first, second):
    return first * weights[0] + second * weights[1]


def theta_edges(corona, kappa, first, second, sems):
    fields, tile_t = corona.shape[0], corona.shape[1]
    odd = parity("lat")
    copies = []
    for n, (out, start) in enumerate(
        ((first, (1 - odd) * (tile_t - 2)), (second, odd * (tile_t - 2)))
    ):
        rows = pl.ds(start, 2)
        copies.append(
            pltpu.make_async_copy(corona.at[:, rows], out.at[pl.ds(0, fields)], sems.at[2 * n])
        )
        copies.append(pltpu.make_async_copy(kappa.at[rows], out.at[fields], sems.at[2 * n + 1]))
    for copy in copies:
        copy.start()
    for copy in copies:
        copy.wait()


def phi_edges(tile_t, tile_p, corona, kappa, first, second):
    fields = corona.shape[0]
    odd = parity("lon")
    for out, upper in ((first, 1 - odd), (second, odd)):
        near = upper * (tile_p - 1)
        far = upper * (tile_p - 3) + 1
        for f in range(fields + 1):
            for at, col in ((0, near), (tile_t, far)):
                rows = pl.ds(col, tile_t, stride=tile_p)
                out[f, at : at + tile_t, :] = corona[f, rows, :] if f < fields else kappa[rows, :]


def corner_cells(t_first, t_second, low, high, first, second):
    count, _, tile_p, _ = t_first.shape
    weights = sides("lat")
    for a, row in ((0, 1), (1, 0)):
        for f in range(count):
            for out, col in ((low, 0), (high, tile_p - 1)):
                cell = slice(col, col + 1)
                out[a, f : f + 1, :] = blend(
                    weights[a], t_first[f, row, cell, :], t_second[f, row, cell, :]
                )
    odd = parity("lon").astype(F32)
    first[...] = blend((odd, 1.0 - odd), low[...], high[...])
    second[...] = blend((1.0 - odd, odd), low[...], high[...])


def plan(
    face_t, tile_t, tile_p, owner, dest, base, frac, rank_out, meta_out, hit_out, high_out, low_out,
    radial_out,
):
    n_dev = meta_out.shape[0]
    count = owner.shape[1]
    width = min(BLOCK, count)
    before = (iota((width, width), 0) < iota((width, width), 1)).astype(F32).astype(BF16)
    owners = iota((n_dev, width), 0)
    slots = iota((CAP, width), 0).astype(F32)
    carry = jnp.zeros((n_dev, 1), F32)
    meta = jnp.zeros((n_dev, 128), F32)
    for b in range(count // width):
        cols = slice(b * width, (b + 1) * width)
        hit = owners == owner[:, cols]
        hit_f = jnp.where(hit, 1.0, 0.0)
        hit_b = hit_f.astype(BF16)
        hit_out[:, cols] = hit_b
        ahead = jnp.dot(hit_b, before, preferred_element_type=F32) + carry
        rank = jnp.sum(jnp.where(hit, ahead, 0.0), axis=0, keepdims=True)
        carry = ahead[:, width - 1 : width] + hit_f[:, width - 1 : width]
        rank_out[:, cols] = rank
        cell = dest[:, cols]
        cell_t = (cell % face_t).astype(F32)
        cell_p = (cell // face_t).astype(F32)
        mine = slots == rank
        rows = jnp.concatenate(
            [
                jnp.where(mine, cell_t, 0.0),
                jnp.where(mine, cell_p, 0.0),
                jnp.zeros((128 - 2 * CAP, width), F32),
            ],
            axis=0,
        ).astype(BF16)
        meta = meta + lax.dot_general(
            hit_b, rows, (((1,), (1,)), ((), ())), preferred_element_type=F32
        )
        corner = base[:, cols]

        def pair(size, at, fraction):
            rows = iota((size, width), 0)
            return jnp.where(rows == at, 1.0 - fraction, jnp.where(rows == at + 1, fraction, 0.0))

        w_t = pair(tile_t, corner // (tile_p * SH), frac[0:1, cols])
        w_p = pair(tile_p, (corner // SH) % tile_p, frac[1:2, cols])
        radial_out[:, cols] = pair(SH, corner % SH, frac[2:3, cols])
        table = (w_t[:, None, :] * w_p[None, :, :]).reshape(tile_t * tile_p, width)
        high_out[:, cols], low_out[:, cols] = halves(table)
    meta_out[...] = meta


def spread(mixing, spread_out):
    fields = mixing.shape[0]
    for g in range(fields):
        for f in range(fields):
            spread_out[g * fields + f] = jnp.full(spread_out.shape[1:], 0.3 * mixing[g, f], F32)


def flux(mix, conds, centres, near):
    kc, *kn = conds
    radial = kc.shape[-1]
    fields = len(centres)
    lane = iota(kc.shape, 1)
    weights = [0.075 * (kc + k) for k in kn]
    up = 0.075 * (kc + jnp.where(lane == radial - 1, 0.0, pltpu.roll(kc, radial - 1, 1)))
    down = 0.075 * (kc + jnp.where(lane == 0, 0.0, pltpu.roll(kc, 1, 1)))
    total = 1.0 - ((weights[0] + weights[1]) + (weights[2] + weights[3]) + (up + down))
    up = jnp.where(lane == radial - 1, 0.0, up)
    down = jnp.where(lane == 0, 0.0, down)
    for g in range(fields):
        c = centres[g]
        acc = total * c
        for w, beside in zip(weights, near(g)):
            acc = acc + w * beside
        acc = acc + up * pltpu.roll(c, radial - 1, 1) + down * pltpu.roll(c, 1, 1)
        for f in range(fields):
            m = mix[g * fields + f]
            acc = acc + jnp.concatenate([m] * (c.shape[0] // 8), axis=0) * centres[f]
        yield g, acc


WIDE = 32


def along_phi(ref, f, t, tile_p, dt=0, dp=0):
    at = (t + dt) * WIDE + 8 + dp
    if isinstance(t, jax.Array) and dp == 0:
        at = pl.multiple_of(at, 8)
    return ref[f, pl.ds(at, tile_p), :]


def along_theta(ref, f, t, p, count):
    return ref[f, pl.ds(t * WIDE + 8 + p, count, stride=WIDE), :]


AROUND = ((-1, 0), (1, 0), (0, -1), (0, 1))


def row_flux(mix, field, cond, t_field, t_cond, tile_p, fields):
    last = cond.shape[0] - 1
    return flux(
        mix,
        [along_phi(cond, last, t_cond, tile_p)]
        + [along_phi(cond, last, t_cond, tile_p, *d) for d in AROUND],
        [along_phi(field, f, t_field, tile_p) for f in range(fields)],
        lambda g: [along_phi(field, g, t_field, tile_p, *d) for d in AROUND],
    )


def column_flux(mix, field, cond, t_field, t_cond, p, count, fields):
    last = cond.shape[0] - 1
    return flux(
        mix,
        [along_theta(cond, last, t_cond, p, count)]
        + [along_theta(cond, last, t_cond + dt, p + dp, count) for dt, dp in AROUND],
        [along_theta(field, f, t_field, p, count) for f in range(fields)],
        lambda g: [along_theta(field, g, t_field + dt, p + dp, count) for dt, dp in AROUND],
    )


def steps(
    mixing, corona, kappa, t_first, t_second, p_first, p_second, stepped, wide, once, mix,
):
    fields, tile_t, tile_p, radial = corona.shape
    by_t, by_p = sides("lat"), sides("lon")
    has_t = [low + high for low, high in by_t]
    has_p = [low + high for low, high in by_p]
    spread(mixing, mix)
    nothing = jnp.zeros((1, radial), F32)
    for f in range(fields + 1):
        for t in range(tile_t):
            own = corona[f, t] if f < fields else kappa[t]
            wide[f, pl.ds((t + 2) * WIDE + 8, tile_p), :] = own
        for k in range(2):
            for side, t in enumerate((k, tile_t + 2 + k)):
                wide[f, pl.ds(t * WIDE + 8, tile_p), :] = blend(
                    by_t[side], t_first[f, k], t_second[f, k]
                )
        for side, (near, far) in enumerate(((7, 6), (8 + tile_p, 9 + tile_p))):
            for k, col in enumerate((near, far)):
                rows = slice(k * tile_t, (k + 1) * tile_t)
                cells = blend(by_p[side], p_first[f, rows, :], p_second[f, rows, :])
                wide[f, pl.ds(2 * WIDE + col, tile_t, stride=WIDE), :] = cells
            for t in (1, tile_t + 2):
                wide[f, pl.ds(t * WIDE + near, 1), :] = nothing

    def first(t):
        for g, acc in row_flux(mix, wide, wide, t + 2, t + 2, tile_p, fields):
            if isinstance(t, int) and t in (-1, tile_t):
                acc = acc * has_t[0 if t < 0 else 1]
            at = (t + 1) * WIDE + 8
            once[g, pl.ds(at if isinstance(t, int) else pl.multiple_of(at, 8), tile_p), :] = acc

    def second(t):
        for g, acc in row_flux(mix, once, wide, t + 1, t + 2, tile_p, fields):
            stepped[g, t] = acc

    first(-1)
    first(tile_t)
    for p in (-1, tile_p):
        for g, acc in column_flux(mix, wide, wide, 2, 2, p, tile_t, fields):
            once[g, pl.ds(WIDE + 8 + p, tile_t, stride=WIDE), :] = acc * has_p[0 if p < 0 else 1]
    for row in (first, second):
        by_rows(row, tile_t)


def by_rows(row, count):
    if UNROLL >= count:
        for t in range(count):
            row(t)
        return

    def some(i, carry):
        for k in range(UNROLL):
            row(i * UNROLL + k)
        return carry

    lax.fori_loop(0, count // UNROLL, some, 0)


def route(
    n_dev, kappa, p_first, p_second, own_low, own_high, c_first, c_second, stepped, rank, meta, hit,
    table_high, table_low, w_r, patch, message, shell,
):
    fields, columns, radial = stepped.shape
    tile_t, tile_p, _ = kappa.shape
    sides_p = sides("lon")
    lane = iota((columns, radial), 1)
    rows = jnp.zeros((columns, radial), F32)
    for f in range(fields):
        moved = pltpu.roll(stepped[f], (f * SH + SH) % radial, 1)
        rows = jnp.where(lane // SH == f, moved, rows)
    shell[...] = rows
    for a in range(2):
        for b, own in enumerate((own_low, own_high)):
            t, p = a * (tile_t - 1), b * (tile_p - 1)

            def beside(f, t=t, weights=sides_p[b]):
                return blend(weights, p_first[f, t : t + 1, :], p_second[f, t : t + 1, :])

            k_t, u_t = own[a, fields : fields + 1], own[a, 0:fields]
            k_p = beside(fields)
            u_p = jnp.concatenate([beside(f) for f in range(fields)], axis=0)
            diagonal = blend(sides_p[b], c_first[a], c_second[a])
            k_d, u_d = diagonal[fields : fields + 1], diagonal[0:fields]
            k = kappa[t, p : p + 1, :]
            by_t = 0.075 * ((k_t + k_d) * u_d - k_d * u_t)
            by_p = 0.075 * ((k_p + k_d) * u_d - k_d * u_p)
            extra = 0.075 * ((k + k_t) * by_t + (k + k_p) * by_p)
            patch[2 * a + b] = extra
            row = jnp.zeros((1, radial), F32)
            for f in range(fields):
                moved = pltpu.roll(extra[f : f + 1], (f * SH + SH) % radial, 1)
                row = jnp.where(lane[0:1] // SH == f, moved, row)
            at = t * tile_p + p
            shell[at : at + 1, :] = shell[at : at + 1, :] + row
    rows = shell[...]
    high = rows.astype(BF16).astype(F32)
    both = high + pltpu.roll(rows - high, fields * SH, 1)
    left = jnp.transpose(both).astype(BF16)

    count = rank.shape[1]
    width = min(BLOCK, count)
    packed = jnp.zeros((n_dev, 2 * fields * CAP), F32)
    for b in range(count // width):
        cols = slice(b * width, (b + 1) * width)
        coarse = jnp.dot(left, table_high[:, cols], preferred_element_type=F32)
        fine = jnp.dot(left[: fields * SH], table_low[:, cols], preferred_element_type=F32)
        by_layer = coarse[: fields * SH] + (coarse[fields * SH :] + fine)
        value = jnp.sum(by_layer.reshape(fields, SH, width) * w_r[:, cols][None], axis=1)
        order = rank[:, cols]
        placed = jnp.concatenate(
            [jnp.where(order == float(k), value, 0.0) for k in range(CAP)], axis=0
        )
        placed_high, placed_low = halves(placed)
        packed = packed + lax.dot_general(
            hit[:, cols],
            jnp.concatenate([placed_high, placed_low], axis=0),
            (((1,), (1,)), ((), ())),
            preferred_element_type=F32,
        )
    half = fields * CAP
    message[pl.ds(0, n_dev, stride=2), :] = packed[:, :half] + packed[:, half:]
    message[pl.ds(1, n_dev, stride=2), :] = meta[...]


def finish(tile_t, tile_p, stepped, patch, out):
    out[...] = stepped[...]
    for a in range(2):
        for b in range(2):
            at = a * (tile_t - 1) * tile_p + b * (tile_p - 1)
            for f in range(stepped.shape[0]):
                out[f, at : at + 1, :] = (
                    stepped[f, at : at + 1, :] + patch[2 * a + b, f : f + 1, :]
                )


def land(n_dev, got, prev, coupled, p_first, p_second, t_first, t_second):
    fields, face_p, face_t = prev.shape
    values = jnp.transpose(got[pl.ds(0, n_dev, stride=2), :])
    cells = jnp.transpose(got[pl.ds(1, n_dev, stride=2), :])
    along_t = iota((face_t, n_dev), 0).astype(F32)
    along_p = iota((face_p, n_dev), 0).astype(F32)
    rows = fields * face_p
    total = jnp.zeros((2 * rows, face_t), F32)
    for k in range(CAP):
        at_t = jnp.where(along_t == cells[k : k + 1, :], 1.0, 0.0).astype(BF16)
        at_p = along_p == cells[CAP + k : CAP + k + 1, :]
        value = values[k * fields : (k + 1) * fields, :]
        high = value.astype(BF16).astype(F32)
        parts = [
            jnp.where(at_p[None], part[:, None, :], 0.0).reshape(rows, n_dev).astype(BF16)
            for part in (high, value - high)
        ]
        total = total + lax.dot_general(
            jnp.concatenate(parts, axis=0),
            at_t,
            (((1,), (1,)), ((), ())),
            preferred_element_type=F32,
        )
    new = prev[...].reshape(rows, face_t) + (total[:rows] + total[rows:])

    def edge(face, p):
        at = [f * face_p + p for f in range(fields)]
        return jnp.concatenate([face[k : k + 1, :] for k in at], axis=0)

    coupled[...] = new.reshape(fields, face_p, face_t)
    turned = jnp.transpose(new)
    for axis, low, high, first, second in (
        ("lat", turned[0:1, :], turned[face_t - 1 : face_t, :], t_first, t_second),
        ("lon", edge(new, 0), edge(new, face_p - 1), p_first, p_second),
    ):
        odd = parity(axis).astype(F32)
        first[...] = blend((odd, 1.0 - odd), low, high)
        second[...] = blend((1.0 - odd, odd), low, high)


def smooth(coupled, p_first, p_second, t_first, t_second, out):
    fields, face_p, face_t = coupled.shape
    x = coupled[...]
    row = iota((face_p, face_t), 0)[None]
    lane = iota((face_p, face_t), 1)[None]

    t_low, t_high = [blend(w, t_first[...], t_second[...]) for w in sides("lat")]
    p_low, p_high = [blend(w, p_first[...], p_second[...]) for w in sides("lon")]

    def column(edge):
        return jnp.transpose(jnp.broadcast_to(edge, (face_t, fields * face_p))).reshape(x.shape)

    below = jnp.where(row == 0, p_low[:, None, :], pltpu.roll(x, 1, 1))
    above = jnp.where(row == face_p - 1, p_high[:, None, :], pltpu.roll(x, face_p - 1, 1))
    left = jnp.where(lane == 0, column(t_low), pltpu.roll(x, 1, 2))
    right = jnp.where(lane == face_t - 1, column(t_high), pltpu.roll(x, face_t - 1, 2))
    out[...] = x + 0.2 * (above + below + right + left - 4.0 * x)


def call(kernel, outs, specs, name, scratch=(), room=40 * 1024 * 1024):
    outs = [s if isinstance(s, jax.ShapeDtypeStruct) else jax.ShapeDtypeStruct(s, F32) for s in outs]
    return pl.pallas_call(
        kernel,
        out_shape=outs,
        in_specs=specs,
        out_specs=[vspec()] * len(outs),
        scratch_shapes=list(scratch),
        name=name,
        compiler_params=pltpu.CompilerParams(vmem_limit_bytes=room),
    )


def body(corona, kappa, mixing, helio_prev, owner, dest_cell, corner_base, fractions):
    fields, tile_t, tile_p, radial = corona.shape
    n_lat, n_lon = lax.axis_size("lat"), lax.axis_size("lon")
    n_dev = n_lat * n_lon
    count = corner_base.shape[0]
    _, face_p, face_t = helio_prev.shape
    owner = owner.reshape(1, count)
    dest_cell = dest_cell.reshape(1, count)
    base = corner_base.reshape(1, count)
    edge = (fields + 1, 2, tile_p, radial)
    first, second = call(
        theta_edges,
        [edge] * 2,
        [pl.BlockSpec(memory_space=pltpu.HBM)] * 2,
        "theta_edges",
        [pltpu.SemaphoreType.DMA((4,))],
        room=58 * 1024 * 1024,
    )(corona, kappa)
    t_first, t_second = swapped(first, second, "lat")

    edge = (fields + 1, 2 * tile_t, radial)
    first, second = call(
        functools.partial(phi_edges, tile_t, tile_p), [edge] * 2, [vspec()] * 2, "phi_edges"
    )(corona.reshape(fields, tile_t * tile_p, radial), kappa.reshape(tile_t * tile_p, radial))
    p_first, p_second = swapped(first, second, "lon")

    table = jax.ShapeDtypeStruct((tile_t * tile_p, count), BF16)
    rank, meta, hit, table_high, table_low, w_r = call(
        functools.partial(plan, face_t, tile_t, tile_p),
        [(1, count), (n_dev, 128), jax.ShapeDtypeStruct((n_dev, count), BF16), table, table]
        + [(SH, count)],
        [vspec()] * 4,
        "plan",
    )(owner, dest_cell, base, fractions)

    t_first, t_second, rank = lax.optimization_barrier((t_first, t_second, rank))
    own_low, own_high, first, second = call(
        corner_cells, [(2, fields + 1, radial)] * 4, [vspec()] * 2, "corner_cells"
    )(t_first, t_second)
    c_first, c_second = swapped(first, second, "lon")

    flat = (fields, tile_t * tile_p, radial)
    (almost,) = call(
        steps,
        [corona.shape],
        [sspec()] + [vspec()] * 6,
        "steps",
        [
            VMEM((fields + 1, (tile_t + 4) * WIDE, radial), F32),
            VMEM((fields, (tile_t + 2) * WIDE, radial), F32),
            VMEM((fields * fields, 8, radial), F32),
        ],
    )(mixing, corona, kappa, t_first, t_second, p_first, p_second)
    almost = almost.reshape(flat)

    patch, message = call(
        functools.partial(route, n_dev),
        [(4, fields, radial), (2 * n_dev, 128)],
        [vspec()] * 14,
        "route",
        [VMEM((tile_t * tile_p, radial), F32)],
    )(
        kappa, p_first, p_second, own_low, own_high, c_first, c_second, almost, rank, meta, hit,
        table_high, table_low, w_r,
    )
    (stepped,) = call(
        functools.partial(finish, tile_t, tile_p), [flat], [vspec()] * 2, "finish"
    )(almost, patch)

    got = lax.all_to_all(message, ("lat", "lon"), split_axis=0, concat_axis=0, tiled=True)

    coupled, p_first, p_second, t_first, t_second = call(
        functools.partial(land, n_dev),
        [helio_prev.shape, (fields, face_t), (fields, face_t)] + [(1, fields * face_p)] * 2,
        [vspec()] * 2,
        "land",
    )(got, helio_prev)
    p_first, p_second = swapped(p_first, p_second, "lon")
    t_first, t_second = swapped(t_first, t_second, "lat")
    (face,) = call(smooth, [helio_prev.shape], [vspec()] * 5, "smooth")(
        coupled, p_first, p_second, t_first, t_second
    )
    return (stepped.reshape(corona.shape), face)


def solution(mesh):
    return jax.shard_map(
        body,
        mesh=mesh,
        in_specs=(
            P(None, "lat", "lon", None),
            P("lat", "lon", None),
            P(),
            P(None, "lon", "lat"),
            P(("lat", "lon"), None),
            P(("lat", "lon")),
            P(("lat", "lon")),
            P(None, ("lat", "lon")),
        ),
        out_specs=(P(None, "lat", "lon", None), P(None, "lon", "lat")),
        check_vma=False,
    )
```

```python
import functools

import jax
import jax.numpy as jnp
from jax import lax
from jax.experimental import pallas as pl
from jax.experimental.pallas import tpu as pltpu
from jax.sharding import PartitionSpec as P

SH = 8
CAP = 16
BLOCK = 256
UNROLL = 16
VMEM = pltpu.VMEM
F32 = jnp.float32
BF16 = jnp.bfloat16


def vspec():
    return pl.BlockSpec(memory_space=VMEM)


def sspec():
    return pl.BlockSpec(memory_space=pltpu.SMEM)


def iota(shape, dim):
    return lax.broadcasted_iota(jnp.int32, shape, dim)


def halves(x):
    high = x.astype(BF16)
    return high, (x - high.astype(F32)).astype(BF16)


def swapped(first, second, axis):
    count = lax.axis_size(axis)
    other = [(i + (1 if i % 2 else -1)) % count for i in range(count)]
    return (
        lax.ppermute(first, axis, [(i, i ^ 1) for i in range(count)]),
        lax.ppermute(second, axis, list(enumerate(other))),
    )


def parity(axis):
    return lax.rem(lax.axis_index(axis), 2)


def sides(axis):
    at, count = lax.axis_index(axis), lax.axis_size(axis)
    odd = parity(axis).astype(F32)
    low = jnp.where(at > 0, 1.0, 0.0)
    high = jnp.where(at < count - 1, 1.0, 0.0)
    return (odd * low, (1.0 - odd) * low), ((1.0 - odd) * high, odd * high)


def blend(weights, first, second):
    return first * weights[0] + second * weights[1]


def theta_edges(corona, kappa, first, second, sems):
    fields, tile_t = corona.shape[0], corona.shape[1]
    odd = parity("lat")
    copies = []
    for n, (out, start) in enumerate(
        ((first, (1 - odd) * (tile_t - 2)), (second, odd * (tile_t - 2)))
    ):
        rows = pl.ds(start, 2)
        copies.append(
            pltpu.make_async_copy(corona.at[:, rows], out.at[pl.ds(0, fields)], sems.at[2 * n])
        )
        copies.append(pltpu.make_async_copy(kappa.at[rows], out.at[fields], sems.at[2 * n + 1]))
    for copy in copies:
        copy.start()
    for copy in copies:
        copy.wait()


def phi_edges(tile_t, tile_p, corona, kappa, t_first, t_second, first, second):
    fields = corona.shape[0]
    odd = parity("lon")
    weights = sides("lat")
    for out, upper in ((first, 1 - odd), (second, odd)):
        near = upper * (tile_p - 1)
        far = upper * (tile_p - 3) + 1
        cell = pl.ds(near, 1)
        for f in range(fields + 1):
            for at, col in ((0, near), (tile_t, far)):
                rows = pl.ds(col, tile_t, stride=tile_p)
                out[f, at : at + tile_t, :] = corona[f, rows, :] if f < fields else kappa[rows, :]
            for a, row in ((0, 1), (1, 0)):
                out[f, 2 * tile_t + a : 2 * tile_t + a + 1, :] = blend(
                    weights[a], t_first[f, row, cell, :], t_second[f, row, cell, :]
                )


def ranks(face_t, owner, dest, rank_out, meta_out, hit_out):
    n_dev = meta_out.shape[0]
    count = owner.shape[1]
    width = min(BLOCK, count)
    before = (iota((width, width), 0) < iota((width, width), 1)).astype(F32).astype(BF16)
    owners = iota((n_dev, width), 0)
    slots = iota((CAP, width), 0).astype(F32)
    carry = jnp.zeros((n_dev, 1), F32)
    meta = jnp.zeros((n_dev, 128), F32)
    for b in range(count // width):
        cols = slice(b * width, (b + 1) * width)
        hit = owners == owner[:, cols]
        hit_f = jnp.where(hit, 1.0, 0.0)
        hit_b = hit_f.astype(BF16)
        hit_out[:, cols] = hit_b
        ahead = jnp.dot(hit_b, before, preferred_element_type=F32) + carry
        rank = jnp.sum(jnp.where(hit, ahead, 0.0), axis=0, keepdims=True)
        carry = ahead[:, width - 1 : width] + hit_f[:, width - 1 : width]
        rank_out[:, cols] = rank
        cell = dest[:, cols]
        cell_t = (cell % face_t).astype(F32)
        cell_p = (cell // face_t).astype(F32)
        mine = slots == rank
        rows = jnp.concatenate(
            [
                jnp.where(mine, cell_t, 0.0),
                jnp.where(mine, cell_p, 0.0),
                jnp.zeros((128 - 2 * CAP, width), F32),
            ],
            axis=0,
        ).astype(BF16)
        meta = meta + lax.dot_general(
            hit_b, rows, (((1,), (1,)), ((), ())), preferred_element_type=F32
        )
    meta_out[...] = meta


def tables(tile_t, tile_p, base, frac, high_out, low_out, radial_out):
    count = base.shape[1]
    width = min(BLOCK, count)
    for b in range(count // width):
        cols = slice(b * width, (b + 1) * width)
        corner = base[:, cols]

        def pair(size, at, fraction):
            rows = iota((size, width), 0)
            return jnp.where(rows == at, 1.0 - fraction, jnp.where(rows == at + 1, fraction, 0.0))

        w_t = pair(tile_t, corner // (tile_p * SH), frac[0:1, cols])
        w_p = pair(tile_p, (corner // SH) % tile_p, frac[1:2, cols])
        radial_out[:, cols] = pair(SH, corner % SH, frac[2:3, cols])
        table = (w_t[:, None, :] * w_p[None, :, :]).reshape(tile_t * tile_p, width)
        high_out[:, cols], low_out[:, cols] = halves(table)


def spread(mixing, spread_out):
    fields = mixing.shape[0]
    for g in range(fields):
        for f in range(fields):
            spread_out[g * fields + f] = jnp.full(spread_out.shape[1:], 0.3 * mixing[g, f], F32)


def flux(mix, conds, centres, near):
    kc, *kn = conds
    radial = kc.shape[-1]
    fields = len(centres)
    lane = iota(kc.shape, 1)
    weights = [0.075 * (kc + k) for k in kn]
    up = 0.075 * (kc + jnp.where(lane == radial - 1, 0.0, pltpu.roll(kc, radial - 1, 1)))
    down = 0.075 * (kc + jnp.where(lane == 0, 0.0, pltpu.roll(kc, 1, 1)))
    total = 1.0 - ((weights[0] + weights[1]) + (weights[2] + weights[3]) + (up + down))
    up = jnp.where(lane == radial - 1, 0.0, up)
    down = jnp.where(lane == 0, 0.0, down)
    for g in range(fields):
        c = centres[g]
        acc = total * c
        for w, beside in zip(weights, near(g)):
            acc = acc + w * beside
        acc = acc + up * pltpu.roll(c, radial - 1, 1) + down * pltpu.roll(c, 1, 1)
        for f in range(fields):
            m = mix[g * fields + f]
            acc = acc + jnp.concatenate([m] * (c.shape[0] // 8), axis=0) * centres[f]
        yield g, acc


WIDE = 32


def along_phi(ref, f, t, tile_p, dt=0, dp=0):
    at = (t + dt) * WIDE + 8 + dp
    if isinstance(t, jax.Array) and dp == 0:
        at = pl.multiple_of(at, 8)
    return ref[f, pl.ds(at, tile_p), :]


def along_theta(ref, f, t, p, count):
    return ref[f, pl.ds(t * WIDE + 8 + p, count, stride=WIDE), :]


AROUND = ((-1, 0), (1, 0), (0, -1), (0, 1))


def row_flux(mix, field, cond, t_field, t_cond, tile_p, fields):
    last = cond.shape[0] - 1
    return flux(
        mix,
        [along_phi(cond, last, t_cond, tile_p)]
        + [along_phi(cond, last, t_cond, tile_p, *d) for d in AROUND],
        [along_phi(field, f, t_field, tile_p) for f in range(fields)],
        lambda g: [along_phi(field, g, t_field, tile_p, *d) for d in AROUND],
    )


def column_flux(mix, field, cond, t_field, t_cond, p, count, fields):
    last = cond.shape[0] - 1
    return flux(
        mix,
        [along_theta(cond, last, t_cond, p, count)]
        + [along_theta(cond, last, t_cond + dt, p + dp, count) for dt, dp in AROUND],
        [along_theta(field, f, t_field, p, count) for f in range(fields)],
        lambda g: [along_theta(field, g, t_field + dt, p + dp, count) for dt, dp in AROUND],
    )


def main(
    n_dev, mixing, corona, kappa, t_first, t_second, p_first, p_second, rank, meta, hit, table_high,
    table_low, w_r, out, message, stepped, wide, once, mix, sem,
):
    fields, tile_t, tile_p, radial = corona.shape
    by_t, by_p = sides("lat"), sides("lon")
    has_t = [low + high for low, high in by_t]
    has_p = [low + high for low, high in by_p]
    spread(mixing, mix)
    for f in range(fields + 1):
        for t in range(tile_t):
            own = corona[f, t] if f < fields else kappa[t]
            wide[f, pl.ds((t + 2) * WIDE + 8, tile_p), :] = own
        for k in range(2):
            for side, t in enumerate((k, tile_t + 2 + k)):
                wide[f, pl.ds(t * WIDE + 8, tile_p), :] = blend(
                    by_t[side], t_first[f, k], t_second[f, k]
                )
        for side, (near, far) in enumerate(((7, 6), (8 + tile_p, 9 + tile_p))):
            for k, col in enumerate((near, far)):
                rows = slice(k * tile_t, (k + 1) * tile_t)
                cells = blend(by_p[side], p_first[f, rows, :], p_second[f, rows, :])
                wide[f, pl.ds(2 * WIDE + col, tile_t, stride=WIDE), :] = cells
            for a, t in enumerate((1, tile_t + 2)):
                row = slice(2 * tile_t + a, 2 * tile_t + a + 1)
                wide[f, pl.ds(t * WIDE + near, 1), :] = blend(
                    by_p[side], p_first[f, row, :], p_second[f, row, :]
                )

    def first(t):
        for g, acc in row_flux(mix, wide, wide, t + 2, t + 2, tile_p, fields):
            if isinstance(t, int) and t in (-1, tile_t):
                acc = acc * has_t[0 if t < 0 else 1]
            at = (t + 1) * WIDE + 8
            once[g, pl.ds(at if isinstance(t, int) else pl.multiple_of(at, 8), tile_p), :] = acc

    def second(t):
        for g, acc in row_flux(mix, once, wide, t + 1, t + 2, tile_p, fields):
            stepped[g, t] = acc

    first(-1)
    first(tile_t)
    for p in (-1, tile_p):
        for g, acc in column_flux(mix, wide, wide, 2, 2, p, tile_t, fields):
            once[g, pl.ds(WIDE + 8 + p, tile_t, stride=WIDE), :] = acc * has_p[0 if p < 0 else 1]
    for row in (first, second):
        by_rows(row, tile_t)

    copy = pltpu.make_async_copy(stepped, out, sem)
    copy.start()
    columns = tile_t * tile_p
    lane = iota((columns, radial), 1)
    rows = jnp.zeros((columns, radial), F32)
    for f in range(fields):
        moved = pltpu.roll(stepped[f].reshape(columns, radial), (f * SH + SH) % radial, 1)
        rows = jnp.where(lane // SH == f, moved, rows)
    high = rows.astype(BF16).astype(F32)
    both = high + pltpu.roll(rows - high, fields * SH, 1)
    left = jnp.transpose(both).astype(BF16)

    count = rank.shape[1]
    width = min(BLOCK, count)
    packed = jnp.zeros((n_dev, 2 * fields * CAP), F32)
    for b in range(count // width):
        cols = slice(b * width, (b + 1) * width)
        coarse = jnp.dot(left, table_high[:, cols], preferred_element_type=F32)
        fine = jnp.dot(left[: fields * SH], table_low[:, cols], preferred_element_type=F32)
        by_layer = coarse[: fields * SH] + (coarse[fields * SH :] + fine)
        value = jnp.sum(by_layer.reshape(fields, SH, width) * w_r[:, cols][None], axis=1)
        order = rank[:, cols]
        placed = jnp.concatenate(
            [jnp.where(order == float(k), value, 0.0) for k in range(CAP)], axis=0
        )
        placed_high, placed_low = halves(placed)
        packed = packed + lax.dot_general(
            hit[:, cols],
            jnp.concatenate([placed_high, placed_low], axis=0),
            (((1,), (1,)), ((), ())),
            preferred_element_type=F32,
        )
    half = fields * CAP
    message[pl.ds(0, n_dev, stride=2), :] = packed[:, :half] + packed[:, half:]
    message[pl.ds(1, n_dev, stride=2), :] = meta[...]
    copy.wait()


def by_rows(row, count):
    if UNROLL >= count:
        for t in range(count):
            row(t)
        return

    def some(i, carry):
        for k in range(UNROLL):
            row(i * UNROLL + k)
        return carry

    lax.fori_loop(0, count // UNROLL, some, 0)


def land(n_dev, got, prev, coupled, p_first, p_second, t_first, t_second):
    fields, face_p, face_t = prev.shape
    values = jnp.transpose(got[pl.ds(0, n_dev, stride=2), :])
    cells = jnp.transpose(got[pl.ds(1, n_dev, stride=2), :])
    along_t = iota((face_t, n_dev), 0).astype(F32)
    along_p = iota((face_p, n_dev), 0).astype(F32)
    rows = fields * face_p
    total = jnp.zeros((2 * rows, face_t), F32)
    for k in range(CAP):
        at_t = jnp.where(along_t == cells[k : k + 1, :], 1.0, 0.0).astype(BF16)
        at_p = along_p == cells[CAP + k : CAP + k + 1, :]
        value = values[k * fields : (k + 1) * fields, :]
        high = value.astype(BF16).astype(F32)
        parts = [
            jnp.where(at_p[None], part[:, None, :], 0.0).reshape(rows, n_dev).astype(BF16)
            for part in (high, value - high)
        ]
        total = total + lax.dot_general(
            jnp.concatenate(parts, axis=0),
            at_t,
            (((1,), (1,)), ((), ())),
            preferred_element_type=F32,
        )
    new = prev[...].reshape(rows, face_t) + (total[:rows] + total[rows:])

    def edge(face, p):
        at = [f * face_p + p for f in range(fields)]
        return jnp.concatenate([face[k : k + 1, :] for k in at], axis=0)

    coupled[...] = new.reshape(fields, face_p, face_t)
    turned = jnp.transpose(new)
    for axis, low, high, first, second in (
        ("lat", turned[0:1, :], turned[face_t - 1 : face_t, :], t_first, t_second),
        ("lon", edge(new, 0), edge(new, face_p - 1), p_first, p_second),
    ):
        odd = parity(axis).astype(F32)
        first[...] = blend((odd, 1.0 - odd), low, high)
        second[...] = blend((1.0 - odd, odd), low, high)


def smooth(coupled, p_first, p_second, t_first, t_second, out):
    fields, face_p, face_t = coupled.shape
    x = coupled[...]
    row = iota((face_p, face_t), 0)[None]
    lane = iota((face_p, face_t), 1)[None]

    t_low, t_high = [blend(w, t_first[...], t_second[...]) for w in sides("lat")]
    p_low, p_high = [blend(w, p_first[...], p_second[...]) for w in sides("lon")]

    def column(edge):
        return jnp.transpose(jnp.broadcast_to(edge, (face_t, fields * face_p))).reshape(x.shape)

    below = jnp.where(row == 0, p_low[:, None, :], pltpu.roll(x, 1, 1))
    above = jnp.where(row == face_p - 1, p_high[:, None, :], pltpu.roll(x, face_p - 1, 1))
    left = jnp.where(lane == 0, column(t_low), pltpu.roll(x, 1, 2))
    right = jnp.where(lane == face_t - 1, column(t_high), pltpu.roll(x, face_t - 1, 2))
    out[...] = x + 0.2 * (above + below + right + left - 4.0 * x)


def call(kernel, outs, specs, name, scratch=(), out_specs=None, room=40 * 1024 * 1024):
    outs = [s if isinstance(s, jax.ShapeDtypeStruct) else jax.ShapeDtypeStruct(s, F32) for s in outs]
    return pl.pallas_call(
        kernel,
        out_shape=outs,
        in_specs=specs,
        out_specs=out_specs or [vspec()] * len(outs),
        scratch_shapes=list(scratch),
        name=name,
        compiler_params=pltpu.CompilerParams(vmem_limit_bytes=room),
    )


def body(corona, kappa, mixing, helio_prev, owner, dest_cell, corner_base, fractions):
    fields, tile_t, tile_p, radial = corona.shape
    n_lat, n_lon = lax.axis_size("lat"), lax.axis_size("lon")
    n_dev = n_lat * n_lon
    count = corner_base.shape[0]
    _, face_p, face_t = helio_prev.shape
    owner = owner.reshape(1, count)
    dest_cell = dest_cell.reshape(1, count)
    base = corner_base.reshape(1, count)
    edge = (fields + 1, 2, tile_p, radial)
    first, second = call(
        theta_edges,
        [edge] * 2,
        [pl.BlockSpec(memory_space=pltpu.HBM)] * 2,
        "theta_edges",
        [pltpu.SemaphoreType.DMA((4,))],
        room=58 * 1024 * 1024,
    )(corona, kappa)
    t_first, t_second = swapped(first, second, "lat")

    rank, meta, hit = call(
        functools.partial(ranks, face_t),
        [(1, count), (n_dev, 128), jax.ShapeDtypeStruct((n_dev, count), BF16)],
        [vspec()] * 2,
        "ranks",
    )(owner, dest_cell)
    t_first, t_second, rank = lax.optimization_barrier((t_first, t_second, rank))

    edge = (fields + 1, 2 * tile_t + 8, radial)
    first, second = call(
        functools.partial(phi_edges, tile_t, tile_p), [edge] * 2, [vspec()] * 4, "phi_edges"
    )(
        corona.reshape(fields, tile_t * tile_p, radial),
        kappa.reshape(tile_t * tile_p, radial),
        t_first,
        t_second,
    )
    p_first, p_second = swapped(first, second, "lon")

    table = jax.ShapeDtypeStruct((tile_t * tile_p, count), BF16)
    table_high, table_low, w_r = call(
        functools.partial(tables, tile_t, tile_p),
        [table, table, (SH, count)],
        [vspec()] * 2,
        "tables",
    )(base, fractions)

    stepped, message = call(
        functools.partial(main, n_dev),
        [corona.shape, (2 * n_dev, 128)],
        [sspec()] + [vspec()] * 12,
        "main",
        [
            VMEM(corona.shape, F32),
            VMEM((fields + 1, (tile_t + 4) * WIDE, radial), F32),
            VMEM((fields, (tile_t + 2) * WIDE, radial), F32),
            VMEM((fields * fields, 8, radial), F32),
            pltpu.SemaphoreType.DMA,
        ],
        [pl.BlockSpec(memory_space=pltpu.HBM), vspec()],
    )(
        mixing, corona, kappa, t_first, t_second, p_first, p_second, rank, meta, hit, table_high,
        table_low, w_r,
    )

    got = lax.all_to_all(message, ("lat", "lon"), split_axis=0, concat_axis=0, tiled=True)

    coupled, p_first, p_second, t_first, t_second = call(
        functools.partial(land, n_dev),
        [helio_prev.shape, (fields, face_t), (fields, face_t)] + [(1, fields * face_p)] * 2,
        [vspec()] * 2,
        "land",
    )(got, helio_prev)
    p_first, p_second = swapped(p_first, p_second, "lon")
    t_first, t_second = swapped(t_first, t_second, "lat")
    (face,) = call(smooth, [helio_prev.shape], [vspec()] * 5, "smooth")(
        coupled, p_first, p_second, t_first, t_second
    )
    return (stepped, face)


def solution(mesh):
    return jax.shard_map(
        body,
        mesh=mesh,
        in_specs=(
            P(None, "lat", "lon", None),
            P("lat", "lon", None),
            P(),
            P(None, "lon", "lat"),
            P(("lat", "lon"), None),
            P(("lat", "lon")),
            P(("lat", "lon")),
            P(None, ("lat", "lon")),
        ),
        out_specs=(P(None, "lat", "lon", None), P(None, "lon", "lat")),
        check_vma=False,
    )
```

```python
import functools

import jax
import jax.numpy as jnp
from jax import lax
from jax.experimental import pallas as pl
from jax.experimental.pallas import tpu as pltpu
from jax.sharding import PartitionSpec as P

SH = 8
CAP = 16
BLOCK = 256
UNROLL = 16
VMEM = pltpu.VMEM
F32 = jnp.float32
BF16 = jnp.bfloat16


def vspec():
    return pl.BlockSpec(memory_space=VMEM)


def sspec():
    return pl.BlockSpec(memory_space=pltpu.SMEM)


def iota(shape, dim):
    return lax.broadcasted_iota(jnp.int32, shape, dim)


def halves(x):
    high = x.astype(BF16)
    return high, (x - high.astype(F32)).astype(BF16)


def swapped(first, second, axis):
    count = lax.axis_size(axis)
    other = [(i + (1 if i % 2 else -1)) % count for i in range(count)]
    return (
        lax.ppermute(first, axis, [(i, i ^ 1) for i in range(count)]),
        lax.ppermute(second, axis, list(enumerate(other))),
    )


def parity(axis):
    return lax.rem(lax.axis_index(axis), 2)


def sides(axis):
    at, count = lax.axis_index(axis), lax.axis_size(axis)
    odd = parity(axis).astype(F32)
    low = jnp.where(at > 0, 1.0, 0.0)
    high = jnp.where(at < count - 1, 1.0, 0.0)
    return (odd * low, (1.0 - odd) * low), ((1.0 - odd) * high, odd * high)


def blend(weights, first, second):
    return first * weights[0] + second * weights[1]


def theta_edges(corona, kappa, first, second, sems):
    fields, tile_t = corona.shape[0], corona.shape[1]
    odd = parity("lat")
    copies = []
    for n, (out, start) in enumerate(
        ((first, (1 - odd) * (tile_t - 2)), (second, odd * (tile_t - 2)))
    ):
        rows = pl.ds(start, 2)
        copies.append(
            pltpu.make_async_copy(corona.at[:, rows], out.at[pl.ds(0, fields)], sems.at[2 * n])
        )
        copies.append(pltpu.make_async_copy(kappa.at[rows], out.at[fields], sems.at[2 * n + 1]))
    for copy in copies:
        copy.start()
    for copy in copies:
        copy.wait()


def phi_edges(tile_t, tile_p, corona, kappa, first, second):
    fields = corona.shape[0]
    odd = parity("lon")
    for out, upper in ((first, 1 - odd), (second, odd)):
        near = upper * (tile_p - 1)
        far = upper * (tile_p - 3) + 1
        for f in range(fields + 1):
            for at, col in ((0, near), (tile_t, far)):
                rows = pl.ds(col, tile_t, stride=tile_p)
                out[f, at : at + tile_t, :] = corona[f, rows, :] if f < fields else kappa[rows, :]


def corner_cells(t_first, t_second, low, high, first, second):
    count, _, tile_p, _ = t_first.shape
    weights = sides("lat")
    for a, row in ((0, 1), (1, 0)):
        for f in range(count):
            for out, col in ((low, 0), (high, tile_p - 1)):
                cell = slice(col, col + 1)
                out[a, f : f + 1, :] = blend(
                    weights[a], t_first[f, row, cell, :], t_second[f, row, cell, :]
                )
    odd = parity("lon").astype(F32)
    first[...] = blend((odd, 1.0 - odd), low[...], high[...])
    second[...] = blend((1.0 - odd, odd), low[...], high[...])


def plan(
    face_t, tile_t, tile_p, owner, dest, base, frac, rank_out, meta_out, hit_out, high_out, low_out,
    radial_out,
):
    n_dev = meta_out.shape[0]
    count = owner.shape[1]
    width = min(BLOCK, count)
    before = (iota((width, width), 0) < iota((width, width), 1)).astype(F32).astype(BF16)
    owners = iota((n_dev, width), 0)
    slots = iota((CAP, width), 0).astype(F32)
    carry = jnp.zeros((n_dev, 1), F32)
    meta = jnp.zeros((n_dev, 128), F32)
    for b in range(count // width):
        cols = slice(b * width, (b + 1) * width)
        hit = owners == owner[:, cols]
        hit_f = jnp.where(hit, 1.0, 0.0)
        hit_b = hit_f.astype(BF16)
        hit_out[:, cols] = hit_b
        ahead = jnp.dot(hit_b, before, preferred_element_type=F32) + carry
        rank = jnp.sum(jnp.where(hit, ahead, 0.0), axis=0, keepdims=True)
        carry = ahead[:, width - 1 : width] + hit_f[:, width - 1 : width]
        rank_out[:, cols] = rank
        cell = dest[:, cols]
        cell_t = (cell % face_t).astype(F32)
        cell_p = (cell // face_t).astype(F32)
        mine = slots == rank
        rows = jnp.concatenate(
            [
                jnp.where(mine, cell_t, 0.0),
                jnp.where(mine, cell_p, 0.0),
                jnp.zeros((128 - 2 * CAP, width), F32),
            ],
            axis=0,
        ).astype(BF16)
        meta = meta + lax.dot_general(
            hit_b, rows, (((1,), (1,)), ((), ())), preferred_element_type=F32
        )
        corner = base[:, cols]

        def pair(size, at, fraction):
            rows = iota((size, width), 0)
            return jnp.where(rows == at, 1.0 - fraction, jnp.where(rows == at + 1, fraction, 0.0))

        w_t = pair(tile_t, corner // (tile_p * SH), frac[0:1, cols])
        w_p = pair(tile_p, (corner // SH) % tile_p, frac[1:2, cols])
        radial_out[:, cols] = pair(SH, corner % SH, frac[2:3, cols])
        table = (w_t[:, None, :] * w_p[None, :, :]).reshape(tile_t * tile_p, width)
        high_out[:, cols], low_out[:, cols] = halves(table)
    meta_out[...] = meta


def spread(mixing, spread_out):
    fields = mixing.shape[0]
    for g in range(fields):
        for f in range(fields):
            spread_out[g * fields + f] = jnp.full(spread_out.shape[1:], 0.3 * mixing[g, f], F32)


def flux(mix, conds, centres, near):
    kc, *kn = conds
    radial = kc.shape[-1]
    fields = len(centres)
    lane = iota(kc.shape, 1)
    weights = [0.075 * (kc + k) for k in kn]
    up = 0.075 * (kc + jnp.where(lane == radial - 1, 0.0, pltpu.roll(kc, radial - 1, 1)))
    down = 0.075 * (kc + jnp.where(lane == 0, 0.0, pltpu.roll(kc, 1, 1)))
    total = 1.0 - ((weights[0] + weights[1]) + (weights[2] + weights[3]) + (up + down))
    up = jnp.where(lane == radial - 1, 0.0, up)
    down = jnp.where(lane == 0, 0.0, down)
    for g in range(fields):
        c = centres[g]
        acc = total * c
        for w, beside in zip(weights, near(g)):
            acc = acc + w * beside
        acc = acc + up * pltpu.roll(c, radial - 1, 1) + down * pltpu.roll(c, 1, 1)
        for f in range(fields):
            m = mix[g * fields + f]
            acc = acc + jnp.concatenate([m] * (c.shape[0] // 8), axis=0) * centres[f]
        yield g, acc


WIDE = 32


def along_phi(ref, f, t, tile_p, dt=0, dp=0):
    at = (t + dt) * WIDE + 8 + dp
    if isinstance(t, jax.Array) and dp == 0:
        at = pl.multiple_of(at, 8)
    return ref[f, pl.ds(at, tile_p), :]


def along_theta(ref, f, t, p, count):
    return ref[f, pl.ds(t * WIDE + 8 + p, count, stride=WIDE), :]


AROUND = ((-1, 0), (1, 0), (0, -1), (0, 1))


def row_flux(mix, field, cond, t_field, t_cond, tile_p, fields):
    last = cond.shape[0] - 1
    return flux(
        mix,
        [along_phi(cond, last, t_cond, tile_p)]
        + [along_phi(cond, last, t_cond, tile_p, *d) for d in AROUND],
        [along_phi(field, f, t_field, tile_p) for f in range(fields)],
        lambda g: [along_phi(field, g, t_field, tile_p, *d) for d in AROUND],
    )


def column_flux(mix, field, cond, t_field, t_cond, p, count, fields):
    last = cond.shape[0] - 1
    return flux(
        mix,
        [along_theta(cond, last, t_cond, p, count)]
        + [along_theta(cond, last, t_cond + dt, p + dp, count) for dt, dp in AROUND],
        [along_theta(field, f, t_field, p, count) for f in range(fields)],
        lambda g: [along_theta(field, g, t_field + dt, p + dp, count) for dt, dp in AROUND],
    )


def steps(
    mixing, corona, kappa, t_first, t_second, p_first, p_second, stepped, wide, once, mix,
):
    fields, tile_t, tile_p, radial = corona.shape
    by_t, by_p = sides("lat"), sides("lon")
    has_t = [low + high for low, high in by_t]
    has_p = [low + high for low, high in by_p]
    spread(mixing, mix)
    nothing = jnp.zeros((1, radial), F32)
    for f in range(fields + 1):
        for t in range(tile_t):
            own = corona[f, t] if f < fields else kappa[t]
            wide[f, pl.ds((t + 2) * WIDE + 8, tile_p), :] = own
        for k in range(2):
            for side, t in enumerate((k, tile_t + 2 + k)):
                wide[f, pl.ds(t * WIDE + 8, tile_p), :] = blend(
                    by_t[side], t_first[f, k], t_second[f, k]
                )
        for side, (near, far) in enumerate(((7, 6), (8 + tile_p, 9 + tile_p))):
            for k, col in enumerate((near, far)):
                rows = slice(k * tile_t, (k + 1) * tile_t)
                cells = blend(by_p[side], p_first[f, rows, :], p_second[f, rows, :])
                wide[f, pl.ds(2 * WIDE + col, tile_t, stride=WIDE), :] = cells
            for t in (1, tile_t + 2):
                wide[f, pl.ds(t * WIDE + near, 1), :] = nothing

    def first(t):
        for g, acc in row_flux(mix, wide, wide, t + 2, t + 2, tile_p, fields):
            if isinstance(t, int) and t in (-1, tile_t):
                acc = acc * has_t[0 if t < 0 else 1]
            at = (t + 1) * WIDE + 8
            once[g, pl.ds(at if isinstance(t, int) else pl.multiple_of(at, 8), tile_p), :] = acc

    def second(t):
        for g, acc in row_flux(mix, once, wide, t + 1, t + 2, tile_p, fields):
            stepped[g, t] = acc

    first(-1)
    first(tile_t)
    for p in (-1, tile_p):
        for g, acc in column_flux(mix, wide, wide, 2, 2, p, tile_t, fields):
            once[g, pl.ds(WIDE + 8 + p, tile_t, stride=WIDE), :] = acc * has_p[0 if p < 0 else 1]
    for row in (first, second):
        by_rows(row, tile_t)


def by_rows(row, count):
    if UNROLL >= count:
        for t in range(count):
            row(t)
        return

    def some(i, carry):
        for k in range(UNROLL):
            row(i * UNROLL + k)
        return carry

    lax.fori_loop(0, count // UNROLL, some, 0)


def route(
    n_dev, kappa, p_first, p_second, own_low, own_high, c_first, c_second, stepped, rank, meta, hit,
    table_high, table_low, w_r, out, message, shell, tiles, sems,
):
    fields, columns, radial = stepped.shape
    tile_t, tile_p, _ = kappa.shape
    sides_p = sides("lon")
    whole = pltpu.make_async_copy(stepped, out, sems.at[4])
    whole.start()
    corrections = []
    lane = iota((columns, radial), 1)
    rows = jnp.zeros((columns, radial), F32)
    for f in range(fields):
        moved = pltpu.roll(stepped[f], (f * SH + SH) % radial, 1)
        rows = jnp.where(lane // SH == f, moved, rows)
    shell[...] = rows
    for a in range(2):
        for b, own in enumerate((own_low, own_high)):
            t, p = a * (tile_t - 1), b * (tile_p - 1)

            def beside(f, t=t, weights=sides_p[b]):
                return blend(weights, p_first[f, t : t + 1, :], p_second[f, t : t + 1, :])

            k_t, u_t = own[a, fields : fields + 1], own[a, 0:fields]
            k_p = beside(fields)
            u_p = jnp.concatenate([beside(f) for f in range(fields)], axis=0)
            diagonal = blend(sides_p[b], c_first[a], c_second[a])
            k_d, u_d = diagonal[fields : fields + 1], diagonal[0:fields]
            k = kappa[t, p : p + 1, :]
            by_t = 0.075 * ((k_t + k_d) * u_d - k_d * u_t)
            by_p = 0.075 * ((k_p + k_d) * u_d - k_d * u_p)
            extra = 0.075 * ((k + k_t) * by_t + (k + k_p) * by_p)
            n, start = 2 * a + b, t * tile_p + b * (tile_p - 8)
            within = p % 8
            for f in range(fields):
                tiles[n, f] = stepped[f, start : start + 8, :]
                tiles[n, f, within : within + 1, :] = (
                    stepped[f, start + within : start + within + 1, :] + extra[f : f + 1]
                )
            corrections.append(
                pltpu.make_async_copy(tiles.at[n], out.at[:, pl.ds(start, 8)], sems.at[n])
            )
            row = jnp.zeros((1, radial), F32)
            for f in range(fields):
                moved = pltpu.roll(extra[f : f + 1], (f * SH + SH) % radial, 1)
                row = jnp.where(lane[0:1] // SH == f, moved, row)
            at = t * tile_p + p
            shell[at : at + 1, :] = shell[at : at + 1, :] + row
    rows = shell[...]
    high = rows.astype(BF16).astype(F32)
    both = high + pltpu.roll(rows - high, fields * SH, 1)
    left = jnp.transpose(both).astype(BF16)

    count = rank.shape[1]
    width = min(BLOCK, count)
    packed = jnp.zeros((n_dev, 2 * fields * CAP), F32)
    for b in range(count // width):
        if b == count // width // 2:
            whole.wait()
            for copy in corrections:
                copy.start()
        cols = slice(b * width, (b + 1) * width)
        coarse = jnp.dot(left, table_high[:, cols], preferred_element_type=F32)
        fine = jnp.dot(left[: fields * SH], table_low[:, cols], preferred_element_type=F32)
        by_layer = coarse[: fields * SH] + (coarse[fields * SH :] + fine)
        value = jnp.sum(by_layer.reshape(fields, SH, width) * w_r[:, cols][None], axis=1)
        order = rank[:, cols]
        placed = jnp.concatenate(
            [jnp.where(order == float(k), value, 0.0) for k in range(CAP)], axis=0
        )
        placed_high, placed_low = halves(placed)
        packed = packed + lax.dot_general(
            hit[:, cols],
            jnp.concatenate([placed_high, placed_low], axis=0),
            (((1,), (1,)), ((), ())),
            preferred_element_type=F32,
        )
    half = fields * CAP
    message[pl.ds(0, n_dev, stride=2), :] = packed[:, :half] + packed[:, half:]
    message[pl.ds(1, n_dev, stride=2), :] = meta[...]
    for copy in corrections:
        copy.wait()


def land(n_dev, got, prev, coupled, p_first, p_second, t_first, t_second):
    fields, face_p, face_t = prev.shape
    values = jnp.transpose(got[pl.ds(0, n_dev, stride=2), :])
    cells = jnp.transpose(got[pl.ds(1, n_dev, stride=2), :])
    along_t = iota((face_t, n_dev), 0).astype(F32)
    along_p = iota((face_p, n_dev), 0).astype(F32)
    rows = fields * face_p
    total = jnp.zeros((2 * rows, face_t), F32)
    for k in range(CAP):
        at_t = jnp.where(along_t == cells[k : k + 1, :], 1.0, 0.0).astype(BF16)
        at_p = along_p == cells[CAP + k : CAP + k + 1, :]
        value = values[k * fields : (k + 1) * fields, :]
        high = value.astype(BF16).astype(F32)
        parts = [
            jnp.where(at_p[None], part[:, None, :], 0.0).reshape(rows, n_dev).astype(BF16)
            for part in (high, value - high)
        ]
        total = total + lax.dot_general(
            jnp.concatenate(parts, axis=0),
            at_t,
            (((1,), (1,)), ((), ())),
            preferred_element_type=F32,
        )
    new = prev[...].reshape(rows, face_t) + (total[:rows] + total[rows:])

    def edge(face, p):
        at = [f * face_p + p for f in range(fields)]
        return jnp.concatenate([face[k : k + 1, :] for k in at], axis=0)

    coupled[...] = new.reshape(fields, face_p, face_t)
    turned = jnp.transpose(new)
    for axis, low, high, first, second in (
        ("lat", turned[0:1, :], turned[face_t - 1 : face_t, :], t_first, t_second),
        ("lon", edge(new, 0), edge(new, face_p - 1), p_first, p_second),
    ):
        odd = parity(axis).astype(F32)
        first[...] = blend((odd, 1.0 - odd), low, high)
        second[...] = blend((1.0 - odd, odd), low, high)


def smooth(coupled, p_first, p_second, t_first, t_second, out):
    fields, face_p, face_t = coupled.shape
    x = coupled[...]
    row = iota((face_p, face_t), 0)[None]
    lane = iota((face_p, face_t), 1)[None]

    t_low, t_high = [blend(w, t_first[...], t_second[...]) for w in sides("lat")]
    p_low, p_high = [blend(w, p_first[...], p_second[...]) for w in sides("lon")]

    def column(edge):
        return jnp.transpose(jnp.broadcast_to(edge, (face_t, fields * face_p))).reshape(x.shape)

    below = jnp.where(row == 0, p_low[:, None, :], pltpu.roll(x, 1, 1))
    above = jnp.where(row == face_p - 1, p_high[:, None, :], pltpu.roll(x, face_p - 1, 1))
    left = jnp.where(lane == 0, column(t_low), pltpu.roll(x, 1, 2))
    right = jnp.where(lane == face_t - 1, column(t_high), pltpu.roll(x, face_t - 1, 2))
    out[...] = x + 0.2 * (above + below + right + left - 4.0 * x)


def call(kernel, outs, specs, name, scratch=(), out_specs=None, room=40 * 1024 * 1024):
    outs = [s if isinstance(s, jax.ShapeDtypeStruct) else jax.ShapeDtypeStruct(s, F32) for s in outs]
    return pl.pallas_call(
        kernel,
        out_shape=outs,
        in_specs=specs,
        out_specs=out_specs or [vspec()] * len(outs),
        scratch_shapes=list(scratch),
        name=name,
        compiler_params=pltpu.CompilerParams(vmem_limit_bytes=room),
    )


def body(corona, kappa, mixing, helio_prev, owner, dest_cell, corner_base, fractions):
    fields, tile_t, tile_p, radial = corona.shape
    n_lat, n_lon = lax.axis_size("lat"), lax.axis_size("lon")
    n_dev = n_lat * n_lon
    count = corner_base.shape[0]
    _, face_p, face_t = helio_prev.shape
    owner = owner.reshape(1, count)
    dest_cell = dest_cell.reshape(1, count)
    base = corner_base.reshape(1, count)
    edge = (fields + 1, 2, tile_p, radial)
    first, second = call(
        theta_edges,
        [edge] * 2,
        [pl.BlockSpec(memory_space=pltpu.HBM)] * 2,
        "theta_edges",
        [pltpu.SemaphoreType.DMA((4,))],
        room=58 * 1024 * 1024,
    )(corona, kappa)
    t_first, t_second = swapped(first, second, "lat")

    edge = (fields + 1, 2 * tile_t, radial)
    first, second = call(
        functools.partial(phi_edges, tile_t, tile_p), [edge] * 2, [vspec()] * 2, "phi_edges"
    )(corona.reshape(fields, tile_t * tile_p, radial), kappa.reshape(tile_t * tile_p, radial))
    p_first, p_second = swapped(first, second, "lon")

    table = jax.ShapeDtypeStruct((tile_t * tile_p, count), BF16)
    rank, meta, hit, table_high, table_low, w_r = call(
        functools.partial(plan, face_t, tile_t, tile_p),
        [(1, count), (n_dev, 128), jax.ShapeDtypeStruct((n_dev, count), BF16), table, table]
        + [(SH, count)],
        [vspec()] * 4,
        "plan",
    )(owner, dest_cell, base, fractions)

    t_first, t_second, rank = lax.optimization_barrier((t_first, t_second, rank))
    own_low, own_high, first, second = call(
        corner_cells, [(2, fields + 1, radial)] * 4, [vspec()] * 2, "corner_cells"
    )(t_first, t_second)
    c_first, c_second = swapped(first, second, "lon")

    flat = (fields, tile_t * tile_p, radial)
    (almost,) = call(
        steps,
        [corona.shape],
        [sspec()] + [vspec()] * 6,
        "steps",
        [
            VMEM((fields + 1, (tile_t + 4) * WIDE, radial), F32),
            VMEM((fields, (tile_t + 2) * WIDE, radial), F32),
            VMEM((fields * fields, 8, radial), F32),
        ],
    )(mixing, corona, kappa, t_first, t_second, p_first, p_second)
    almost = almost.reshape(flat)

    stepped, message = call(
        functools.partial(route, n_dev),
        [flat, (2 * n_dev, 128)],
        [vspec()] * 14,
        "route",
        [
            VMEM((tile_t * tile_p, radial), F32),
            VMEM((4, fields, 8, radial), F32),
            pltpu.SemaphoreType.DMA((5,)),
        ],
        [pl.BlockSpec(memory_space=pltpu.HBM), vspec()],
    )(
        kappa, p_first, p_second, own_low, own_high, c_first, c_second, almost, rank, meta, hit,
        table_high, table_low, w_r,
    )
    got = lax.all_to_all(message, ("lat", "lon"), split_axis=0, concat_axis=0, tiled=True)

    coupled, p_first, p_second, t_first, t_second = call(
        functools.partial(land, n_dev),
        [helio_prev.shape, (fields, face_t), (fields, face_t)] + [(1, fields * face_p)] * 2,
        [vspec()] * 2,
        "land",
    )(got, helio_prev)
    p_first, p_second = swapped(p_first, p_second, "lon")
    t_first, t_second = swapped(t_first, t_second, "lat")
    (face,) = call(smooth, [helio_prev.shape], [vspec()] * 5, "smooth")(
        coupled, p_first, p_second, t_first, t_second
    )
    return (stepped.reshape(corona.shape), face)


def solution(mesh):
    return jax.shard_map(
        body,
        mesh=mesh,
        in_specs=(
            P(None, "lat", "lon", None),
            P("lat", "lon", None),
            P(),
            P(None, "lon", "lat"),
            P(("lat", "lon"), None),
            P(("lat", "lon")),
            P(("lat", "lon")),
            P(None, ("lat", "lon")),
        ),
        out_specs=(P(None, "lat", "lon", None), P(None, "lon", "lat")),
        check_vma=False,
    )
```

```python
import functools

import jax
import jax.numpy as jnp
from jax import lax
from jax.experimental import pallas as pl
from jax.experimental.pallas import tpu as pltpu
from jax.sharding import PartitionSpec as P

SH = 8
CAP = 16
BLOCK = 256
UNROLL = 16
VMEM = pltpu.VMEM
F32 = jnp.float32
BF16 = jnp.bfloat16


def vspec():
    return pl.BlockSpec(memory_space=VMEM)


def sspec():
    return pl.BlockSpec(memory_space=pltpu.SMEM)


def iota(shape, dim):
    return lax.broadcasted_iota(jnp.int32, shape, dim)


def halves(x):
    high = x.astype(BF16)
    return high, (x - high.astype(F32)).astype(BF16)


def swapped(first, second, axis):
    count = lax.axis_size(axis)
    other = [(i + (1 if i % 2 else -1)) % count for i in range(count)]
    second = lax.ppermute(second, axis, list(enumerate(other)))
    return lax.ppermute(first, axis, [(i, i ^ 1) for i in range(count)]), second


def parity(axis):
    return lax.rem(lax.axis_index(axis), 2)


def sides(axis):
    at, count = lax.axis_index(axis), lax.axis_size(axis)
    odd = parity(axis).astype(F32)
    low = jnp.where(at > 0, 1.0, 0.0)
    high = jnp.where(at < count - 1, 1.0, 0.0)
    return (odd * low, (1.0 - odd) * low), ((1.0 - odd) * high, odd * high)


def blend(weights, first, second):
    return first * weights[0] + second * weights[1]


def theta_edges(corona, kappa, first, second, sems):
    fields, tile_t = corona.shape[0], corona.shape[1]
    odd = parity("lat")
    copies = []
    for n, (out, start) in enumerate(
        ((first, (1 - odd) * (tile_t - 2)), (second, odd * (tile_t - 2)))
    ):
        rows = pl.ds(start, 2)
        copies.append(
            pltpu.make_async_copy(corona.at[:, rows], out.at[pl.ds(0, fields)], sems.at[2 * n])
        )
        copies.append(pltpu.make_async_copy(kappa.at[rows], out.at[fields], sems.at[2 * n + 1]))
    for copy in copies:
        copy.start()
    for copy in copies:
        copy.wait()


def phi_edges(tile_t, tile_p, corona, kappa, first, second):
    fields = corona.shape[0]
    odd = parity("lon")
    for out, upper in ((first, 1 - odd), (second, odd)):
        near = upper * (tile_p - 1)
        far = upper * (tile_p - 3) + 1
        for f in range(fields + 1):
            for at, col in ((0, near), (tile_t, far)):
                rows = pl.ds(col, tile_t, stride=tile_p)
                out[f, at : at + tile_t, :] = corona[f, rows, :] if f < fields else kappa[rows, :]


def corner_cells(t_first, t_second, low, high, first, second):
    count, _, tile_p, _ = t_first.shape
    weights = sides("lat")
    for a, row in ((0, 1), (1, 0)):
        for f in range(count):
            for out, col in ((low, 0), (high, tile_p - 1)):
                cell = slice(col, col + 1)
                out[a, f : f + 1, :] = blend(
                    weights[a], t_first[f, row, cell, :], t_second[f, row, cell, :]
                )
    odd = parity("lon").astype(F32)
    first[...] = blend((odd, 1.0 - odd), low[...], high[...])
    second[...] = blend((1.0 - odd, odd), low[...], high[...])


def plan(
    face_t, tile_t, tile_p, owner, dest, base, frac, rank_out, meta_out, hit_out, high_out, low_out,
    radial_out,
):
    n_dev = meta_out.shape[0]
    count = owner.shape[1]
    width = min(BLOCK, count)
    before = (iota((width, width), 0) < iota((width, width), 1)).astype(F32).astype(BF16)
    owners = iota((n_dev, width), 0)
    slots = iota((CAP, width), 0).astype(F32)
    carry = jnp.zeros((n_dev, 1), F32)
    meta = jnp.zeros((n_dev, 128), F32)
    for b in range(count // width):
        cols = slice(b * width, (b + 1) * width)
        hit = owners == owner[:, cols]
        hit_f = jnp.where(hit, 1.0, 0.0)
        hit_b = hit_f.astype(BF16)
        hit_out[:, cols] = hit_b
        ahead = jnp.dot(hit_b, before, preferred_element_type=F32) + carry
        rank = jnp.sum(jnp.where(hit, ahead, 0.0), axis=0, keepdims=True)
        carry = ahead[:, width - 1 : width] + hit_f[:, width - 1 : width]
        rank_out[:, cols] = rank
        cell = dest[:, cols]
        cell_t = (cell % face_t).astype(F32)
        cell_p = (cell // face_t).astype(F32)
        mine = slots == rank
        rows = jnp.concatenate(
            [
                jnp.where(mine, cell_t, 0.0),
                jnp.where(mine, cell_p, 0.0),
                jnp.zeros((128 - 2 * CAP, width), F32),
            ],
            axis=0,
        ).astype(BF16)
        meta = meta + lax.dot_general(
            hit_b, rows, (((1,), (1,)), ((), ())), preferred_element_type=F32
        )
        corner = base[:, cols]

        def pair(size, at, fraction):
            rows = iota((size, width), 0)
            return jnp.where(rows == at, 1.0 - fraction, jnp.where(rows == at + 1, fraction, 0.0))

        w_t = pair(tile_t, corner // (tile_p * SH), frac[0:1, cols])
        w_p = pair(tile_p, (corner // SH) % tile_p, frac[1:2, cols])
        radial_out[:, cols] = pair(SH, corner % SH, frac[2:3, cols])
        table = (w_t[:, None, :] * w_p[None, :, :]).reshape(tile_t * tile_p, width)
        high_out[:, cols], low_out[:, cols] = halves(table)
    meta_out[...] = meta


def spread(mixing, spread_out):
    fields = mixing.shape[0]
    for g in range(fields):
        for f in range(fields):
            spread_out[g * fields + f] = jnp.full(spread_out.shape[1:], 0.3 * mixing[g, f], F32)


def flux(mix, conds, centres, near):
    kc, *kn = conds
    radial = kc.shape[-1]
    fields = len(centres)
    lane = iota(kc.shape, 1)
    weights = [0.075 * (kc + k) for k in kn]
    up = 0.075 * (kc + jnp.where(lane == radial - 1, 0.0, pltpu.roll(kc, radial - 1, 1)))
    down = 0.075 * (kc + jnp.where(lane == 0, 0.0, pltpu.roll(kc, 1, 1)))
    total = 1.0 - ((weights[0] + weights[1]) + (weights[2] + weights[3]) + (up + down))
    up = jnp.where(lane == radial - 1, 0.0, up)
    down = jnp.where(lane == 0, 0.0, down)
    for g in range(fields):
        c = centres[g]
        acc = total * c
        for w, beside in zip(weights, near(g)):
            acc = acc + w * beside
        acc = acc + up * pltpu.roll(c, radial - 1, 1) + down * pltpu.roll(c, 1, 1)
        for f in range(fields):
            m = mix[g * fields + f]
            acc = acc + jnp.concatenate([m] * (c.shape[0] // 8), axis=0) * centres[f]
        yield g, acc


WIDE = 32


def along_phi(ref, f, t, tile_p, dt=0, dp=0):
    at = (t + dt) * WIDE + 8 + dp
    if isinstance(t, jax.Array) and dp == 0:
        at = pl.multiple_of(at, 8)
    return ref[f, pl.ds(at, tile_p), :]


def along_theta(ref, f, t, p, count):
    return ref[f, pl.ds(t * WIDE + 8 + p, count, stride=WIDE), :]


AROUND = ((-1, 0), (1, 0), (0, -1), (0, 1))


def row_flux(mix, field, cond, t_field, t_cond, tile_p, fields):
    last = cond.shape[0] - 1
    return flux(
        mix,
        [along_phi(cond, last, t_cond, tile_p)]
        + [along_phi(cond, last, t_cond, tile_p, *d) for d in AROUND],
        [along_phi(field, f, t_field, tile_p) for f in range(fields)],
        lambda g: [along_phi(field, g, t_field, tile_p, *d) for d in AROUND],
    )


def column_flux(mix, field, cond, t_field, t_cond, p, count, fields):
    last = cond.shape[0] - 1
    return flux(
        mix,
        [along_theta(cond, last, t_cond, p, count)]
        + [along_theta(cond, last, t_cond + dt, p + dp, count) for dt, dp in AROUND],
        [along_theta(field, f, t_field, p, count) for f in range(fields)],
        lambda g: [along_theta(field, g, t_field + dt, p + dp, count) for dt, dp in AROUND],
    )


def steps(
    mixing, corona, kappa, t_first, t_second, p_second, p_first, stepped, wide, once, mix,
):
    fields, tile_t, tile_p, radial = corona.shape
    by_t, by_p = sides("lat"), sides("lon")
    has_t = [low + high for low, high in by_t]
    has_p = [low + high for low, high in by_p]
    spread(mixing, mix)
    nothing = jnp.zeros((1, radial), F32)
    for f in range(fields + 1):
        for t in range(tile_t):
            own = corona[f, t] if f < fields else kappa[t]
            wide[f, pl.ds((t + 2) * WIDE + 8, tile_p), :] = own
        for k in range(2):
            for side, t in enumerate((k, tile_t + 2 + k)):
                wide[f, pl.ds(t * WIDE + 8, tile_p), :] = blend(
                    by_t[side], t_first[f, k], t_second[f, k]
                )
        for side, (near, far) in enumerate(((7, 6), (8 + tile_p, 9 + tile_p))):
            for k, col in enumerate((near, far)):
                rows = slice(k * tile_t, (k + 1) * tile_t)
                cells = blend(by_p[side], p_first[f, rows, :], p_second[f, rows, :])
                wide[f, pl.ds(2 * WIDE + col, tile_t, stride=WIDE), :] = cells
            for t in (1, tile_t + 2):
                wide[f, pl.ds(t * WIDE + near, 1), :] = nothing

    def first(t):
        for g, acc in row_flux(mix, wide, wide, t + 2, t + 2, tile_p, fields):
            if isinstance(t, int) and t in (-1, tile_t):
                acc = acc * has_t[0 if t < 0 else 1]
            at = (t + 1) * WIDE + 8
            once[g, pl.ds(at if isinstance(t, int) else pl.multiple_of(at, 8), tile_p), :] = acc

    def second(t):
        for g, acc in row_flux(mix, once, wide, t + 1, t + 2, tile_p, fields):
            stepped[g, t] = acc

    first(-1)
    first(tile_t)
    for p in (-1, tile_p):
        for g, acc in column_flux(mix, wide, wide, 2, 2, p, tile_t, fields):
            once[g, pl.ds(WIDE + 8 + p, tile_t, stride=WIDE), :] = acc * has_p[0 if p < 0 else 1]
    for row in (first, second):
        by_rows(row, tile_t)


def by_rows(row, count):
    if UNROLL >= count:
        for t in range(count):
            row(t)
        return

    def some(i, carry):
        for k in range(UNROLL):
            row(i * UNROLL + k)
        return carry

    lax.fori_loop(0, count // UNROLL, some, 0)


def route(
    n_dev, kappa, p_first, p_second, own_low, own_high, c_second, c_first, stepped, rank, meta, hit,
    table_high, table_low, w_r, patch, message, shell,
):
    fields, columns, radial = stepped.shape
    tile_t, tile_p, _ = kappa.shape
    sides_p = sides("lon")
    lane = iota((columns, radial), 1)
    rows = jnp.zeros((columns, radial), F32)
    for f in range(fields):
        moved = pltpu.roll(stepped[f], (f * SH + SH) % radial, 1)
        rows = jnp.where(lane // SH == f, moved, rows)
    shell[...] = rows
    for a in range(2):
        for b, own in enumerate((own_low, own_high)):
            t, p = a * (tile_t - 1), b * (tile_p - 1)

            def beside(f, t=t, weights=sides_p[b]):
                return blend(weights, p_first[f, t : t + 1, :], p_second[f, t : t + 1, :])

            k_t, u_t = own[a, fields : fields + 1], own[a, 0:fields]
            k_p = beside(fields)
            u_p = jnp.concatenate([beside(f) for f in range(fields)], axis=0)
            diagonal = blend(sides_p[b], c_first[a], c_second[a])
            k_d, u_d = diagonal[fields : fields + 1], diagonal[0:fields]
            k = kappa[t, p : p + 1, :]
            by_t = 0.075 * ((k_t + k_d) * u_d - k_d * u_t)
            by_p = 0.075 * ((k_p + k_d) * u_d - k_d * u_p)
            extra = 0.075 * ((k + k_t) * by_t + (k + k_p) * by_p)
            patch[2 * a + b] = extra
            row = jnp.zeros((1, radial), F32)
            for f in range(fields):
                moved = pltpu.roll(extra[f : f + 1], (f * SH + SH) % radial, 1)
                row = jnp.where(lane[0:1] // SH == f, moved, row)
            at = t * tile_p + p
            shell[at : at + 1, :] = shell[at : at + 1, :] + row
    rows = shell[...]
    high = rows.astype(BF16).astype(F32)
    both = high + pltpu.roll(rows - high, fields * SH, 1)
    left = jnp.transpose(both).astype(BF16)

    count = rank.shape[1]
    width = min(BLOCK, count)
    packed = jnp.zeros((n_dev, 2 * fields * CAP), F32)
    for b in range(count // width):
        cols = slice(b * width, (b + 1) * width)
        coarse = jnp.dot(left, table_high[:, cols], preferred_element_type=F32)
        fine = jnp.dot(left[: fields * SH], table_low[:, cols], preferred_element_type=F32)
        by_layer = coarse[: fields * SH] + (coarse[fields * SH :] + fine)
        value = jnp.sum(by_layer.reshape(fields, SH, width) * w_r[:, cols][None], axis=1)
        order = rank[:, cols]
        placed = jnp.concatenate(
            [jnp.where(order == float(k), value, 0.0) for k in range(CAP)], axis=0
        )
        placed_high, placed_low = halves(placed)
        packed = packed + lax.dot_general(
            hit[:, cols],
            jnp.concatenate([placed_high, placed_low], axis=0),
            (((1,), (1,)), ((), ())),
            preferred_element_type=F32,
        )
    half = fields * CAP
    message[pl.ds(0, n_dev, stride=2), :] = packed[:, :half] + packed[:, half:]
    message[pl.ds(1, n_dev, stride=2), :] = meta[...]


def finish(tile_t, tile_p, stepped, patch, out):
    out[...] = stepped[...]
    for a in range(2):
        for b in range(2):
            at = a * (tile_t - 1) * tile_p + b * (tile_p - 1)
            for f in range(stepped.shape[0]):
                out[f, at : at + 1, :] = (
                    stepped[f, at : at + 1, :] + patch[2 * a + b, f : f + 1, :]
                )


def land(n_dev, got, prev, coupled, t_first, t_second, p_second, p_first):
    fields, face_p, face_t = prev.shape
    values = jnp.transpose(got[pl.ds(0, n_dev, stride=2), :])
    cells = jnp.transpose(got[pl.ds(1, n_dev, stride=2), :])
    along_t = iota((face_t, n_dev), 0).astype(F32)
    along_p = iota((face_p, n_dev), 0).astype(F32)
    rows = fields * face_p
    total = jnp.zeros((2 * rows, face_t), F32)
    for k in range(CAP):
        at_t = jnp.where(along_t == cells[k : k + 1, :], 1.0, 0.0).astype(BF16)
        at_p = along_p == cells[CAP + k : CAP + k + 1, :]
        value = values[k * fields : (k + 1) * fields, :]
        high = value.astype(BF16).astype(F32)
        parts = [
            jnp.where(at_p[None], part[:, None, :], 0.0).reshape(rows, n_dev).astype(BF16)
            for part in (high, value - high)
        ]
        total = total + lax.dot_general(
            jnp.concatenate(parts, axis=0),
            at_t,
            (((1,), (1,)), ((), ())),
            preferred_element_type=F32,
        )
    new = prev[...].reshape(rows, face_t) + (total[:rows] + total[rows:])

    def edge(face, p):
        at = [f * face_p + p for f in range(fields)]
        return jnp.concatenate([face[k : k + 1, :] for k in at], axis=0)

    coupled[...] = new.reshape(fields, face_p, face_t)
    turned = jnp.transpose(new)
    for axis, low, high, first, second in (
        ("lat", turned[0:1, :], turned[face_t - 1 : face_t, :], t_first, t_second),
        ("lon", edge(new, 0), edge(new, face_p - 1), p_first, p_second),
    ):
        odd = parity(axis).astype(F32)
        first[...] = jnp.broadcast_to(blend((odd, 1.0 - odd), low, high), first.shape)
        second[...] = jnp.broadcast_to(blend((1.0 - odd, odd), low, high), second.shape)


def smooth(coupled, t_first, t_second, p_second, p_first, out):
    fields, face_p, face_t = coupled.shape
    x = coupled[...]
    row = iota((face_p, face_t), 0)[None]
    lane = iota((face_p, face_t), 1)[None]

    t_low, t_high = [blend(w, t_first[0:1], t_second[0:1]) for w in sides("lat")]
    p_low, p_high = [blend(w, p_first[...], p_second[...]) for w in sides("lon")]

    def column(edge):
        return jnp.transpose(jnp.broadcast_to(edge, (face_t, fields * face_p))).reshape(x.shape)

    below = jnp.where(row == 0, p_low[:, None, :], pltpu.roll(x, 1, 1))
    above = jnp.where(row == face_p - 1, p_high[:, None, :], pltpu.roll(x, face_p - 1, 1))
    left = jnp.where(lane == 0, column(t_low), pltpu.roll(x, 1, 2))
    right = jnp.where(lane == face_t - 1, column(t_high), pltpu.roll(x, face_t - 1, 2))
    out[...] = x + 0.2 * (above + below + right + left - 4.0 * x)


def call(kernel, outs, specs, name, scratch=(), room=40 * 1024 * 1024):
    outs = [s if isinstance(s, jax.ShapeDtypeStruct) else jax.ShapeDtypeStruct(s, F32) for s in outs]
    return pl.pallas_call(
        kernel,
        out_shape=outs,
        in_specs=specs,
        out_specs=[vspec()] * len(outs),
        scratch_shapes=list(scratch),
        name=name,
        compiler_params=pltpu.CompilerParams(vmem_limit_bytes=room),
    )


def body(corona, kappa, mixing, helio_prev, owner, dest_cell, corner_base, fractions):
    fields, tile_t, tile_p, radial = corona.shape
    n_lat, n_lon = lax.axis_size("lat"), lax.axis_size("lon")
    n_dev = n_lat * n_lon
    count = corner_base.shape[0]
    _, face_p, face_t = helio_prev.shape
    owner = owner.reshape(1, count)
    dest_cell = dest_cell.reshape(1, count)
    base = corner_base.reshape(1, count)
    edge = (fields + 1, 2, tile_p, radial)
    first, second = call(
        theta_edges,
        [edge] * 2,
        [pl.BlockSpec(memory_space=pltpu.HBM)] * 2,
        "theta_edges",
        [pltpu.SemaphoreType.DMA((4,))],
        room=58 * 1024 * 1024,
    )(corona, kappa)
    t_first, t_second = swapped(first, second, "lat")

    edge = (fields + 1, 2 * tile_t, radial)
    first, second = call(
        functools.partial(phi_edges, tile_t, tile_p), [edge] * 2, [vspec()] * 2, "phi_edges"
    )(corona.reshape(fields, tile_t * tile_p, radial), kappa.reshape(tile_t * tile_p, radial))
    p_first, p_second = swapped(first, second, "lon")

    table = jax.ShapeDtypeStruct((tile_t * tile_p, count), BF16)
    rank, meta, hit, table_high, table_low, w_r = call(
        functools.partial(plan, face_t, tile_t, tile_p),
        [(1, count), (n_dev, 128), jax.ShapeDtypeStruct((n_dev, count), BF16), table, table]
        + [(SH, count)],
        [vspec()] * 4,
        "plan",
    )(owner, dest_cell, base, fractions)

    t_first, t_second, rank = lax.optimization_barrier((t_first, t_second, rank))
    own_low, own_high, first, second = call(
        corner_cells, [(2, fields + 1, radial)] * 4, [vspec()] * 2, "corner_cells"
    )(t_first, t_second)
    c_first, c_second = swapped(first, second, "lon")

    flat = (fields, tile_t * tile_p, radial)
    (almost,) = call(
        steps,
        [corona.shape],
        [sspec()] + [vspec()] * 6,
        "steps",
        [
            VMEM((fields + 1, (tile_t + 4) * WIDE, radial), F32),
            VMEM((fields, (tile_t + 2) * WIDE, radial), F32),
            VMEM((fields * fields, 8, radial), F32),
        ],
    )(mixing, corona, kappa, t_first, t_second, p_second, p_first)
    almost = almost.reshape(flat)

    patch, message = call(
        functools.partial(route, n_dev),
        [(4, fields, radial), (2 * n_dev, 128)],
        [vspec()] * 14,
        "route",
        [VMEM((tile_t * tile_p, radial), F32)],
    )(
        kappa, p_first, p_second, own_low, own_high, c_second, c_first, almost, rank, meta, hit,
        table_high, table_low, w_r,
    )
    (stepped,) = call(
        functools.partial(finish, tile_t, tile_p), [flat], [vspec()] * 2, "finish"
    )(almost, patch)

    got = lax.all_to_all(message, ("lat", "lon"), split_axis=0, concat_axis=0, tiled=True)

    coupled, t_first, t_second, p_second, p_first = call(
        functools.partial(land, n_dev),
        [helio_prev.shape] + [(16, fields * face_p)] * 2 + [(fields, face_t)] * 2,
        [vspec()] * 2,
        "land",
    )(got, helio_prev)
    t_first, t_second = swapped(t_first, t_second, "lat")
    p_first, p_second = swapped(p_first, p_second, "lon")
    (face,) = call(smooth, [helio_prev.shape], [vspec()] * 5, "smooth")(
        coupled, t_first, t_second, p_second, p_first
    )
    return (stepped.reshape(corona.shape), face)


def solution(mesh):
    return jax.shard_map(
        body,
        mesh=mesh,
        in_specs=(
            P(None, "lat", "lon", None),
            P("lat", "lon", None),
            P(),
            P(None, "lon", "lat"),
            P(("lat", "lon"), None),
            P(("lat", "lon")),
            P(("lat", "lon")),
            P(None, ("lat", "lon")),
        ),
        out_specs=(P(None, "lat", "lon", None), P(None, "lon", "lat")),
        check_vma=False,
    )
```

```python
import functools

import jax
import jax.numpy as jnp
from jax import lax
from jax.experimental import pallas as pl
from jax.experimental.pallas import tpu as pltpu
from jax.sharding import PartitionSpec as P

SH = 8
CAP = 16
BLOCK = 256
UNROLL = 16
VMEM = pltpu.VMEM
F32 = jnp.float32
BF16 = jnp.bfloat16


def vspec():
    return pl.BlockSpec(memory_space=VMEM)


def sspec():
    return pl.BlockSpec(memory_space=pltpu.SMEM)


def iota(shape, dim):
    return lax.broadcasted_iota(jnp.int32, shape, dim)


def halves(x):
    high = x.astype(BF16)
    return high, (x - high.astype(F32)).astype(BF16)


def swapped(first, second, axis):
    count = lax.axis_size(axis)
    other = [(i + (1 if i % 2 else -1)) % count for i in range(count)]
    second = lax.ppermute(second, axis, list(enumerate(other)))
    return lax.ppermute(first, axis, [(i, i ^ 1) for i in range(count)]), second


def parity(axis):
    return lax.rem(lax.axis_index(axis), 2)


def sides(axis):
    at, count = lax.axis_index(axis), lax.axis_size(axis)
    odd = parity(axis).astype(F32)
    low = jnp.where(at > 0, 1.0, 0.0)
    high = jnp.where(at < count - 1, 1.0, 0.0)
    return (odd * low, (1.0 - odd) * low), ((1.0 - odd) * high, odd * high)


def blend(weights, first, second):
    return first * weights[0] + second * weights[1]


def theta_edges(corona, kappa, first, second, sems):
    fields, tile_t = corona.shape[0], corona.shape[1]
    odd = parity("lat")
    copies = []
    for n, (out, start) in enumerate(
        ((first, (1 - odd) * (tile_t - 2)), (second, odd * (tile_t - 2)))
    ):
        rows = pl.ds(start, 2)
        copies.append(
            pltpu.make_async_copy(corona.at[:, rows], out.at[pl.ds(0, fields)], sems.at[2 * n])
        )
        copies.append(pltpu.make_async_copy(kappa.at[rows], out.at[fields], sems.at[2 * n + 1]))
    for copy in copies:
        copy.start()
    for copy in copies:
        copy.wait()


def phi_edges(tile_t, tile_p, corona, kappa, first, second):
    fields = corona.shape[0]
    odd = parity("lon")
    for out, upper in ((first, 1 - odd), (second, odd)):
        near = upper * (tile_p - 1)
        far = upper * (tile_p - 3) + 1
        for f in range(fields + 1):
            for at, col in ((0, near), (tile_t, far)):
                rows = pl.ds(col, tile_t, stride=tile_p)
                out[f, at : at + tile_t, :] = corona[f, rows, :] if f < fields else kappa[rows, :]


def corner_cells(t_first, t_second, low, high, first, second):
    count, _, tile_p, _ = t_first.shape
    weights = sides("lat")
    for a, row in ((0, 1), (1, 0)):
        for f in range(count):
            for out, col in ((low, 0), (high, tile_p - 1)):
                cell = slice(col, col + 1)
                out[a, f : f + 1, :] = blend(
                    weights[a], t_first[f, row, cell, :], t_second[f, row, cell, :]
                )
    odd = parity("lon").astype(F32)
    first[...] = blend((odd, 1.0 - odd), low[...], high[...])
    second[...] = blend((1.0 - odd, odd), low[...], high[...])


def plan(
    face_t, tile_t, tile_p, owner, dest, base, frac, rank_out, meta_out, hit_out, high_out, low_out,
    radial_out,
):
    n_dev = meta_out.shape[0]
    count = owner.shape[1]
    width = min(BLOCK, count)
    before = (iota((width, width), 0) < iota((width, width), 1)).astype(F32).astype(BF16)
    owners = iota((n_dev, width), 0)
    slots = iota((CAP, width), 0).astype(F32)
    carry = jnp.zeros((n_dev, 1), F32)
    meta = jnp.zeros((n_dev, 128), F32)
    for b in range(count // width):
        cols = slice(b * width, (b + 1) * width)
        hit = owners == owner[:, cols]
        hit_f = jnp.where(hit, 1.0, 0.0)
        hit_b = hit_f.astype(BF16)
        hit_out[:, cols] = hit_b
        ahead = jnp.dot(hit_b, before, preferred_element_type=F32) + carry
        rank = jnp.sum(jnp.where(hit, ahead, 0.0), axis=0, keepdims=True)
        carry = ahead[:, width - 1 : width] + hit_f[:, width - 1 : width]
        rank_out[:, cols] = rank
        cell = dest[:, cols]
        cell_t = (cell % face_t).astype(F32)
        cell_p = (cell // face_t).astype(F32)
        mine = slots == rank
        rows = jnp.concatenate(
            [
                jnp.where(mine, cell_t, 0.0),
                jnp.where(mine, cell_p, 0.0),
                jnp.zeros((128 - 2 * CAP, width), F32),
            ],
            axis=0,
        ).astype(BF16)
        meta = meta + lax.dot_general(
            hit_b, rows, (((1,), (1,)), ((), ())), preferred_element_type=F32
        )
        corner = base[:, cols]

        def pair(size, at, fraction):
            rows = iota((size, width), 0)
            return jnp.where(rows == at, 1.0 - fraction, jnp.where(rows == at + 1, fraction, 0.0))

        w_t = pair(tile_t, corner // (tile_p * SH), frac[0:1, cols])
        w_p = pair(tile_p, (corner // SH) % tile_p, frac[1:2, cols])
        radial_out[:, cols] = pair(SH, corner % SH, frac[2:3, cols])
        table = (w_t[:, None, :] * w_p[None, :, :]).reshape(tile_t * tile_p, width)
        high_out[:, cols], low_out[:, cols] = halves(table)
    meta_out[...] = meta


def spread(mixing, spread_out):
    fields = mixing.shape[0]
    for g in range(fields):
        for f in range(fields):
            spread_out[g * fields + f] = jnp.full(spread_out.shape[1:], 0.3 * mixing[g, f], F32)


def flux(mix, conds, centres, near):
    kc, *kn = conds
    radial = kc.shape[-1]
    fields = len(centres)
    lane = iota(kc.shape, 1)
    weights = [0.075 * (kc + k) for k in kn]
    up = 0.075 * (kc + jnp.where(lane == radial - 1, 0.0, pltpu.roll(kc, radial - 1, 1)))
    down = 0.075 * (kc + jnp.where(lane == 0, 0.0, pltpu.roll(kc, 1, 1)))
    total = 1.0 - ((weights[0] + weights[1]) + (weights[2] + weights[3]) + (up + down))
    up = jnp.where(lane == radial - 1, 0.0, up)
    down = jnp.where(lane == 0, 0.0, down)
    for g in range(fields):
        c = centres[g]
        acc = total * c
        for w, beside in zip(weights, near(g)):
            acc = acc + w * beside
        acc = acc + up * pltpu.roll(c, radial - 1, 1) + down * pltpu.roll(c, 1, 1)
        for f in range(fields):
            m = mix[g * fields + f]
            acc = acc + jnp.concatenate([m] * (c.shape[0] // 8), axis=0) * centres[f]
        yield g, acc


WIDE = 32


def along_phi(ref, f, t, tile_p, dt=0, dp=0):
    at = (t + dt) * WIDE + 8 + dp
    if isinstance(t, jax.Array) and dp == 0:
        at = pl.multiple_of(at, 8)
    return ref[f, pl.ds(at, tile_p), :]


def along_theta(ref, f, t, p, count):
    return ref[f, pl.ds(t * WIDE + 8 + p, count, stride=WIDE), :]


AROUND = ((-1, 0), (1, 0), (0, -1), (0, 1))


def row_flux(mix, field, cond, t_field, t_cond, tile_p, fields):
    last = cond.shape[0] - 1
    return flux(
        mix,
        [along_phi(cond, last, t_cond, tile_p)]
        + [along_phi(cond, last, t_cond, tile_p, *d) for d in AROUND],
        [along_phi(field, f, t_field, tile_p) for f in range(fields)],
        lambda g: [along_phi(field, g, t_field, tile_p, *d) for d in AROUND],
    )


def column_flux(mix, field, cond, t_field, t_cond, p, count, fields):
    last = cond.shape[0] - 1
    return flux(
        mix,
        [along_theta(cond, last, t_cond, p, count)]
        + [along_theta(cond, last, t_cond + dt, p + dp, count) for dt, dp in AROUND],
        [along_theta(field, f, t_field, p, count) for f in range(fields)],
        lambda g: [along_theta(field, g, t_field + dt, p + dp, count) for dt, dp in AROUND],
    )


def steps(
    mixing, corona, kappa, t_first, t_second, p_second, p_first, stepped, wide, once, mix,
):
    fields, tile_t, tile_p, radial = corona.shape
    by_t, by_p = sides("lat"), sides("lon")
    has_t = [low + high for low, high in by_t]
    has_p = [low + high for low, high in by_p]
    spread(mixing, mix)
    nothing = jnp.zeros((1, radial), F32)
    for f in range(fields + 1):
        for t in range(tile_t):
            own = corona[f, t] if f < fields else kappa[t]
            wide[f, pl.ds((t + 2) * WIDE + 8, tile_p), :] = own
        for k in range(2):
            for side, t in enumerate((k, tile_t + 2 + k)):
                wide[f, pl.ds(t * WIDE + 8, tile_p), :] = blend(
                    by_t[side], t_first[f, k], t_second[f, k]
                )
        for side, (near, far) in enumerate(((7, 6), (8 + tile_p, 9 + tile_p))):
            for k, col in enumerate((near, far)):
                rows = slice(k * tile_t, (k + 1) * tile_t)
                cells = blend(by_p[side], p_first[f, rows, :], p_second[f, rows, :])
                wide[f, pl.ds(2 * WIDE + col, tile_t, stride=WIDE), :] = cells
            for t in (1, tile_t + 2):
                wide[f, pl.ds(t * WIDE + near, 1), :] = nothing

    def first(t):
        for g, acc in row_flux(mix, wide, wide, t + 2, t + 2, tile_p, fields):
            if isinstance(t, int) and t in (-1, tile_t):
                acc = acc * has_t[0 if t < 0 else 1]
            at = (t + 1) * WIDE + 8
            once[g, pl.ds(at if isinstance(t, int) else pl.multiple_of(at, 8), tile_p), :] = acc

    def second(t):
        for g, acc in row_flux(mix, once, wide, t + 1, t + 2, tile_p, fields):
            stepped[g, t] = acc

    first(-1)
    first(tile_t)
    for p in (-1, tile_p):
        for g, acc in column_flux(mix, wide, wide, 2, 2, p, tile_t, fields):
            once[g, pl.ds(WIDE + 8 + p, tile_t, stride=WIDE), :] = acc * has_p[0 if p < 0 else 1]
    for row in (first, second):
        by_rows(row, tile_t)


def by_rows(row, count):
    if UNROLL >= count:
        for t in range(count):
            row(t)
        return

    def some(i, carry):
        for k in range(UNROLL):
            row(i * UNROLL + k)
        return carry

    lax.fori_loop(0, count // UNROLL, some, 0)


def route(
    n_dev, kappa, p_first, p_second, own_low, own_high, c_second, c_first, stepped, rank, meta, hit,
    table_high, table_low, w_r, patch, message, shell,
):
    fields, columns, radial = stepped.shape
    tile_t, tile_p, _ = kappa.shape
    sides_p = sides("lon")
    lane = iota((columns, radial), 1)
    rows = jnp.zeros((columns, radial), F32)
    for f in range(fields):
        moved = pltpu.roll(stepped[f], (f * SH + SH) % radial, 1)
        rows = jnp.where(lane // SH == f, moved, rows)
    shell[...] = rows
    for a in range(2):
        for b, own in enumerate((own_low, own_high)):
            t, p = a * (tile_t - 1), b * (tile_p - 1)

            def beside(f, t=t, weights=sides_p[b]):
                return blend(weights, p_first[f, t : t + 1, :], p_second[f, t : t + 1, :])

            k_t, u_t = own[a, fields : fields + 1], own[a, 0:fields]
            k_p = beside(fields)
            u_p = jnp.concatenate([beside(f) for f in range(fields)], axis=0)
            diagonal = blend(sides_p[b], c_first[a], c_second[a])
            k_d, u_d = diagonal[fields : fields + 1], diagonal[0:fields]
            k = kappa[t, p : p + 1, :]
            by_t = 0.075 * ((k_t + k_d) * u_d - k_d * u_t)
            by_p = 0.075 * ((k_p + k_d) * u_d - k_d * u_p)
            extra = 0.075 * ((k + k_t) * by_t + (k + k_p) * by_p)
            patch[2 * a + b] = extra
            row = jnp.zeros((1, radial), F32)
            for f in range(fields):
                moved = pltpu.roll(extra[f : f + 1], (f * SH + SH) % radial, 1)
                row = jnp.where(lane[0:1] // SH == f, moved, row)
            at = t * tile_p + p
            shell[at : at + 1, :] = shell[at : at + 1, :] + row
    rows = shell[...]
    high = rows.astype(BF16).astype(F32)
    both = high + pltpu.roll(rows - high, fields * SH, 1)
    left = jnp.transpose(both).astype(BF16)

    count = rank.shape[1]
    width = min(BLOCK, count)
    packed = jnp.zeros((n_dev, 2 * fields * CAP), F32)
    for b in range(count // width):
        cols = slice(b * width, (b + 1) * width)
        coarse = jnp.dot(left, table_high[:, cols], preferred_element_type=F32)
        fine = jnp.dot(left[: fields * SH], table_low[:, cols], preferred_element_type=F32)
        by_layer = coarse[: fields * SH] + (coarse[fields * SH :] + fine)
        value = jnp.sum(by_layer.reshape(fields, SH, width) * w_r[:, cols][None], axis=1)
        order = rank[:, cols]
        placed = jnp.concatenate(
            [jnp.where(order == float(k), value, 0.0) for k in range(CAP)], axis=0
        )
        placed_high, placed_low = halves(placed)
        packed = packed + lax.dot_general(
            hit[:, cols],
            jnp.concatenate([placed_high, placed_low], axis=0),
            (((1,), (1,)), ((), ())),
            preferred_element_type=F32,
        )
    half = fields * CAP
    message[pl.ds(0, n_dev, stride=2), :] = packed[:, :half] + packed[:, half:]
    message[pl.ds(1, n_dev, stride=2), :] = meta[...]


def finish(tile_t, tile_p, stepped, patch, out):
    out[...] = stepped[...]
    for a in range(2):
        for b in range(2):
            at = a * (tile_t - 1) * tile_p + b * (tile_p - 1)
            for f in range(stepped.shape[0]):
                out[f, at : at + 1, :] = (
                    stepped[f, at : at + 1, :] + patch[2 * a + b, f : f + 1, :]
                )


def land(n_dev, got, prev, coupled, t_first, t_second, p_second, p_first):
    fields, face_p, face_t = prev.shape
    values = jnp.transpose(got[pl.ds(0, n_dev, stride=2), :])
    cells = jnp.transpose(got[pl.ds(1, n_dev, stride=2), :])
    along_t = iota((face_t, n_dev), 0).astype(F32)
    along_p = iota((face_p, n_dev), 0).astype(F32)
    rows = fields * face_p
    total = jnp.zeros((2 * rows, face_t), F32)
    for k in range(CAP):
        at_t = jnp.where(along_t == cells[k : k + 1, :], 1.0, 0.0).astype(BF16)
        at_p = along_p == cells[CAP + k : CAP + k + 1, :]
        value = values[k * fields : (k + 1) * fields, :]
        high = value.astype(BF16).astype(F32)
        parts = [
            jnp.where(at_p[None], part[:, None, :], 0.0).reshape(rows, n_dev).astype(BF16)
            for part in (high, value - high)
        ]
        total = total + lax.dot_general(
            jnp.concatenate(parts, axis=0),
            at_t,
            (((1,), (1,)), ((), ())),
            preferred_element_type=F32,
        )
    new = prev[...].reshape(rows, face_t) + (total[:rows] + total[rows:])

    def edge(face, p):
        at = [f * face_p + p for f in range(fields)]
        return jnp.concatenate([face[k : k + 1, :] for k in at], axis=0)

    coupled[...] = new.reshape(fields, face_p, face_t)
    turned = jnp.transpose(new)
    for axis, low, high, first, second in (
        ("lat", turned[0:1, :], turned[face_t - 1 : face_t, :], t_first, t_second),
        ("lon", edge(new, 0), edge(new, face_p - 1), p_first, p_second),
    ):
        odd = parity(axis).astype(F32)
        first[...] = blend((odd, 1.0 - odd), low, high)
        second[...] = blend((1.0 - odd, odd), low, high)


def smooth(coupled, t_first, t_second, p_second, p_first, out):
    fields, face_p, face_t = coupled.shape
    x = coupled[...]
    row = iota((face_p, face_t), 0)[None]
    lane = iota((face_p, face_t), 1)[None]

    t_low, t_high = [blend(w, t_first[...], t_second[...]) for w in sides("lat")]
    p_low, p_high = [blend(w, p_first[...], p_second[...]) for w in sides("lon")]

    def column(edge):
        return jnp.transpose(jnp.broadcast_to(edge, (face_t, fields * face_p))).reshape(x.shape)

    below = jnp.where(row == 0, p_low[:, None, :], pltpu.roll(x, 1, 1))
    above = jnp.where(row == face_p - 1, p_high[:, None, :], pltpu.roll(x, face_p - 1, 1))
    left = jnp.where(lane == 0, column(t_low), pltpu.roll(x, 1, 2))
    right = jnp.where(lane == face_t - 1, column(t_high), pltpu.roll(x, face_t - 1, 2))
    out[...] = x + 0.2 * (above + below + right + left - 4.0 * x)


def call(kernel, outs, specs, name, scratch=(), room=40 * 1024 * 1024):
    outs = [s if isinstance(s, jax.ShapeDtypeStruct) else jax.ShapeDtypeStruct(s, F32) for s in outs]
    return pl.pallas_call(
        kernel,
        out_shape=outs,
        in_specs=specs,
        out_specs=[vspec()] * len(outs),
        scratch_shapes=list(scratch),
        name=name,
        compiler_params=pltpu.CompilerParams(vmem_limit_bytes=room),
    )


def body(corona, kappa, mixing, helio_prev, owner, dest_cell, corner_base, fractions):
    fields, tile_t, tile_p, radial = corona.shape
    n_lat, n_lon = lax.axis_size("lat"), lax.axis_size("lon")
    n_dev = n_lat * n_lon
    count = corner_base.shape[0]
    _, face_p, face_t = helio_prev.shape
    owner = owner.reshape(1, count)
    dest_cell = dest_cell.reshape(1, count)
    base = corner_base.reshape(1, count)
    edge = (fields + 1, 2, tile_p, radial)
    first, second = call(
        theta_edges,
        [edge] * 2,
        [pl.BlockSpec(memory_space=pltpu.HBM)] * 2,
        "theta_edges",
        [pltpu.SemaphoreType.DMA((4,))],
        room=58 * 1024 * 1024,
    )(corona, kappa)
    t_first, t_second = swapped(first, second, "lat")

    edge = (fields + 1, 2 * tile_t, radial)
    first, second = call(
        functools.partial(phi_edges, tile_t, tile_p), [edge] * 2, [vspec()] * 2, "phi_edges"
    )(corona.reshape(fields, tile_t * tile_p, radial), kappa.reshape(tile_t * tile_p, radial))
    p_first, p_second = swapped(first, second, "lon")

    table = jax.ShapeDtypeStruct((tile_t * tile_p, count), BF16)
    rank, meta, hit, table_high, table_low, w_r = call(
        functools.partial(plan, face_t, tile_t, tile_p),
        [(1, count), (n_dev, 128), jax.ShapeDtypeStruct((n_dev, count), BF16), table, table]
        + [(SH, count)],
        [vspec()] * 4,
        "plan",
    )(owner, dest_cell, base, fractions)

    t_first, t_second, rank = lax.optimization_barrier((t_first, t_second, rank))
    own_low, own_high, first, second = call(
        corner_cells, [(2, fields + 1, radial)] * 4, [vspec()] * 2, "corner_cells"
    )(t_first, t_second)
    c_first, c_second = swapped(first, second, "lon")

    flat = (fields, tile_t * tile_p, radial)
    (almost,) = call(
        steps,
        [corona.shape],
        [sspec()] + [vspec()] * 6,
        "steps",
        [
            VMEM((fields + 1, (tile_t + 4) * WIDE, radial), F32),
            VMEM((fields, (tile_t + 2) * WIDE, radial), F32),
            VMEM((fields * fields, 8, radial), F32),
        ],
    )(mixing, corona, kappa, t_first, t_second, p_second, p_first)
    almost = almost.reshape(flat)

    patch, message = call(
        functools.partial(route, n_dev),
        [(4, fields, radial), (2 * n_dev, 128)],
        [vspec()] * 14,
        "route",
        [VMEM((tile_t * tile_p, radial), F32)],
    )(
        kappa, p_first, p_second, own_low, own_high, c_second, c_first, almost, rank, meta, hit,
        table_high, table_low, w_r,
    )
    (stepped,) = call(
        functools.partial(finish, tile_t, tile_p), [flat], [vspec()] * 2, "finish"
    )(almost, patch)

    got = lax.all_to_all(message, ("lat", "lon"), split_axis=0, concat_axis=0, tiled=True)

    coupled, t_first, t_second, p_second, p_first = call(
        functools.partial(land, n_dev),
        [helio_prev.shape] + [(1, fields * face_p)] * 2 + [(fields, face_t)] * 2,
        [vspec()] * 2,
        "land",
    )(got, helio_prev)
    t_first, t_second = swapped(t_first, t_second, "lat")
    p_first, p_second = swapped(p_first, p_second, "lon")
    (face,) = call(smooth, [helio_prev.shape], [vspec()] * 5, "smooth")(
        coupled, t_first, t_second, p_second, p_first
    )
    return (stepped.reshape(corona.shape), face)


def solution(mesh):
    return jax.shard_map(
        body,
        mesh=mesh,
        in_specs=(
            P(None, "lat", "lon", None),
            P("lat", "lon", None),
            P(),
            P(None, "lon", "lat"),
            P(("lat", "lon"), None),
            P(("lat", "lon")),
            P(("lat", "lon")),
            P(None, ("lat", "lon")),
        ),
        out_specs=(P(None, "lat", "lon", None), P(None, "lon", "lat")),
        check_vma=False,
    )
```
